32 devices in a mesh: dp: 4 (over x, core), context: 2 (over y), tensor: 4 (over z).
Axes of the slice: x: 2, y: 2, z: 4, core: 2. Of those that a mesh axis runs over, the one named last changes fastest.
Arguments:
- layer_input: bfloat16 [4, 4096, 2048], P('dp', 'context'), may hold values from -6 to 6
- cotangent: bfloat16 [4, 4096, 2048], P('dp', 'context'), may hold values from -6 to 6
- w_qkv: bfloat16 [2048, 1536], P(('dp', 'context'), 'tensor'), may hold values from -0.125 to 0.125
- w_out: bfloat16 [1024, 2048], P('tensor', ('dp', 'context')), may hold values from -1.5 to 1.5
- attn_gain: bfloat16 [2048], P(('dp', 'context')), may hold values from 0.5 to 1.5
- qk_gain: float32 [2, 64], replicated, may hold values from 0.1 to 1.9
- w_gate: bfloat16 [2048, 5120], P(('dp', 'context'), 'tensor'), may hold values from -0.125 to 0.125
- w_up: bfloat16 [2048, 5120], P(('dp', 'context'), 'tensor'), may hold values from -0.125 to 0.125
- w_down: bfloat16 [5120, 2048], P('tensor', ('dp', 'context')), may hold values from -0.078125 to 0.078125
- ffn_gain: bfloat16 [2048], P(('dp', 'context')), may hold values from 0.5 to 1.5
- seg_ids: int32 [4, 4096], P('dp'), may hold values from 0 to 8, as said below
- pos_ids: int32 [4, 4096], P('dp'), may hold values from 0 to 2431, as said below
Outputs:
- layer_output: bfloat16 [4, 4096, 2048], P('dp', 'context')
- grad_input: bfloat16 [4, 4096, 2048], P('dp', 'context')
- grad_qkv: float32 [2048, 1536], P(('dp', 'context'), 'tensor')
- grad_out_proj: float32 [1024, 2048], P('tensor', ('dp', 'context'))
- grad_attn_gain: float32 [2048], P(('dp', 'context'))
- grad_qk_gain: float32 [2, 64], replicated
- grad_gate: float32 [2048, 5120], P(('dp', 'context'), 'tensor')
- grad_up: float32 [2048, 5120], P(('dp', 'context'), 'tensor')
- grad_down: float32 [5120, 2048], P('tensor', ('dp', 'context'))
- grad_ffn_gain: float32 [2048], P(('dp', 'context'))
The draws below stay inside these ranges and needn't reach their ends.
Inputs may be any that keep to these rules, and one draw needn't show every extreme that they name: `seg_ids`: within each group the first 2048 tokens have id 0; the rest form 8 runs of consecutive tokens with ids 1 to 8 rising along the tokens, each run 1 to 384 tokens long, one of exactly 384 in every group. `pos_ids`: prompt token t has position t; the tokens of a continuation have positions 2048, 2049, ... in order.
All inputs are finite; a program needn't handle non-finite values.
Results may differ from the reference program's by a relative error of at most 0.024.
Values may be sent and summed in bfloat16 or wider, within the bound.
A program may use at most 256 MiB of HBM per device.

```python
import math
import jax
import jax.numpy as jnp
from jax import lax

D = 2048
HEADS = 16
KV_HEADS = 4
HEAD_DIM = 64
FF = 5120
PROMPT = 2048
CONTS = 8
CONT_LEN = 256
CONT_MOST = 384
GT = 4096
GROUPS = 4
QKV = 1536


def one_layout(key):
    first_key, second_key = jax.random.split(key)
    pair_count = CONTS // 2
    shifts = jax.random.randint(first_key, (pair_count,), 1 - CONT_LEN // 2, CONT_LEN // 2)
    shifts = shifts.at[0].set(CONT_MOST - CONT_LEN)
    lengths = jnp.concatenate([CONT_LEN + shifts, CONT_LEN - shifts]).astype(jnp.int32)
    lengths = lengths[jax.random.permutation(second_key, CONTS)]
    run_ends = jnp.cumsum(lengths)
    run_starts = run_ends - lengths
    places = jnp.arange(CONTS * CONT_LEN, dtype=jnp.int32)
    run_index = jnp.sum((places[:, None] >= run_ends[None, :]).astype(jnp.int32), axis=1)
    owner = run_index[:, None] == jnp.arange(CONTS, dtype=jnp.int32)[None, :]
    offsets = places - jnp.sum(jnp.where(owner, run_starts[None, :], 0), axis=1)
    segments = jnp.concatenate([jnp.zeros((PROMPT,), jnp.int32), run_index + 1]).astype(jnp.int32)
    positions = jnp.concatenate([jnp.arange(PROMPT, dtype=jnp.int32), PROMPT + offsets]).astype(jnp.int32)
    return (segments, positions)


def layout(key):
    group_keys = jax.random.split(jax.random.fold_in(key, 11), GROUPS)
    return jax.vmap(one_layout)(group_keys)


def draw_seg_ids(key, part):
    return layout(key)[0]


def draw_pos_ids(key, part):
    return layout(key)[1]


def shard_levels(stream_key, dims, cuts, smallest, top_value):
    def one(position, blocks):
        heights = jax.random.uniform(jax.random.fold_in(jax.random.fold_in(stream_key, 6), position), (blocks,), jnp.float32, smallest / len(cuts), top_value / len(cuts))
        return jnp.repeat(jnp.exp(heights), dims[position] // blocks).reshape((-1,) + (1,) * (len(dims) - position - 1))

    level = one(*cuts[0])
    for cut in cuts[1:]:
        level = level * one(*cut)
    return level


def centred(key, shape, deviation, limit, cuts=(), kind=jnp.bfloat16):
    level = shard_levels(key, shape, cuts, -0.22, 0.18) if cuts else 1.0
    drawn = jax.random.normal(key, shape, jnp.float32) * deviation * level
    return jnp.minimum(jnp.maximum(drawn, -limit), limit).astype(kind)


def setup_inputs(seed: int = 0) -> dict:
    streams_of = jax.random.split(jax.random.key(seed), 13)
    return {
        "layer_input": centred(streams_of[0], (GROUPS, GT, D), 1.0, 6.0, ((0, 4), (1, 2))),
        "cotangent": centred(streams_of[1], (GROUPS, GT, D), 1.0, 6.0, ((0, 4), (1, 2))),
        "w_qkv": centred(streams_of[2], (D, QKV), D ** -0.5, 0.125, ((0, 8), (1, 4))),
        "w_out": centred(streams_of[3], (HEADS * HEAD_DIM, D), (HEADS * HEAD_DIM // 64) ** -0.5, 1.5, ((0, 4), (1, 8))),
        "attn_gain": jnp.clip(1.0 + 0.1 * jax.random.normal(streams_of[4], (D,), jnp.float32), 0.5, 1.5).astype(jnp.bfloat16),
        "qk_gain": jnp.clip(1.0 + 0.18 * jax.random.normal(streams_of[5], (2, HEAD_DIM), jnp.float32), 0.1, 1.9),
        "w_gate": centred(streams_of[6], (D, FF), D ** -0.5, 0.125, ((0, 8), (1, 4))),
        "w_up": centred(streams_of[7], (D, FF), D ** -0.5, 0.125, ((0, 8), (1, 4))),
        "w_down": centred(streams_of[8], (FF, D), FF ** -0.5, 0.078125, ((0, 4), (1, 8))),
        "ffn_gain": jnp.clip(1.0 + 0.1 * jax.random.normal(streams_of[9], (D,), jnp.float32), 0.5, 1.5).astype(jnp.bfloat16),
        "seg_ids": draw_seg_ids(jax.random.fold_in(streams_of[12], 71), 0),
        "pos_ids": draw_pos_ids(jax.random.fold_in(streams_of[12], 71), 0),
    }


epsilon = 1e-06
rope_base = 10000.0

@jax.custom_vjp
def low(v):
    return lax.optimization_barrier(v.astype(jnp.bfloat16)).astype(jnp.float32)

@jax.custom_vjp
def low_back(v):
    return v

def low_keep(v):
    return (low(v), None)

def low_pass(kept, grad):
    return (grad,)

def back_keep(v):
    return (v, None)

def back_low(kept, grad):
    return (low(grad),)
low.defvjp(low_keep, low_pass)
low_back.defvjp(back_keep, back_low)

def matmul(left, right):
    return jnp.dot(left, right, preferred_element_type=jnp.float32, precision=lax.Precision.HIGHEST)

def norm_rows(values, gains):
    return values * lax.rsqrt(lax.optimization_barrier(jnp.mean(values * values, axis=-1, keepdims=True)) + epsilon) * gains

def rope_tables(positions, head_width):
    half_width = head_width // 2
    inverse = jnp.exp(-math.log(rope_base) * jnp.arange(half_width, dtype=jnp.float32) * 2.0 / head_width)
    angles = positions.astype(jnp.float32)[..., None] * inverse
    cosine_tab = jnp.concatenate([jnp.cos(angles), jnp.cos(angles)], axis=-1)
    sine_table = jnp.concatenate([jnp.sin(angles), jnp.sin(angles)], axis=-1)
    return (cosine_tab, sine_table)

def rotate(values, cosine_tab, sine_table):
    half_width = values.shape[-1] // 2
    lower_half = values[..., :half_width]
    upper_half = values[..., half_width:]
    return values * cosine_tab + jnp.concatenate([-upper_half, lower_half], axis=-1) * sine_table

def visible(query_pos, query_seg, key_pos, key_seg):
    same_run = (key_seg[None, :] == 0) | (key_seg[None, :] == query_seg[:, None])
    return (key_pos[None, :] <= query_pos[:, None]) & same_run

def reference(layer_input, cotangent, w_qkv, w_out, attn_gain, qk_gain, w_gate, w_up, w_down, ffn_gain, seg_ids, pos_ids):
    head_ratio = HEADS // KV_HEADS
    score_scale = HEAD_DIM ** (-0.5)
    block_rows = min(GT, 128)
    block_count = GT // block_rows

    def group_layer(inputs, segments, positions, qkv_weight, out_weight, gain_in, gains_qk, gate_weight, up_weight, down_weight, gain_ffn):
        normed = low(norm_rows(inputs, gain_in))
        joint = low_back(matmul(normed, qkv_weight)).reshape(GT, KV_HEADS, head_ratio + 2, HEAD_DIM)
        cosine_tab, sine_table = rope_tables(positions, HEAD_DIM)
        queries = low(rotate(norm_rows(joint[:, :, :head_ratio], gains_qk[0]), cosine_tab[:, None, None, :], sine_table[:, None, None, :]))
        keys = low(rotate(norm_rows(joint[:, :, head_ratio], gains_qk[1]), cosine_tab[:, None, :], sine_table[:, None, :]))
        values = low(joint[:, :, head_ratio + 1])

        def attend(block_items):
            query_block, query_pos, query_seg = block_items
            scores = low_back(jnp.einsum('qkrd,tkd->qkrt', query_block, keys, precision=lax.Precision.HIGHEST))
            allowed = visible(query_pos, query_seg, positions, segments)
            scores = jnp.where(allowed[:, None, None, :], scores * score_scale, -1e+30)
            probs = low(jax.nn.softmax(scores, axis=-1))
            return jnp.einsum('qkrt,tkd->qkrd', probs, values, precision=lax.Precision.HIGHEST)
        attended = lax.map(jax.checkpoint(attend), (queries.reshape(block_count, block_rows, KV_HEADS, head_ratio, HEAD_DIM), positions.reshape(block_count, block_rows), segments.reshape(block_count, block_rows)))
        attended = low(low_back(attended.reshape(GT, HEADS * HEAD_DIM)))
        resid = inputs + low_back(matmul(attended, out_weight))
        normed_ffn = low(norm_rows(resid, gain_ffn))
        gate = low_back(matmul(normed_ffn, gate_weight))
        up = low_back(matmul(normed_ffn, up_weight))
        act = low(jax.nn.silu(gate) * up)
        return resid + matmul(act, down_weight)

    def layer(inputs, qkv_weight, out_weight, gain_in, gains_qk, gate_weight, up_weight, down_weight, gain_ffn):

        def step(carry, items):
            result = jax.checkpoint(group_layer)(items[0], items[1], items[2], qkv_weight, out_weight, gain_in, gains_qk, gate_weight, up_weight, down_weight, gain_ffn)
            return (carry, result)
        _, outputs = lax.scan(step, jnp.zeros((), jnp.float32), (inputs, seg_ids, pos_ids))
        return outputs
    primals = (layer_input.astype(jnp.float32), w_qkv.astype(jnp.float32), w_out.astype(jnp.float32), attn_gain.astype(jnp.float32), qk_gain.astype(jnp.float32), w_gate.astype(jnp.float32), w_up.astype(jnp.float32), w_down.astype(jnp.float32), ffn_gain.astype(jnp.float32))
    result, pullback = jax.vjp(layer, *primals)
    grads = pullback(cotangent.astype(jnp.float32))
    return (result.astype(jnp.bfloat16), grads[0].astype(jnp.bfloat16), grads[1], grads[2], grads[3], grads[4], grads[5], grads[6], grads[7], grads[8])
```

```python
import functools, math
import jax, jax.numpy as jnp
from jax import lax
from jax.experimental import pallas as pl
from jax.experimental.pallas import tpu as pltpu
from jax.sharding import PartitionSpec as P

HEAD_DIM = 64
LOG2E = math.log2(math.e)
LN2 = math.log(2.0)
f32 = jnp.float32
bf16 = jnp.bfloat16
epsilon = 1e-6


def dot_nt(a, b):
    return lax.dot_general(a, b, (((1,), (1,)), ((), ())), preferred_element_type=f32)

def dot_nn(a, b):
    return lax.dot_general(a, b, (((1,), (0,)), ((), ())), preferred_element_type=f32)

def dot_tn(a, b):
    return lax.dot_general(a, b, (((0,), (0,)), ((), ())), preferred_element_type=f32)


def head_norm(x):
    return x * lax.rsqrt(jnp.mean(x * x, axis=0, keepdims=True) + epsilon)


def prep_kernel(heads, joint_ref, cos_ref, sin_ref, gain_ref, q_ref, kv_ref):
    half = HEAD_DIM // 2
    cos, sin = cos_ref[...], sin_ref[...]

    def one(row, gain, scale):
        x = head_norm(joint_ref[row : row + HEAD_DIM, :]) * gain
        lo, hi = x[:half], x[half:]
        return jnp.concatenate([lo * cos - hi * sin, hi * cos + lo * sin], axis=0) * scale

    for h in range(heads):
        row = h * HEAD_DIM
        q_ref[row : row + HEAD_DIM, :] = one(row, gain_ref[:, 0:1], LOG2E * HEAD_DIM**-0.5).astype(bf16)
    row = heads * HEAD_DIM
    key = one(row, gain_ref[:, 1:2], 1.0)
    both = jnp.concatenate([key, joint_ref[row + HEAD_DIM : row + 2 * HEAD_DIM, :]], axis=0)
    kv_ref[...] = both.T.astype(bf16)


def prep(joint, cos, sin, gains, heads, block):
    rows, count = joint.shape
    block = min(block, count)
    return pl.pallas_call(
        functools.partial(prep_kernel, heads),
        out_shape=(
            jax.ShapeDtypeStruct((heads * HEAD_DIM, count), bf16),
            jax.ShapeDtypeStruct((count, 2 * HEAD_DIM), bf16),
        ),
        grid=(count // block,),
        in_specs=[
            pl.BlockSpec((rows, block), lambda i: (0, i)),
            pl.BlockSpec((HEAD_DIM // 2, block), lambda i: (0, i)),
            pl.BlockSpec((HEAD_DIM // 2, block), lambda i: (0, i)),
            pl.BlockSpec((HEAD_DIM, 2), lambda i: (0, 0)),
        ],
        out_specs=(
            pl.BlockSpec((heads * HEAD_DIM, block), lambda i: (0, i)),
            pl.BlockSpec((block, 2 * HEAD_DIM), lambda i: (i, 0)),
        ),
        cost_estimate=pl.CostEstimate(flops=rows * count * 20, bytes_accessed=rows * count * 6, transcendentals=0),
        name="prep",
    )(joint, cos, sin, gains)


def unprep_kernel(heads, joint_ref, cos_ref, sin_ref, gain_ref, dq_ref, dkv_ref, out_ref, dgain_ref):
    half = HEAD_DIM // 2
    cos, sin = cos_ref[...], sin_ref[...]

    @pl.when(pl.program_id(0) == 0)
    def _():
        dgain_ref[...] = jnp.zeros_like(dgain_ref)

    def one(row, grad, gain):
        x = joint_ref[row : row + HEAD_DIM, :]
        r = lax.rsqrt(jnp.mean(x * x, axis=0, keepdims=True) + epsilon)
        n = x * r
        lo, hi = grad[:half], grad[half:]
        back = jnp.concatenate([lo * cos + hi * sin, hi * cos - lo * sin], axis=0)
        scaled = back * gain
        result = r * (scaled - n * jnp.mean(scaled * n, axis=0, keepdims=True))
        out_ref[row : row + HEAD_DIM, :] = result.astype(bf16)
        return jnp.sum(back * n, axis=1, keepdims=True)

    total = None
    for h in range(heads):
        row = h * HEAD_DIM
        part = one(row, dq_ref[row : row + HEAD_DIM, :], gain_ref[:, 0:1])
        total = part if total is None else total + part
    row = heads * HEAD_DIM
    dkv = dkv_ref[...].astype(f32).T
    part = one(row, dkv[:HEAD_DIM], gain_ref[:, 1:2])
    out_ref[row + HEAD_DIM : row + 2 * HEAD_DIM, :] = dkv[HEAD_DIM:].astype(bf16)
    dgain_ref[...] += jnp.concatenate([total, part], axis=1)


def unprep(joint, cos, sin, gains, dq, dkv, heads, block):
    rows, count = joint.shape
    block = min(block, count)
    return pl.pallas_call(
        functools.partial(unprep_kernel, heads),
        out_shape=(
            jax.ShapeDtypeStruct((rows, count), bf16),
            jax.ShapeDtypeStruct((HEAD_DIM, 2), f32),
        ),
        grid=(count // block,),
        in_specs=[
            pl.BlockSpec((rows, block), lambda i: (0, i)),
            pl.BlockSpec((HEAD_DIM // 2, block), lambda i: (0, i)),
            pl.BlockSpec((HEAD_DIM // 2, block), lambda i: (0, i)),
            pl.BlockSpec((HEAD_DIM, 2), lambda i: (0, 0)),
            pl.BlockSpec((heads * HEAD_DIM, block), lambda i: (0, i)),
            pl.BlockSpec((block, 2 * HEAD_DIM), lambda i: (i, 0)),
        ],
        out_specs=(
            pl.BlockSpec((rows, block), lambda i: (0, i)),
            pl.BlockSpec((HEAD_DIM, 2), lambda i: (0, 0)),
        ),
        cost_estimate=pl.CostEstimate(flops=rows * count * 30, bytes_accessed=rows * count * 10, transcendentals=0),
        name="unprep",
    )(joint, cos, sin, gains, dq, dkv)


def block_state(seg_ref, start_ref, q_index, k_index, bq, bk):
    q_first = start_ref[0] + q_index * bq
    k_first = k_index * bk
    k_last_seg = seg_ref[k_first + bk - 1]
    needed = (k_first <= q_first + bq - 1) & ((k_last_seg == 0) | (k_last_seg >= seg_ref[q_first]) | (seg_ref[k_first] == 0))
    whole = (k_last_seg == 0) & (k_first + bk - 1 <= q_first)
    return needed, whole


def fwd_kernel(heads, bq, bk, start_ref, seg_ref, q_ref, kv_ref, qpos_ref, qseg_ref, kpos_ref, kseg_ref, o_ref, l_ref, vaug, qs, acc):
    qi = pl.program_id(0)
    nk = kv_ref.shape[0] // bk
    lane = lax.broadcasted_iota(jnp.int32, kv_ref.shape, 1)

    @pl.when(qi == 0)
    def _():
        vaug[...] = jnp.where(lane >= HEAD_DIM, kv_ref[...].astype(f32), jnp.where(lane == 0, 1.0, 0.0)).astype(bf16)

    zeros = jnp.zeros((HEAD_DIM, bq), f32)
    for h in range(heads):
        full = jnp.concatenate([q_ref[h * HEAD_DIM : (h + 1) * HEAD_DIM, :].astype(f32), zeros], axis=0)
        qs[h * bq : (h + 1) * bq, :] = full.T.astype(bf16)
    acc[...] = jnp.zeros_like(acc)

    def step(k_index, masked):
        rows = pl.ds(pl.multiple_of(k_index * bk, bk), bk)
        kb, vb = kv_ref[rows, :], vaug[rows, :]
        if masked:
            kseg = kseg_ref[k_index]
            mask = (kpos_ref[k_index] <= qpos_ref[...]) & ((kseg == 0) | (kseg == qseg_ref[...]))
        for h in range(heads):
            s = dot_nt(qs[h * bq : (h + 1) * bq, :], kb)
            p = jnp.exp2(s)
            if masked:
                p = jnp.where(mask, p, 0.0)
            acc[h * bq : (h + 1) * bq, :] += dot_nn(p.astype(bf16), vb)

    @pl.loop(0, nk)
    def _(k_index):
        needed, whole = block_state(seg_ref, start_ref, qi, k_index, bq, bk)

        @pl.when(needed & whole)
        def _():
            step(k_index, False)

        @pl.when(needed & jnp.logical_not(whole))
        def _():
            step(k_index, True)

    for h in range(heads):
        out = acc[h * bq : (h + 1) * bq, :].T
        total = out[0:1, :]
        o_ref[h * HEAD_DIM : (h + 1) * HEAD_DIM, :] = (out[HEAD_DIM:, :] / total).astype(bf16)
        l_ref[h : h + 1, :] = jnp.log2(total)


def attention(start, seg, q, kv, qpos, qseg, kpos, kseg, bq, bk):
    heads = q.shape[0] // HEAD_DIM
    count, total = q.shape[1], kv.shape[0]
    bq, bk = min(bq, count), min(bk, total)
    whole = lambda *shape: pl.BlockSpec(shape, lambda i, *_: (0,) * len(shape))
    return pl.pallas_call(
        functools.partial(fwd_kernel, heads, bq, bk),
        out_shape=(
            jax.ShapeDtypeStruct(q.shape, bf16),
            jax.ShapeDtypeStruct((heads, count), f32),
        ),
        grid_spec=pltpu.PrefetchScalarGridSpec(
            num_scalar_prefetch=2,
            grid=(count // bq,),
            in_specs=[
                pl.BlockSpec((q.shape[0], bq), lambda i, *_: (0, i)),
                whole(*kv.shape),
                pl.BlockSpec((bq, 1), lambda i, *_: (i, 0)),
                pl.BlockSpec((bq, 1), lambda i, *_: (i, 0)),
                whole(total // bk, 1, bk),
                whole(total // bk, 1, bk),
            ],
            out_specs=(
                pl.BlockSpec((q.shape[0], bq), lambda i, *_: (0, i)),
                pl.BlockSpec((heads, bq), lambda i, *_: (0, i)),
            ),
            scratch_shapes=[
                pltpu.VMEM(kv.shape, bf16),
                pltpu.VMEM((heads * bq, 2 * HEAD_DIM), bf16),
                pltpu.VMEM((heads * bq, 2 * HEAD_DIM), f32),
            ],
        ),
        cost_estimate=pl.CostEstimate(flops=heads * count * total * 256, bytes_accessed=4 << 20, transcendentals=heads * count * total // 2),
        name="attend",
    )(start, seg, q, kv, qpos.reshape(-1, 1), qseg.reshape(-1, 1), kpos.reshape(-1, 1, bk), kseg.reshape(-1, 1, bk))


def split3(x):
    a = x.astype(bf16).astype(f32)
    b = (x - a).astype(bf16).astype(f32)
    return a, b, x - a - b


def bwd_kernel(heads, bq, bk, start_ref, seg_ref, q_ref, kv_ref, o_ref, do_ref, l_ref, qpos_ref, qseg_ref, kpos_ref, kseg_ref,
               dq_ref, dkv_ref, kaug, vaug, qst, dst, qs, ds, dacc, dkv):
    qi = pl.program_id(0)
    nk = kv_ref.shape[0] // bk
    D = HEAD_DIM

    @pl.when(qi == 0)
    def _():
        lane = lax.broadcasted_iota(jnp.int32, kv_ref.shape, 1)
        kv = kv_ref[...].astype(f32)
        kaug[...] = jnp.where(lane < D, kv, jnp.where(lane < D + 3, -1.0, 0.0)).astype(bf16)
        vaug[...] = jnp.where(lane >= D, kv, jnp.where(lane < 3, -1.0, 0.0)).astype(bf16)
        dkv[...] = jnp.zeros_like(dkv)

    row = lax.broadcasted_iota(jnp.int32, (D, bq), 0)

    def extra(x):
        a, b, c = split3(x)
        return jnp.where(row == 0, a, jnp.where(row == 1, b, jnp.where(row == 2, c, 0.0)))

    zeros = jnp.zeros((D, bq), f32)
    for h in range(heads):
        part = slice(h * D, (h + 1) * D)
        wide = slice(h * 2 * D, (h + 1) * 2 * D)
        q, do, o = q_ref[part, :].astype(f32), do_ref[part, :].astype(f32), o_ref[part, :].astype(f32)
        delta = jnp.sum(do * o, axis=0, keepdims=True)
        qst[wide, :] = jnp.concatenate([q, extra(l_ref[h : h + 1, :])], axis=0).astype(bf16)
        dst[wide, :] = jnp.concatenate([extra(delta), do], axis=0).astype(bf16)
        qs[h * bq : (h + 1) * bq, :] = jnp.concatenate([q, zeros], axis=0).T.astype(bf16)
        ds[h * bq : (h + 1) * bq, :] = jnp.concatenate([zeros, do], axis=0).T.astype(bf16)
    dacc[...] = jnp.zeros_like(dacc)

    def step(k_index, masked):
        rows = pl.ds(pl.multiple_of(k_index * bk, bk), bk)
        kb, vb, kvb = kaug[rows, :], vaug[rows, :], kv_ref[rows, :]
        if masked:
            kseg = kseg_ref[rows, :]
            mask = (kpos_ref[rows, :] <= qpos_ref[...]) & ((kseg == 0) | (kseg == qseg_ref[...]))
        add = None
        for h in range(heads):
            wide = slice(h * 2 * D, (h + 1) * 2 * D)
            tall = slice(h * bq, (h + 1) * bq)
            p = jnp.exp2(dot_nn(kb, qst[wide, :]))
            if masked:
                p = jnp.where(mask, p, 0.0)
            sg = (p * dot_nn(vb, dst[wide, :])).astype(bf16)
            part = dot_nn(sg, qs[tall, :]) + dot_nn(p.astype(bf16), ds[tall, :])
            add = part if add is None else add + part
            dacc[tall, :] += dot_tn(sg, kvb)
        dkv[rows, :] += add

    @pl.loop(0, nk)
    def _(k_index):
        needed, whole = block_state(seg_ref, start_ref, qi, k_index, bq, bk)

        @pl.when(needed & whole)
        def _():
            step(k_index, False)

        @pl.when(needed & jnp.logical_not(whole))
        def _():
            step(k_index, True)

    for h in range(heads):
        dq_ref[h * D : (h + 1) * D, :] = dacc[h * bq : (h + 1) * bq, :].T[:D, :] * D**-0.5

    @pl.when(qi == pl.num_programs(0) - 1)
    def _():
        lane = lax.broadcasted_iota(jnp.int32, dkv.shape, 1)
        dkv_ref[...] = (dkv[...] * jnp.where(lane < D, LN2, 1.0)).astype(bf16)


def attention_grad(start, seg, q, kv, o, do, l, qpos, qseg, kpos, kseg, bq, bk):
    heads = q.shape[0] // HEAD_DIM
    count, total = q.shape[1], kv.shape[0]
    bq, bk = min(bq, count), min(bk, total)
    whole = lambda *shape: pl.BlockSpec(shape, lambda i, *_: (0,) * len(shape))
    wide = pl.BlockSpec((q.shape[0], bq), lambda i, *_: (0, i))
    return pl.pallas_call(
        functools.partial(bwd_kernel, heads, bq, bk),
        out_shape=(
            jax.ShapeDtypeStruct(q.shape, f32),
            jax.ShapeDtypeStruct(kv.shape, bf16),
        ),
        grid_spec=pltpu.PrefetchScalarGridSpec(
            num_scalar_prefetch=2,
            grid=(count // bq,),
            in_specs=[
                wide,
                whole(*kv.shape),
                wide,
                wide,
                pl.BlockSpec((heads, bq), lambda i, *_: (0, i)),
                pl.BlockSpec((1, bq), lambda i, *_: (0, i)),
                pl.BlockSpec((1, bq), lambda i, *_: (0, i)),
                whole(total, 1),
                whole(total, 1),
            ],
            out_specs=(wide, whole(*kv.shape)),
            scratch_shapes=[
                pltpu.VMEM(kv.shape, bf16),
                pltpu.VMEM(kv.shape, bf16),
                pltpu.VMEM((heads * 2 * HEAD_DIM, bq), bf16),
                pltpu.VMEM((heads * 2 * HEAD_DIM, bq), bf16),
                pltpu.VMEM((heads * bq, 2 * HEAD_DIM), bf16),
                pltpu.VMEM((heads * bq, 2 * HEAD_DIM), bf16),
                pltpu.VMEM((heads * bq, 2 * HEAD_DIM), f32),
                pltpu.VMEM(kv.shape, f32),
            ],
        ),
        cost_estimate=pl.CostEstimate(flops=heads * count * total * 640, bytes_accessed=8 << 20, transcendentals=heads * count * total // 2),
        name="attend_grad",
    )(start, seg, q, kv, o, do, l, qpos.reshape(1, -1), qseg.reshape(1, -1), kpos.reshape(-1, 1), kseg.reshape(-1, 1))


HEADS = 16
KV_HEADS = 4
rope_base = 10000.0
SHARE = ("dp", "context")
EVERY = ("dp", "context", "tensor")
QUERY_BLOCK = 512
KEY_BLOCK = 512


def unit_rows(values):
    r = lax.rsqrt(jnp.mean(values * values, axis=-1, keepdims=True) + epsilon)
    return values * r, r


def norm_back(grad, values, gains):
    n, r = unit_rows(values)
    scaled = grad * gains
    return r * (scaled - n * jnp.mean(scaled * n, axis=-1, keepdims=True)), jnp.sum(grad * n, axis=0)


def mixed_silu(gate_in, up_in):
    return jax.nn.silu(gate_in) * up_in


def gathered(part, axes, axis):
    return lax.all_gather(part, axes, axis=axis, tiled=True)


def scattered(part, axes, axis):
    return lax.psum_scatter(part.astype(bf16), axes, scatter_dimension=axis, tiled=True)


def rope_tables(positions):
    half = HEAD_DIM // 2
    inverse = jnp.exp(-math.log(rope_base) * jnp.arange(half, dtype=f32) * 2.0 / HEAD_DIM)
    angles = inverse[:, None] * positions.astype(f32)[None, :]
    return jnp.cos(angles), jnp.sin(angles)


def body(
    layer_input, cotangent, w_qkv, w_out, attn_gain, qk_gain, w_gate, w_up, w_down, ffn_gain, seg_ids, pos_ids
):
    _, rows, width = layer_input.shape
    ways = lax.axis_size("tensor")
    heads = HEADS // ways
    mine = lax.axis_index("tensor")
    group_seg, group_pos = seg_ids[0], pos_ids[0]
    first_row = lax.axis_index("context") * rows
    my_seg = lax.dynamic_slice_in_dim(group_seg, first_row, rows, 0)
    my_pos = lax.dynamic_slice_in_dim(group_pos, first_row, rows, 0)
    start = jnp.reshape(first_row, (1,)).astype(jnp.int32)
    part_rows = rows // ways

    def own_rows(values):
        return lax.dynamic_slice_in_dim(values, mine * part_rows, part_rows, 0)

    columns = w_qkv.shape[1]
    qkv_shard = w_qkv.T
    packed = jnp.concatenate(
        [qkv_shard, attn_gain[None], ffn_gain[None], jnp.zeros((14, w_qkv.shape[0]), bf16)], axis=0
    )
    packed_all = gathered(packed, SHARE, 1)
    qkv_mine = packed_all[:columns]
    attn_gain_all = packed_all[columns].astype(f32)
    ffn_gain_all = packed_all[columns + 1].astype(f32)
    out_all = gathered(gathered(w_out, "tensor", 0), SHARE, 1)
    out_mine = lax.dynamic_slice_in_dim(out_all, mine * w_out.shape[0], w_out.shape[0], 0)
    gate_all = gathered(w_gate, SHARE, 0)
    up_all = gathered(w_up, SHARE, 0)
    down_all = gathered(w_down, SHARE, 1)
    qkv_all = gathered(gathered(qkv_shard, "tensor", 0), SHARE, 1)

    inputs = layer_input.reshape(rows, width).astype(f32)
    normed_low = (unit_rows(inputs)[0] * attn_gain_all).astype(bf16)
    joint = dot_nt(qkv_mine, normed_low)
    cos, sin = rope_tables(my_pos)
    gains = qk_gain.T
    queries, kv_mine = prep(joint, cos, sin, gains, heads, 512)
    kv = gathered(kv_mine, "context", 0)
    places = (my_pos, my_seg, group_pos, group_seg)
    attended, log_total = attention(start, group_seg, queries, kv, *places, QUERY_BLOCK, KEY_BLOCK)
    attended_all = gathered(attended, "tensor", 0)
    resid = inputs + dot_tn(attended_all, out_all)

    normed_ffn = (unit_rows(resid)[0] * ffn_gain_all).astype(bf16)
    gate = dot_nn(normed_ffn, gate_all)
    up = dot_nn(normed_ffn, up_all)
    act = mixed_silu(gate, up).astype(bf16)
    resid_part = own_rows(resid)
    ffn_part = scattered(dot_nn(act, down_all), "tensor", 0).astype(f32)
    layer_output = gathered((resid_part + ffn_part).astype(bf16), "tensor", 0)

    cot = cotangent.reshape(rows, width)
    act_grad = dot_nt(cot, down_all)
    _, silu_pull = jax.vjp(mixed_silu, gate, up)
    gate_grad, up_grad = (g.astype(bf16) for g in silu_pull(act_grad))
    ffn_in_grad = scattered(dot_nt(gate_grad, gate_all) + dot_nt(up_grad, up_all), "tensor", 0).astype(f32)
    grad_gate = dot_tn(normed_ffn, gate_grad)
    grad_up = dot_tn(normed_ffn, up_grad)
    grad_down = dot_tn(act, cot)
    norm_grad, ffn_gain_part = norm_back(ffn_in_grad, resid_part, ffn_gain_all)
    branch_part = (own_rows(cot).astype(f32) + norm_grad).astype(bf16)
    branch = gathered(branch_part, "tensor", 0)

    attended_grad = dot_nt(out_mine, branch).astype(bf16)
    grad_out = dot_nn(attended, branch)
    query_grad, kv_grad_group = attention_grad(
        start, group_seg, queries, kv, attended, attended_grad, log_total, *places, QUERY_BLOCK, KEY_BLOCK
    )
    kv_grad = scattered(kv_grad_group, "context", 0)
    joint_grad, qk_part = unprep(joint, cos, sin, gains, query_grad, kv_grad, heads, 512)
    joint_grad_all = gathered(joint_grad, "tensor", 0)
    grad_qkv = lax.dot_general(normed_low, joint_grad, (((0,), (1,)), ((), ())), preferred_element_type=f32)
    attn_gain_part = jnp.sum(qkv_mine.astype(f32) * grad_qkv.T, axis=0) / attn_gain_all
    in_grad = dot_tn(joint_grad_all, qkv_all)
    grad_input = (branch.astype(f32) + norm_back(in_grad, inputs, attn_gain_all)[0]).astype(bf16)

    small = lax.psum(jnp.concatenate([attn_gain_part, ffn_gain_part, qk_part.T.reshape(-1)]), EVERY)
    share = attn_gain.shape[0]
    place = (lax.axis_index("dp") * lax.axis_size("context") + lax.axis_index("context")) * share
    grad_attn_gain = lax.dynamic_slice_in_dim(small, place, share, 0)
    grad_ffn_gain = lax.dynamic_slice_in_dim(small, width + place, share, 0)
    grad_qk_gain = small[2 * width :].reshape(2, HEAD_DIM)
    return (
        layer_output.reshape(layer_input.shape),
        grad_input.reshape(layer_input.shape),
        scattered(grad_qkv, SHARE, 0).astype(f32),
        scattered(grad_out, SHARE, 1).astype(f32),
        grad_attn_gain,
        grad_qk_gain,
        scattered(grad_gate, SHARE, 0).astype(f32),
        scattered(grad_up, SHARE, 0).astype(f32),
        scattered(grad_down, SHARE, 1).astype(f32),
        grad_ffn_gain,
    )


def solution(mesh):
    tokens, by_row, by_column = P("dp", "context", None), P(SHARE, "tensor"), P("tensor", SHARE)
    gain = P(SHARE)
    return jax.shard_map(
        body,
        mesh=mesh,
        in_specs=(
            tokens, tokens, by_row, by_column, gain, P(), by_row, by_row, by_column, gain, P("dp", None), P("dp", None)
        ),
        out_specs=(tokens, tokens, by_row, by_column, gain, P(), by_row, by_row, by_column, gain),
        check_vma=False,
    )
```

```python
import functools, math
import jax, jax.numpy as jnp
from jax import lax
from jax.experimental import pallas as pl
from jax.experimental.pallas import tpu as pltpu
from jax.experimental.layout import Layout, with_layout_constraint
from jax.sharding import PartitionSpec as P

HEAD_DIM = 64
LOG2E = math.log2(math.e)
LN2 = math.log(2.0)
f32 = jnp.float32
bf16 = jnp.bfloat16
epsilon = 1e-6


def dot_nt(a, b):
    return lax.dot_general(a, b, (((1,), (1,)), ((), ())), preferred_element_type=f32)

def dot_nn(a, b):
    return lax.dot_general(a, b, (((1,), (0,)), ((), ())), preferred_element_type=f32)

def dot_tn(a, b):
    return lax.dot_general(a, b, (((0,), (0,)), ((), ())), preferred_element_type=f32)


def head_norm(x):
    return x * lax.rsqrt(jnp.mean(x * x, axis=0, keepdims=True) + epsilon)


def prep_kernel(heads, joint_ref, cos_ref, sin_ref, gain_ref, q_ref, kv_ref):
    half = HEAD_DIM // 2
    cos, sin = cos_ref[...], sin_ref[...]

    def one(row, gain, scale):
        x = head_norm(joint_ref[row : row + HEAD_DIM, :]) * gain
        lo, hi = x[:half], x[half:]
        return jnp.concatenate([lo * cos - hi * sin, hi * cos + lo * sin], axis=0) * scale

    for h in range(heads):
        row = h * HEAD_DIM
        q_ref[row : row + HEAD_DIM, :] = one(row, gain_ref[:, 0:1], LOG2E * HEAD_DIM**-0.5).astype(bf16)
    row = heads * HEAD_DIM
    key = one(row, gain_ref[:, 1:2], 1.0)
    both = jnp.concatenate([key, joint_ref[row + HEAD_DIM : row + 2 * HEAD_DIM, :]], axis=0)
    kv_ref[...] = both.T.astype(bf16)


def prep(joint, cos, sin, gains, heads, block):
    rows, count = joint.shape
    block = min(block, count)
    return pl.pallas_call(
        functools.partial(prep_kernel, heads),
        out_shape=(
            jax.ShapeDtypeStruct((heads * HEAD_DIM, count), bf16),
            jax.ShapeDtypeStruct((count, 2 * HEAD_DIM), bf16),
        ),
        grid=(count // block,),
        in_specs=[
            pl.BlockSpec((rows, block), lambda i: (0, i)),
            pl.BlockSpec((HEAD_DIM // 2, block), lambda i: (0, i)),
            pl.BlockSpec((HEAD_DIM // 2, block), lambda i: (0, i)),
            pl.BlockSpec((HEAD_DIM, 2), lambda i: (0, 0)),
        ],
        out_specs=(
            pl.BlockSpec((heads * HEAD_DIM, block), lambda i: (0, i)),
            pl.BlockSpec((block, 2 * HEAD_DIM), lambda i: (i, 0)),
        ),
        cost_estimate=pl.CostEstimate(flops=rows * count * 20, bytes_accessed=rows * count * 6, transcendentals=0),
        name="prep",
    )(joint, cos, sin, gains)


def unprep_kernel(heads, joint_ref, cos_ref, sin_ref, gain_ref, dq_ref, dkv_ref, out_ref, dgain_ref):
    half = HEAD_DIM // 2
    cos, sin = cos_ref[...], sin_ref[...]

    @pl.when(pl.program_id(0) == 0)
    def _():
        dgain_ref[...] = jnp.zeros_like(dgain_ref)

    def one(row, grad, gain):
        x = joint_ref[row : row + HEAD_DIM, :]
        r = lax.rsqrt(jnp.mean(x * x, axis=0, keepdims=True) + epsilon)
        n = x * r
        lo, hi = grad[:half], grad[half:]
        back = jnp.concatenate([lo * cos + hi * sin, hi * cos - lo * sin], axis=0)
        scaled = back * gain
        result = r * (scaled - n * jnp.mean(scaled * n, axis=0, keepdims=True))
        out_ref[row : row + HEAD_DIM, :] = result.astype(bf16)
        return jnp.sum(back * n, axis=1, keepdims=True)

    total = None
    for h in range(heads):
        row = h * HEAD_DIM
        part = one(row, dq_ref[row : row + HEAD_DIM, :], gain_ref[:, 0:1])
        total = part if total is None else total + part
    row = heads * HEAD_DIM
    dkv = dkv_ref[...].astype(f32).T
    part = one(row, dkv[:HEAD_DIM], gain_ref[:, 1:2])
    out_ref[row + HEAD_DIM : row + 2 * HEAD_DIM, :] = dkv[HEAD_DIM:].astype(bf16)
    dgain_ref[...] += jnp.concatenate([total, part], axis=1)


def unprep(joint, cos, sin, gains, dq, dkv, heads, block):
    rows, count = joint.shape
    block = min(block, count)
    return pl.pallas_call(
        functools.partial(unprep_kernel, heads),
        out_shape=(
            jax.ShapeDtypeStruct((rows, count), bf16),
            jax.ShapeDtypeStruct((HEAD_DIM, 2), f32),
        ),
        grid=(count // block,),
        in_specs=[
            pl.BlockSpec((rows, block), lambda i: (0, i)),
            pl.BlockSpec((HEAD_DIM // 2, block), lambda i: (0, i)),
            pl.BlockSpec((HEAD_DIM // 2, block), lambda i: (0, i)),
            pl.BlockSpec((HEAD_DIM, 2), lambda i: (0, 0)),
            pl.BlockSpec((heads * HEAD_DIM, block), lambda i: (0, i)),
            pl.BlockSpec((block, 2 * HEAD_DIM), lambda i: (i, 0)),
        ],
        out_specs=(
            pl.BlockSpec((rows, block), lambda i: (0, i)),
            pl.BlockSpec((HEAD_DIM, 2), lambda i: (0, 0)),
        ),
        cost_estimate=pl.CostEstimate(flops=rows * count * 30, bytes_accessed=rows * count * 10, transcendentals=0),
        name="unprep",
    )(joint, cos, sin, gains, dq, dkv)


def block_state(seg_ref, start_ref, q_index, k_index, bq, bk):
    q_first = start_ref[0] + q_index * bq
    k_first = k_index * bk
    k_last_seg = seg_ref[k_first + bk - 1]
    needed = (k_first <= q_first + bq - 1) & ((k_last_seg == 0) | (k_last_seg >= seg_ref[q_first]) | (seg_ref[k_first] == 0))
    whole = (k_last_seg == 0) & (k_first + bk - 1 <= q_first)
    return needed, whole


def fwd_kernel(heads, bq, bk, start_ref, seg_ref, q_ref, kv_ref, qpos_ref, qseg_ref, kpos_ref, kseg_ref, o_ref, l_ref, vaug, qs, acc):
    qi = pl.program_id(0)
    nk = kv_ref.shape[0] // bk
    lane = lax.broadcasted_iota(jnp.int32, kv_ref.shape, 1)

    @pl.when(qi == 0)
    def _():
        vaug[...] = jnp.where(lane >= HEAD_DIM, kv_ref[...].astype(f32), jnp.where(lane == 0, 1.0, 0.0)).astype(bf16)

    zeros = jnp.zeros((HEAD_DIM, bq), f32)
    for h in range(heads):
        full = jnp.concatenate([q_ref[h * HEAD_DIM : (h + 1) * HEAD_DIM, :].astype(f32), zeros], axis=0)
        qs[h * bq : (h + 1) * bq, :] = full.T.astype(bf16)
    acc[...] = jnp.zeros_like(acc)

    def step(k_index, masked):
        rows = pl.ds(pl.multiple_of(k_index * bk, bk), bk)
        kb, vb = kv_ref[rows, :], vaug[rows, :]
        if masked:
            kseg = kseg_ref[k_index]
            mask = (kpos_ref[k_index] <= qpos_ref[...]) & ((kseg == 0) | (kseg == qseg_ref[...]))
        for h in range(heads):
            s = dot_nt(qs[h * bq : (h + 1) * bq, :], kb)
            p = jnp.exp2(s)
            if masked:
                p = jnp.where(mask, p, 0.0)
            acc[h * bq : (h + 1) * bq, :] += dot_nn(p.astype(bf16), vb)

    @pl.loop(0, nk)
    def _(k_index):
        needed, whole = block_state(seg_ref, start_ref, qi, k_index, bq, bk)

        @pl.when(needed & whole)
        def _():
            step(k_index, False)

        @pl.when(needed & jnp.logical_not(whole))
        def _():
            step(k_index, True)

    for h in range(heads):
        out = acc[h * bq : (h + 1) * bq, :].T
        total = out[0:1, :]
        o_ref[h * HEAD_DIM : (h + 1) * HEAD_DIM, :] = (out[HEAD_DIM:, :] / total).astype(bf16)
        l_ref[h : h + 1, :] = jnp.log2(total)


def attention(start, seg, q, kv, qpos, qseg, kpos, kseg, bq, bk):
    heads = q.shape[0] // HEAD_DIM
    count, total = q.shape[1], kv.shape[0]
    bq, bk = min(bq, count), min(bk, total)
    whole = lambda *shape: pl.BlockSpec(shape, lambda i, *_: (0,) * len(shape))
    return pl.pallas_call(
        functools.partial(fwd_kernel, heads, bq, bk),
        out_shape=(
            jax.ShapeDtypeStruct(q.shape, bf16),
            jax.ShapeDtypeStruct((heads, count), f32),
        ),
        grid_spec=pltpu.PrefetchScalarGridSpec(
            num_scalar_prefetch=2,
            grid=(count // bq,),
            in_specs=[
                pl.BlockSpec((q.shape[0], bq), lambda i, *_: (0, i)),
                whole(*kv.shape),
                pl.BlockSpec((bq, 1), lambda i, *_: (i, 0)),
                pl.BlockSpec((bq, 1), lambda i, *_: (i, 0)),
                whole(total // bk, 1, bk),
                whole(total // bk, 1, bk),
            ],
            out_specs=(
                pl.BlockSpec((q.shape[0], bq), lambda i, *_: (0, i)),
                pl.BlockSpec((heads, bq), lambda i, *_: (0, i)),
            ),
            scratch_shapes=[
                pltpu.VMEM(kv.shape, bf16),
                pltpu.VMEM((heads * bq, 2 * HEAD_DIM), bf16),
                pltpu.VMEM((heads * bq, 2 * HEAD_DIM), f32),
            ],
        ),
        cost_estimate=pl.CostEstimate(flops=heads * count * total * 256, bytes_accessed=4 << 20, transcendentals=heads * count * total // 2),
        name="attend",
    )(start, seg, q, kv, qpos.reshape(-1, 1), qseg.reshape(-1, 1), kpos.reshape(-1, 1, bk), kseg.reshape(-1, 1, bk))


def split3(x):
    a = x.astype(bf16).astype(f32)
    b = (x - a).astype(bf16).astype(f32)
    return a, b, x - a - b


def bwd_kernel(heads, bq, bk, start_ref, seg_ref, q_ref, kv_ref, o_ref, do_ref, l_ref, qpos_ref, qseg_ref, kpos_ref, kseg_ref,
               dq_ref, dkv_ref, kaug, vaug, qst, dst, qs, ds, dacc, dkv):
    qi = pl.program_id(0)
    nk = kv_ref.shape[0] // bk
    D = HEAD_DIM

    @pl.when(qi == 0)
    def _():
        lane = lax.broadcasted_iota(jnp.int32, kv_ref.shape, 1)
        kv = kv_ref[...].astype(f32)
        kaug[...] = jnp.where(lane < D, kv, jnp.where(lane < D + 3, -1.0, 0.0)).astype(bf16)
        vaug[...] = jnp.where(lane >= D, kv, jnp.where(lane < 3, -1.0, 0.0)).astype(bf16)
        dkv[...] = jnp.zeros_like(dkv)

    row = lax.broadcasted_iota(jnp.int32, (D, bq), 0)

    def extra(x):
        a, b, c = split3(x)
        return jnp.where(row == 0, a, jnp.where(row == 1, b, jnp.where(row == 2, c, 0.0)))

    zeros = jnp.zeros((D, bq), f32)
    for h in range(heads):
        part = slice(h * D, (h + 1) * D)
        wide = slice(h * 2 * D, (h + 1) * 2 * D)
        q, do, o = q_ref[part, :].astype(f32), do_ref[part, :].astype(f32), o_ref[part, :].astype(f32)
        delta = jnp.sum(do * o, axis=0, keepdims=True)
        qst[wide, :] = jnp.concatenate([q, extra(l_ref[h : h + 1, :])], axis=0).astype(bf16)
        dst[wide, :] = jnp.concatenate([extra(delta), do], axis=0).astype(bf16)
        qs[h * bq : (h + 1) * bq, :] = jnp.concatenate([q, zeros], axis=0).T.astype(bf16)
        ds[h * bq : (h + 1) * bq, :] = jnp.concatenate([zeros, do], axis=0).T.astype(bf16)
    dacc[...] = jnp.zeros_like(dacc)

    def step(k_index, masked):
        rows = pl.ds(pl.multiple_of(k_index * bk, bk), bk)
        kb, vb, kvb = kaug[rows, :], vaug[rows, :], kv_ref[rows, :]
        if masked:
            kseg = kseg_ref[rows, :]
            mask = (kpos_ref[rows, :] <= qpos_ref[...]) & ((kseg == 0) | (kseg == qseg_ref[...]))
        add = None
        for h in range(heads):
            wide = slice(h * 2 * D, (h + 1) * 2 * D)
            tall = slice(h * bq, (h + 1) * bq)
            p = jnp.exp2(dot_nn(kb, qst[wide, :]))
            if masked:
                p = jnp.where(mask, p, 0.0)
            sg = (p * dot_nn(vb, dst[wide, :])).astype(bf16)
            part = dot_nn(sg, qs[tall, :]) + dot_nn(p.astype(bf16), ds[tall, :])
            add = part if add is None else add + part
            dacc[tall, :] += dot_tn(sg, kvb)
        dkv[rows, :] += add

    @pl.loop(0, nk)
    def _(k_index):
        needed, whole = block_state(seg_ref, start_ref, qi, k_index, bq, bk)

        @pl.when(needed & whole)
        def _():
            step(k_index, False)

        @pl.when(needed & jnp.logical_not(whole))
        def _():
            step(k_index, True)

    for h in range(heads):
        dq_ref[h * D : (h + 1) * D, :] = dacc[h * bq : (h + 1) * bq, :].T[:D, :] * D**-0.5

    @pl.when(qi == pl.num_programs(0) - 1)
    def _():
        lane = lax.broadcasted_iota(jnp.int32, dkv.shape, 1)
        dkv_ref[...] = (dkv[...] * jnp.where(lane < D, LN2, 1.0)).astype(bf16)


def attention_grad(start, seg, q, kv, o, do, l, qpos, qseg, kpos, kseg, bq, bk):
    heads = q.shape[0] // HEAD_DIM
    count, total = q.shape[1], kv.shape[0]
    bq, bk = min(bq, count), min(bk, total)
    whole = lambda *shape: pl.BlockSpec(shape, lambda i, *_: (0,) * len(shape))
    wide = pl.BlockSpec((q.shape[0], bq), lambda i, *_: (0, i))
    return pl.pallas_call(
        functools.partial(bwd_kernel, heads, bq, bk),
        out_shape=(
            jax.ShapeDtypeStruct(q.shape, f32),
            jax.ShapeDtypeStruct(kv.shape, bf16),
        ),
        grid_spec=pltpu.PrefetchScalarGridSpec(
            num_scalar_prefetch=2,
            grid=(count // bq,),
            in_specs=[
                wide,
                whole(*kv.shape),
                wide,
                wide,
                pl.BlockSpec((heads, bq), lambda i, *_: (0, i)),
                pl.BlockSpec((1, bq), lambda i, *_: (0, i)),
                pl.BlockSpec((1, bq), lambda i, *_: (0, i)),
                whole(total, 1),
                whole(total, 1),
            ],
            out_specs=(wide, whole(*kv.shape)),
            scratch_shapes=[
                pltpu.VMEM(kv.shape, bf16),
                pltpu.VMEM(kv.shape, bf16),
                pltpu.VMEM((heads * 2 * HEAD_DIM, bq), bf16),
                pltpu.VMEM((heads * 2 * HEAD_DIM, bq), bf16),
                pltpu.VMEM((heads * bq, 2 * HEAD_DIM), bf16),
                pltpu.VMEM((heads * bq, 2 * HEAD_DIM), bf16),
                pltpu.VMEM((heads * bq, 2 * HEAD_DIM), f32),
                pltpu.VMEM(kv.shape, f32),
            ],
        ),
        cost_estimate=pl.CostEstimate(flops=heads * count * total * 640, bytes_accessed=8 << 20, transcendentals=heads * count * total // 2),
        name="attend_grad",
    )(start, seg, q, kv, o, do, l, qpos.reshape(1, -1), qseg.reshape(1, -1), kpos.reshape(-1, 1), kseg.reshape(-1, 1))


HEADS = 16
KV_HEADS = 4
rope_base = 10000.0
SHARE = ("dp", "context")
EVERY = ("dp", "context", "tensor")
QUERY_BLOCK = 512
KEY_BLOCK = 512


def unit_rows(values):
    r = lax.rsqrt(jnp.mean(values * values, axis=-1, keepdims=True) + epsilon)
    return values * r, r


def norm_back(grad, values, gains):
    n, r = unit_rows(values)
    scaled = grad * gains
    return r * (scaled - n * jnp.mean(scaled * n, axis=-1, keepdims=True)), jnp.sum(grad * n, axis=0)


def mixed_silu(gate_in, up_in):
    return jax.nn.silu(gate_in) * up_in


def gathered(part, axes, axis):
    return lax.all_gather(part, axes, axis=axis, tiled=True)


def scattered(part, axes, axis):
    return lax.psum_scatter(part.astype(bf16), axes, scatter_dimension=axis, tiled=True)


def natural(values):
    return with_layout_constraint(values, Layout(major_to_minor=tuple(range(values.ndim))))


def after(value, *others):
    return lax.optimization_barrier((value,) + others)[0]


def both_halves(part):
    if lax.axis_size("context") != 2:
        return gathered(part, "context", 0)
    other = lax.ppermute(part, "context", [(0, 1), (1, 0)])
    low = lax.axis_index("context") == 0
    return jnp.concatenate([jnp.where(low, part, other), jnp.where(low, other, part)], axis=0)


def halving_scatter(terms, axes):
    sizes = [lax.axis_size(axis) for axis in axes]
    blocks = terms.reshape(tuple(sizes) + (-1,) + terms.shape[1:])
    for place, axis in enumerate(axes):
        size, me = sizes[place], lax.axis_index(axis)
        stride = 1
        while stride < size:
            shape = blocks.shape
            split = blocks.reshape(shape[:place] + (shape[place] // 2, 2) + shape[place + 1 :])
            bit = (me // stride) % 2
            kept, sent = (
                lax.dynamic_index_in_dim(split, index, place + 1, keepdims=False) for index in (bit, 1 - bit)
            )
            got = lax.ppermute(sent, axis, [(i, i ^ stride) for i in range(size)])
            blocks = (kept.astype(f32) + got.astype(f32)).astype(bf16)
            stride *= 2
    return blocks.reshape((-1,) + terms.shape[1:])


def spread(part):
    ways, me = lax.axis_size("tensor"), lax.axis_index("tensor")
    out = lax.dynamic_update_index_in_dim(jnp.zeros((ways,) + part.shape, part.dtype), part, me, 0)
    for step in range(1, ways):
        got = lax.ppermute(part, "tensor", [(i, (i + step) % ways) for i in range(ways)])
        out = lax.dynamic_update_index_in_dim(out, got, (me - step) % ways, 0)
    return out


def line_total(part):
    total = part
    ways = lax.axis_size("tensor")
    for step in range(1, ways):
        total = total + lax.ppermute(part, "tensor", [(i, (i + step) % ways) for i in range(ways)])
    return total


def swap(blocks):
    ways, me = lax.axis_size("tensor"), lax.axis_index("tensor")
    out = blocks
    for step in range(1, ways):
        sent = lax.dynamic_index_in_dim(blocks, (me + step) % ways, 0, keepdims=False)
        got = lax.ppermute(sent, "tensor", [(i, (i + step) % ways) for i in range(ways)])
        out = lax.dynamic_update_index_in_dim(out, got, (me - step) % ways, 0)
    return out


def rope_tables(positions):
    half = HEAD_DIM // 2
    inverse = jnp.exp(-math.log(rope_base) * jnp.arange(half, dtype=f32) * 2.0 / HEAD_DIM)
    angles = inverse[:, None] * positions.astype(f32)[None, :]
    return jnp.cos(angles), jnp.sin(angles)


def body(
    layer_input, cotangent, w_qkv, w_out, attn_gain, qk_gain, w_gate, w_up, w_down, ffn_gain, seg_ids, pos_ids
):
    _, rows, width = layer_input.shape
    ways = lax.axis_size("tensor")
    heads = HEADS // ways
    mine = lax.axis_index("tensor")
    group_seg, group_pos = seg_ids[0], pos_ids[0]
    first_row = lax.axis_index("context") * rows
    my_seg = lax.dynamic_slice_in_dim(group_seg, first_row, rows, 0)
    my_pos = lax.dynamic_slice_in_dim(group_pos, first_row, rows, 0)
    start = jnp.reshape(first_row, (1,)).astype(jnp.int32)
    part_rows = rows // ways

    def own_rows(values):
        return lax.dynamic_slice_in_dim(values, mine * part_rows, part_rows, 0)

    columns = w_qkv.shape[1]
    qkv_shard = w_qkv.T
    packed = jnp.concatenate(
        [qkv_shard, attn_gain[None], ffn_gain[None], jnp.zeros((14, w_qkv.shape[0]), bf16)], axis=0
    )
    packed_all = gathered(packed, SHARE, 1)
    qkv_mine = packed_all[:columns]
    attn_gain_all = packed_all[columns].astype(f32)
    ffn_gain_all = packed_all[columns + 1].astype(f32)
    out_all = gathered(spread(w_out).reshape(ways * w_out.shape[0], -1), SHARE, 1)
    gate_all = gathered(w_gate, SHARE, 0)
    up_all = gathered(w_up, SHARE, 0)
    down_all = gathered(w_down, SHARE, 1)
    qkv_all = gathered(spread(qkv_shard).reshape(ways * columns, -1), SHARE, 1)

    inputs = layer_input.reshape(rows, width).astype(f32)
    cot = cotangent.reshape(rows, width)
    normed_low = (unit_rows(inputs)[0] * attn_gain_all).astype(bf16)
    joint = dot_nt(qkv_mine, normed_low)
    cos, sin = rope_tables(my_pos)
    gains = qk_gain.T
    queries, kv_mine = prep(joint, cos, sin, gains, heads, 512)
    kv = both_halves(kv_mine)
    places = (my_pos, my_seg, group_pos, group_seg)
    attended, log_total = attention(start, group_seg, queries, kv, *places, QUERY_BLOCK, KEY_BLOCK)
    attended_all = gathered(attended, "tensor", 0)
    act_grad = dot_nt(after(cot, attended), down_all)
    resid = inputs + natural(dot_tn(attended_all, out_all))

    normed_ffn = (unit_rows(resid)[0] * ffn_gain_all).astype(bf16)
    gate = dot_nn(after(normed_ffn, act_grad), gate_all)
    up = dot_nn(normed_ffn, up_all)
    act, silu_pull = jax.vjp(mixed_silu, gate, up)
    act = act.astype(bf16)
    gate_grad, up_grad = (g.astype(bf16) for g in silu_pull(act_grad))
    ffn_in_part = (dot_nt(gate_grad, gate_all) + dot_nt(up_grad, up_all)).astype(bf16)
    ffn_in_grad = scattered(ffn_in_part, "tensor", 0).astype(f32)
    act, gate_grad, up_grad, _ = lax.optimization_barrier((act, gate_grad, up_grad, ffn_in_part))
    ffn_part = dot_nn(act, down_all).astype(bf16)
    grad_down = dot_tn(cot, act).astype(bf16)
    grad_gate = dot_tn(normed_ffn, gate_grad).astype(bf16)
    grad_up = dot_tn(normed_ffn, up_grad).astype(bf16)
    resid_part = own_rows(resid)
    norm_grad, ffn_gain_part = norm_back(ffn_in_grad, resid_part, ffn_gain_all)
    resid_grad = own_rows(cot).astype(f32) + norm_grad
    branch = after(resid_grad.astype(bf16), ffn_part, grad_down, grad_gate, grad_up)

    attended_grad = dot_nt(out_all, branch).astype(bf16)
    attended_grad = swap(attended_grad.reshape(ways, heads * HEAD_DIM, part_rows))
    attended_grad = jnp.concatenate([attended_grad[i] for i in range(ways)], axis=1)
    ffn_sum = scattered(ffn_part, "tensor", 0).astype(f32)
    layer_output = gathered((resid_part + ffn_sum).astype(bf16), "tensor", 0)
    attended_part = lax.dynamic_slice_in_dim(attended_all, mine * part_rows, part_rows, 1)
    grad_out = lax.dot_general(branch, attended_part, (((0,), (1,)), ((), ())), preferred_element_type=f32)
    grad_out = halving_scatter(grad_out.astype(bf16), SHARE)
    grad_out = swap(jnp.stack([part.T for part in jnp.split(grad_out, ways, axis=1)]))
    query_grad, kv_grad_group = attention_grad(
        start, group_seg, queries, kv, attended, attended_grad, log_total, *places, QUERY_BLOCK, KEY_BLOCK
    )
    kv_grad = halving_scatter(kv_grad_group, ("context",))
    joint_grad, qk_part = unprep(joint, cos, sin, gains, query_grad, kv_grad, heads, 512)
    joint_grad_part = swap(jnp.stack([joint_grad[:, i * part_rows : (i + 1) * part_rows] for i in range(ways)]))
    in_grad = natural(dot_tn(joint_grad_part.reshape(ways * columns, part_rows), qkv_all))
    grad_qkv = dot_nn(joint_grad, normed_low)
    attn_gain_part = jnp.sum(qkv_mine.astype(f32) * grad_qkv, axis=0) / attn_gain_all
    norm_grad = norm_back(in_grad, own_rows(inputs), attn_gain_all)[0]
    grad_input = gathered((resid_grad + norm_grad).astype(bf16), "tensor", 0)

    share = attn_gain.shape[0]
    qk_rows = jnp.tile(qk_part.T, (1, width // HEAD_DIM))
    grad_qkv = jnp.concatenate(
        [grad_qkv, attn_gain_part[None], ffn_gain_part[None], qk_rows, jnp.zeros((12, width), f32)], axis=0
    )
    grad_qkv = halving_scatter(grad_qkv.astype(bf16).T, SHARE).astype(f32)
    small = line_total(grad_qkv[:, columns:].T)
    return (
        layer_output.reshape(layer_input.shape),
        grad_input.reshape(layer_input.shape),
        grad_qkv[:, :columns],
        jnp.sum(grad_out.astype(f32), axis=0),
        small[0],
        small[2:4, :HEAD_DIM],
        halving_scatter(grad_gate, SHARE).astype(f32),
        halving_scatter(grad_up, SHARE).astype(f32),
        halving_scatter(grad_down, SHARE).astype(f32).T,
        small[1],
    )


def solution(mesh):
    tokens, by_row, by_column = P("dp", "context", None), P(SHARE, "tensor"), P("tensor", SHARE)
    gain = P(SHARE)
    return jax.shard_map(
        body,
        mesh=mesh,
        in_specs=(
            tokens, tokens, by_row, by_column, gain, P(), by_row, by_row, by_column, gain, P("dp", None), P("dp", None)
        ),
        out_specs=(tokens, tokens, by_row, by_column, gain, P(), by_row, by_row, by_column, gain),
        check_vma=False,
    )
```

```python
import functools, math
import jax, jax.numpy as jnp
from jax import lax
from jax.experimental import pallas as pl
from jax.experimental.pallas import tpu as pltpu
from jax.experimental.layout import Layout, with_layout_constraint
from jax.sharding import PartitionSpec as P

HEAD_DIM = 64
LOG2E = math.log2(math.e)
LN2 = math.log(2.0)
f32 = jnp.float32
bf16 = jnp.bfloat16
epsilon = 1e-6


def dot_nt(a, b):
    return lax.dot_general(a, b, (((1,), (1,)), ((), ())), preferred_element_type=f32)

def dot_nn(a, b):
    return lax.dot_general(a, b, (((1,), (0,)), ((), ())), preferred_element_type=f32)

def dot_tn(a, b):
    return lax.dot_general(a, b, (((0,), (0,)), ((), ())), preferred_element_type=f32)


def dot_tt(a, b):
    return lax.dot_general(a, b, (((0,), (1,)), ((), ())), preferred_element_type=f32)


def head_norm(x):
    return x * lax.rsqrt(jnp.mean(x * x, axis=0, keepdims=True) + epsilon)


def prep_kernel(heads, joint_ref, cos_ref, sin_ref, gain_ref, q_ref, kv_ref):
    half = HEAD_DIM // 2
    cos, sin = cos_ref[...], sin_ref[...]

    def one(row, gain, scale):
        x = head_norm(joint_ref[row : row + HEAD_DIM, :]) * gain
        lo, hi = x[:half], x[half:]
        return jnp.concatenate([lo * cos - hi * sin, hi * cos + lo * sin], axis=0) * scale

    for h in range(heads):
        row = h * HEAD_DIM
        q_ref[row : row + HEAD_DIM, :] = one(row, gain_ref[:, 0:1], LOG2E * HEAD_DIM**-0.5).astype(bf16)
    row = heads * HEAD_DIM
    key = one(row, gain_ref[:, 1:2], 1.0)
    both = jnp.concatenate([key, joint_ref[row + HEAD_DIM : row + 2 * HEAD_DIM, :]], axis=0)
    kv_ref[...] = both.T.astype(bf16)


def prep(joint, cos, sin, gains, heads, block):
    rows, count = joint.shape
    block = min(block, count)
    return pl.pallas_call(
        functools.partial(prep_kernel, heads),
        out_shape=(
            jax.ShapeDtypeStruct((heads * HEAD_DIM, count), bf16),
            jax.ShapeDtypeStruct((count, 2 * HEAD_DIM), bf16),
        ),
        grid=(count // block,),
        in_specs=[
            pl.BlockSpec((rows, block), lambda i: (0, i)),
            pl.BlockSpec((HEAD_DIM // 2, block), lambda i: (0, i)),
            pl.BlockSpec((HEAD_DIM // 2, block), lambda i: (0, i)),
            pl.BlockSpec((HEAD_DIM, 2), lambda i: (0, 0)),
        ],
        out_specs=(
            pl.BlockSpec((heads * HEAD_DIM, block), lambda i: (0, i)),
            pl.BlockSpec((block, 2 * HEAD_DIM), lambda i: (i, 0)),
        ),
        cost_estimate=pl.CostEstimate(flops=rows * count * 20, bytes_accessed=rows * count * 6, transcendentals=0),
        name="prep",
    )(joint, cos, sin, gains)


def unprep_kernel(heads, joint_ref, cos_ref, sin_ref, gain_ref, dq_ref, dkv_ref, out_ref, dgain_ref):
    half = HEAD_DIM // 2
    cos, sin = cos_ref[...], sin_ref[...]

    @pl.when(pl.program_id(0) == 0)
    def _():
        dgain_ref[...] = jnp.zeros_like(dgain_ref)

    def one(row, grad, gain):
        x = joint_ref[row : row + HEAD_DIM, :]
        r = lax.rsqrt(jnp.mean(x * x, axis=0, keepdims=True) + epsilon)
        n = x * r
        lo, hi = grad[:half], grad[half:]
        back = jnp.concatenate([lo * cos + hi * sin, hi * cos - lo * sin], axis=0)
        scaled = back * gain
        result = r * (scaled - n * jnp.mean(scaled * n, axis=0, keepdims=True))
        out_ref[row : row + HEAD_DIM, :] = result.astype(bf16)
        return jnp.sum(back * n, axis=1, keepdims=True)

    total = None
    for h in range(heads):
        row = h * HEAD_DIM
        part = one(row, dq_ref[row : row + HEAD_DIM, :], gain_ref[:, 0:1])
        total = part if total is None else total + part
    row = heads * HEAD_DIM
    dkv = dkv_ref[...].astype(f32).T
    part = one(row, dkv[:HEAD_DIM], gain_ref[:, 1:2])
    out_ref[row + HEAD_DIM : row + 2 * HEAD_DIM, :] = dkv[HEAD_DIM:].astype(bf16)
    dgain_ref[...] += jnp.concatenate([total, part], axis=1)


def unprep(joint, cos, sin, gains, dq, dkv, heads, block):
    rows, count = joint.shape
    block = min(block, count)
    return pl.pallas_call(
        functools.partial(unprep_kernel, heads),
        out_shape=(
            jax.ShapeDtypeStruct((rows, count), bf16),
            jax.ShapeDtypeStruct((HEAD_DIM, 2), f32),
        ),
        grid=(count // block,),
        in_specs=[
            pl.BlockSpec((rows, block), lambda i: (0, i)),
            pl.BlockSpec((HEAD_DIM // 2, block), lambda i: (0, i)),
            pl.BlockSpec((HEAD_DIM // 2, block), lambda i: (0, i)),
            pl.BlockSpec((HEAD_DIM, 2), lambda i: (0, 0)),
            pl.BlockSpec((heads * HEAD_DIM, block), lambda i: (0, i)),
            pl.BlockSpec((block, 2 * HEAD_DIM), lambda i: (i, 0)),
        ],
        out_specs=(
            pl.BlockSpec((rows, block), lambda i: (0, i)),
            pl.BlockSpec((HEAD_DIM, 2), lambda i: (0, 0)),
        ),
        cost_estimate=pl.CostEstimate(flops=rows * count * 30, bytes_accessed=rows * count * 10, transcendentals=0),
        name="unprep",
    )(joint, cos, sin, gains, dq, dkv)


def block_state(seg_ref, start_ref, q_index, k_index, bq, bk):
    q_first = start_ref[0] + q_index * bq
    k_first = k_index * bk
    k_last_seg = seg_ref[k_first + bk - 1]
    needed = (k_first <= q_first + bq - 1) & ((k_last_seg == 0) | (k_last_seg >= seg_ref[q_first]) | (seg_ref[k_first] == 0))
    whole = (k_last_seg == 0) & (k_first + bk - 1 <= q_first)
    return needed, whole


def fwd_kernel(heads, bq, bk, start_ref, seg_ref, q_ref, kv_ref, qpos_ref, qseg_ref, kpos_ref, kseg_ref, o_ref, l_ref, vaug, qs, acc):
    qi = pl.program_id(0)
    nk = kv_ref.shape[0] // bk
    lane = lax.broadcasted_iota(jnp.int32, kv_ref.shape, 1)

    @pl.when(qi == 0)
    def _():
        vaug[...] = jnp.where(lane >= HEAD_DIM, kv_ref[...].astype(f32), jnp.where(lane == 0, 1.0, 0.0)).astype(bf16)

    zeros = jnp.zeros((HEAD_DIM, bq), f32)
    for h in range(heads):
        full = jnp.concatenate([q_ref[h * HEAD_DIM : (h + 1) * HEAD_DIM, :].astype(f32), zeros], axis=0)
        qs[h * bq : (h + 1) * bq, :] = full.T.astype(bf16)
    acc[...] = jnp.zeros_like(acc)

    def step(k_index, masked):
        rows = pl.ds(pl.multiple_of(k_index * bk, bk), bk)
        kb, vb = kv_ref[rows, :], vaug[rows, :]
        if masked:
            kseg = kseg_ref[k_index]
            mask = (kpos_ref[k_index] <= qpos_ref[...]) & ((kseg == 0) | (kseg == qseg_ref[...]))
        for h in range(heads):
            s = dot_nt(qs[h * bq : (h + 1) * bq, :], kb)
            p = jnp.exp2(s)
            if masked:
                p = jnp.where(mask, p, 0.0)
            acc[h * bq : (h + 1) * bq, :] += dot_nn(p.astype(bf16), vb)

    @pl.loop(0, nk)
    def _(k_index):
        needed, whole = block_state(seg_ref, start_ref, qi, k_index, bq, bk)

        @pl.when(needed & whole)
        def _():
            step(k_index, False)

        @pl.when(needed & jnp.logical_not(whole))
        def _():
            step(k_index, True)

    for h in range(heads):
        out = acc[h * bq : (h + 1) * bq, :].T
        total = out[0:1, :]
        o_ref[h * HEAD_DIM : (h + 1) * HEAD_DIM, :] = (out[HEAD_DIM:, :] / total).astype(bf16)
        l_ref[h : h + 1, :] = jnp.log2(total)


def attention(start, seg, q, kv, qpos, qseg, kpos, kseg, bq, bk, part, parts):
    heads = q.shape[0] // HEAD_DIM
    count, total = q.shape[1] // parts, kv.shape[0]
    bq, bk = min(bq, count), min(bk, total)
    first = part * (count // bq)
    whole = lambda *shape: pl.BlockSpec(shape, lambda i, *_: (0,) * len(shape))
    return pl.pallas_call(
        functools.partial(fwd_kernel, heads, bq, bk),
        out_shape=(
            jax.ShapeDtypeStruct((q.shape[0], count), bf16),
            jax.ShapeDtypeStruct((heads, count), f32),
        ),
        grid_spec=pltpu.PrefetchScalarGridSpec(
            num_scalar_prefetch=2,
            grid=(count // bq,),
            in_specs=[
                pl.BlockSpec((q.shape[0], bq), lambda i, *_: (0, i + first)),
                whole(*kv.shape),
                pl.BlockSpec((bq, 1), lambda i, *_: (i + first, 0)),
                pl.BlockSpec((bq, 1), lambda i, *_: (i + first, 0)),
                whole(total // bk, 1, bk),
                whole(total // bk, 1, bk),
            ],
            out_specs=(
                pl.BlockSpec((q.shape[0], bq), lambda i, *_: (0, i)),
                pl.BlockSpec((heads, bq), lambda i, *_: (0, i)),
            ),
            scratch_shapes=[
                pltpu.VMEM(kv.shape, bf16),
                pltpu.VMEM((heads * bq, 2 * HEAD_DIM), bf16),
                pltpu.VMEM((heads * bq, 2 * HEAD_DIM), f32),
            ],
        ),
        cost_estimate=pl.CostEstimate(flops=heads * count * total * 256, bytes_accessed=4 << 20, transcendentals=heads * count * total // 2),
        name="attend",
    )(start, seg, q, kv, qpos.reshape(-1, 1), qseg.reshape(-1, 1), kpos.reshape(-1, 1, bk), kseg.reshape(-1, 1, bk))


def split3(x):
    a = x.astype(bf16).astype(f32)
    b = (x - a).astype(bf16).astype(f32)
    return a, b, x - a - b


def bwd_kernel(heads, bq, bk, start_ref, seg_ref, q_ref, kv_ref, o_ref, do_ref, l_ref, qpos_ref, qseg_ref, kpos_ref, kseg_ref,
               dq_ref, dkv_ref, kaug, vaug, qst, dst, qs, ds, dacc, dkv):
    qi = pl.program_id(0)
    nk = kv_ref.shape[0] // bk
    D = HEAD_DIM

    @pl.when(qi == 0)
    def _():
        lane = lax.broadcasted_iota(jnp.int32, kv_ref.shape, 1)
        kv = kv_ref[...].astype(f32)
        kaug[...] = jnp.where(lane < D, kv, jnp.where(lane < D + 3, -1.0, 0.0)).astype(bf16)
        vaug[...] = jnp.where(lane >= D, kv, jnp.where(lane < 3, -1.0, 0.0)).astype(bf16)
        dkv[...] = jnp.zeros_like(dkv)

    row = lax.broadcasted_iota(jnp.int32, (D, bq), 0)

    def extra(x):
        a, b, c = split3(x)
        return jnp.where(row == 0, a, jnp.where(row == 1, b, jnp.where(row == 2, c, 0.0)))

    zeros = jnp.zeros((D, bq), f32)
    do_all = do_ref[...].astype(f32).T
    for h in range(heads):
        part = slice(h * D, (h + 1) * D)
        wide = slice(h * 2 * D, (h + 1) * 2 * D)
        q, do, o = q_ref[part, :].astype(f32), do_all[part, :], o_ref[part, :].astype(f32)
        delta = jnp.sum(do * o, axis=0, keepdims=True)
        qst[wide, :] = jnp.concatenate([q, extra(l_ref[h : h + 1, :])], axis=0).astype(bf16)
        dst[wide, :] = jnp.concatenate([extra(delta), do], axis=0).astype(bf16)
        qs[h * bq : (h + 1) * bq, :] = jnp.concatenate([q, zeros], axis=0).T.astype(bf16)
        ds[h * bq : (h + 1) * bq, :] = jnp.concatenate([zeros, do], axis=0).T.astype(bf16)
    dacc[...] = jnp.zeros_like(dacc)

    def step(k_index, masked):
        rows = pl.ds(pl.multiple_of(k_index * bk, bk), bk)
        kb, vb, kvb = kaug[rows, :], vaug[rows, :], kv_ref[rows, :]
        if masked:
            kseg = kseg_ref[rows, :]
            mask = (kpos_ref[rows, :] <= qpos_ref[...]) & ((kseg == 0) | (kseg == qseg_ref[...]))
        add = None
        for h in range(heads):
            wide = slice(h * 2 * D, (h + 1) * 2 * D)
            tall = slice(h * bq, (h + 1) * bq)
            p = jnp.exp2(dot_nn(kb, qst[wide, :]))
            if masked:
                p = jnp.where(mask, p, 0.0)
            sg = (p * dot_nn(vb, dst[wide, :])).astype(bf16)
            part = dot_nn(sg, qs[tall, :]) + dot_nn(p.astype(bf16), ds[tall, :])
            add = part if add is None else add + part
            dacc[tall, :] += dot_tn(sg, kvb)
        dkv[rows, :] += add

    @pl.loop(0, nk)
    def _(k_index):
        needed, whole = block_state(seg_ref, start_ref, qi, k_index, bq, bk)

        @pl.when(needed & whole)
        def _():
            step(k_index, False)

        @pl.when(needed & jnp.logical_not(whole))
        def _():
            step(k_index, True)

    for h in range(heads):
        dq_ref[h * D : (h + 1) * D, :] = dacc[h * bq : (h + 1) * bq, :].T[:D, :] * D**-0.5

    @pl.when(qi == pl.num_programs(0) - 1)
    def _():
        lane = lax.broadcasted_iota(jnp.int32, dkv.shape, 1)
        dkv_ref[...] = (dkv[...] * jnp.where(lane < D, LN2, 1.0)).astype(bf16)


def attention_grad(start, seg, q, kv, o, do, l, qpos, qseg, kpos, kseg, bq, bk):
    heads = q.shape[0] // HEAD_DIM
    count, total = q.shape[1], kv.shape[0]
    bq, bk = min(bq, count), min(bk, total)
    whole = lambda *shape: pl.BlockSpec(shape, lambda i, *_: (0,) * len(shape))
    wide = pl.BlockSpec((q.shape[0], bq), lambda i, *_: (0, i))
    return pl.pallas_call(
        functools.partial(bwd_kernel, heads, bq, bk),
        out_shape=(
            jax.ShapeDtypeStruct(q.shape, f32),
            jax.ShapeDtypeStruct(kv.shape, bf16),
        ),
        grid_spec=pltpu.PrefetchScalarGridSpec(
            num_scalar_prefetch=2,
            grid=(count // bq,),
            in_specs=[
                wide,
                whole(*kv.shape),
                wide,
                pl.BlockSpec((bq, q.shape[0]), lambda i, *_: (i, 0)),
                pl.BlockSpec((heads, bq), lambda i, *_: (0, i)),
                pl.BlockSpec((1, bq), lambda i, *_: (0, i)),
                pl.BlockSpec((1, bq), lambda i, *_: (0, i)),
                whole(total, 1),
                whole(total, 1),
            ],
            out_specs=(wide, whole(*kv.shape)),
            scratch_shapes=[
                pltpu.VMEM(kv.shape, bf16),
                pltpu.VMEM(kv.shape, bf16),
                pltpu.VMEM((heads * 2 * HEAD_DIM, bq), bf16),
                pltpu.VMEM((heads * 2 * HEAD_DIM, bq), bf16),
                pltpu.VMEM((heads * bq, 2 * HEAD_DIM), bf16),
                pltpu.VMEM((heads * bq, 2 * HEAD_DIM), bf16),
                pltpu.VMEM((heads * bq, 2 * HEAD_DIM), f32),
                pltpu.VMEM(kv.shape, f32),
            ],
        ),
        cost_estimate=pl.CostEstimate(flops=heads * count * total * 640, bytes_accessed=8 << 20, transcendentals=heads * count * total // 2),
        name="attend_grad",
    )(start, seg, q, kv, o, do, l, qpos.reshape(1, -1), qseg.reshape(1, -1), kpos.reshape(-1, 1), kseg.reshape(-1, 1))


HEADS = 16
KV_HEADS = 4
rope_base = 10000.0
SHARE = ("dp", "context")
EVERY = ("dp", "context", "tensor")
QUERY_BLOCK = 512
KEY_BLOCK = 512
CHUNKS = 2


def unit_rows(values):
    r = lax.rsqrt(jnp.mean(values * values, axis=-1, keepdims=True) + epsilon)
    return values * r, r


def norm_back(grad, values, gains):
    n, r = unit_rows(values)
    scaled = grad * gains
    return r * (scaled - n * jnp.mean(scaled * n, axis=-1, keepdims=True)), jnp.sum(grad * n, axis=0)


def mixed_silu(gate_in, up_in):
    return jax.nn.silu(gate_in) * up_in


def gathered(part, axes, axis):
    return lax.all_gather(part, axes, axis=axis, tiled=True)


def scattered(part, axes, axis):
    return lax.psum_scatter(part.astype(bf16), axes, scatter_dimension=axis, tiled=True)


def natural(values):
    return with_layout_constraint(values, Layout(major_to_minor=tuple(range(values.ndim))))


def after(value, *others):
    return lax.optimization_barrier((value,) + others)[0]


def both_halves(part):
    if lax.axis_size("context") != 2:
        return gathered(part, "context", 0)
    other = lax.ppermute(part, "context", [(0, 1), (1, 0)])
    low = lax.axis_index("context") == 0
    return jnp.concatenate([jnp.where(low, part, other), jnp.where(low, other, part)], axis=0)


def halving_scatter(terms, axes):
    sizes = [lax.axis_size(axis) for axis in axes]
    blocks = terms.reshape(tuple(sizes) + (-1,) + terms.shape[1:])
    for place, axis in enumerate(axes):
        size, me = sizes[place], lax.axis_index(axis)
        stride = 1
        while stride < size:
            shape = blocks.shape
            split = blocks.reshape(shape[:place] + (shape[place] // 2, 2) + shape[place + 1 :])
            bit = (me // stride) % 2
            kept, sent = (
                lax.dynamic_index_in_dim(split, index, place + 1, keepdims=False) for index in (bit, 1 - bit)
            )
            got = lax.ppermute(sent, axis, [(i, i ^ stride) for i in range(size)])
            blocks = (kept.astype(f32) + got.astype(f32)).astype(bf16)
            stride *= 2
    return blocks.reshape((-1,) + terms.shape[1:])


def spread(part):
    ways, me = lax.axis_size("tensor"), lax.axis_index("tensor")
    out = lax.dynamic_update_index_in_dim(jnp.zeros((ways,) + part.shape, part.dtype), part, me, 0)
    for step in range(1, ways):
        got = lax.ppermute(part, "tensor", [(i, (i + step) % ways) for i in range(ways)])
        out = lax.dynamic_update_index_in_dim(out, got, (me - step) % ways, 0)
    return out


def line_total(part):
    total = part
    ways = lax.axis_size("tensor")
    for step in range(1, ways):
        total = total + lax.ppermute(part, "tensor", [(i, (i + step) % ways) for i in range(ways)])
    return total


def swap(blocks):
    ways, me = lax.axis_size("tensor"), lax.axis_index("tensor")
    out = blocks
    for step in range(1, ways):
        sent = lax.dynamic_index_in_dim(blocks, (me + step) % ways, 0, keepdims=False)
        got = lax.ppermute(sent, "tensor", [(i, (i + step) % ways) for i in range(ways)])
        out = lax.dynamic_update_index_in_dim(out, got, (me - step) % ways, 0)
    return out


def gather_kernel(count, *refs):
    sources, targets = refs[:count], refs[count : 2 * count]
    own_sem, send_sem, recv_sem = refs[2 * count :]
    dp, context = lax.axis_index("dp"), lax.axis_index("context")
    outer, inner = dp // 2, dp % 2
    across, along, beside = (
        {"dp": dp + 2 - 4 * outer},
        {"context": 1 - context},
        {"dp": dp + 1 - 2 * inner},
    )
    barrier = pltpu.get_barrier_semaphore()
    for device in (across, along, beside):
        pl.semaphore_signal(barrier, inc=1, device_id=device, device_id_type=pl.DeviceIdType.MESH)
    pl.semaphore_wait(barrier, 3)

    def place(array, o, k, first=0, parts=1):
        rows = sources[array].shape[0]
        start = ((2 * o + inner) * 2 + k) * rows + first * (rows // parts)
        return targets[array].at[pl.ds(pl.multiple_of(start, rows // parts), rows // parts), :]

    def send(array, kind, source, target, device):
        copy = pltpu.make_async_remote_copy(
            src_ref=source,
            dst_ref=target,
            send_sem=send_sem.at[array, kind],
            recv_sem=recv_sem.at[array, kind],
            device_id=device,
            device_id_type=pl.DeviceIdType.MESH,
        )
        copy.start()
        return copy

    copies, kept = {}, []
    for a in range(count):
        mine = place(a, outer, context)
        copies[a, 0] = send(a, 0, sources[a], mine, across)
        copies[a, 1] = send(a, 1, sources[a], mine, along)
        copies[a, 2] = send(a, 2, sources[a], mine, beside)
        keep = pltpu.make_async_copy(sources[a], mine, own_sem.at[a])
        keep.start()
        kept.append(keep)
    for a in range(count):
        copies[a, 0].wait_recv()
        got = place(a, 1 - outer, context)
        half = place(a, 1 - outer, context, 0, 2)
        copies[a, 3] = send(a, 3, half, half, along)
        copies[a, 4] = send(a, 4, got, got, beside)
        copies[a, 1].wait_recv()
        got = place(a, outer, 1 - context)
        half = place(a, outer, 1 - context, 1, 2)
        copies[a, 5] = send(a, 5, half, half, across)
        copies[a, 6] = send(a, 6, got, got, beside)
    for a in range(count):
        for kind, first in ((3, 0), (5, 1)):
            copies[a, kind].wait_recv()
            half = place(a, 1 - outer, 1 - context, first, 2)
            copies[a, 7 + first] = send(a, 7 + first, half, half, beside)
    for a in range(count):
        kept[a].wait()
        for kind in (2, 4, 6, 7, 8):
            copies[a, kind].wait_recv()
    for copy in copies.values():
        copy.wait_send()


def plane_gather(parts, collective):
    share = lax.axis_size("dp") * lax.axis_size("context")
    if (lax.axis_size("dp"), lax.axis_size("context")) != (4, 2):
        return [gathered(part, SHARE, 0) for part in parts]
    count = len(parts)
    return pl.pallas_call(
        functools.partial(gather_kernel, count),
        out_shape=tuple(jax.ShapeDtypeStruct((share * part.shape[0],) + part.shape[1:], part.dtype) for part in parts),
        in_specs=[pl.BlockSpec(memory_space=pltpu.VMEM)] * count,
        out_specs=(pl.BlockSpec(memory_space=pl.ANY),) * count,
        scratch_shapes=[
            pltpu.SemaphoreType.DMA((count,)),
            pltpu.SemaphoreType.DMA((count, 9)),
            pltpu.SemaphoreType.DMA((count, 9)),
        ],
        compiler_params=pltpu.CompilerParams(collective_id=collective, has_side_effects=True),
        name="plane_gather",
    )(*parts)


def rope_tables(positions):
    half = HEAD_DIM // 2
    inverse = jnp.exp(-math.log(rope_base) * jnp.arange(half, dtype=f32) * 2.0 / HEAD_DIM)
    angles = inverse[:, None] * positions.astype(f32)[None, :]
    return jnp.cos(angles), jnp.sin(angles)


def body(
    layer_input, cotangent, w_qkv, w_out, attn_gain, qk_gain, w_gate, w_up, w_down, ffn_gain, seg_ids, pos_ids
):
    _, rows, width = layer_input.shape
    ways = lax.axis_size("tensor")
    heads = HEADS // ways
    mine = lax.axis_index("tensor")
    group_seg, group_pos = seg_ids[0], pos_ids[0]
    first_row = lax.axis_index("context") * rows
    my_seg = lax.dynamic_slice_in_dim(group_seg, first_row, rows, 0)
    my_pos = lax.dynamic_slice_in_dim(group_pos, first_row, rows, 0)
    start = jnp.reshape(first_row, (1,)).astype(jnp.int32)
    columns = w_qkv.shape[1]
    qkv_shard = w_qkv.T
    packed = jnp.concatenate(
        [qkv_shard, attn_gain[None], ffn_gain[None], jnp.zeros((14, w_qkv.shape[0]), bf16)], axis=0
    )
    packed_all, gate_all, up_all = plane_gather([packed.T, w_gate, w_up], 0)
    packed_all = packed_all.T
    qkv_mine = packed_all[:columns]
    attn_gain_all = packed_all[columns].astype(f32)
    ffn_gain_all = packed_all[columns + 1].astype(f32)
    out_t = jnp.concatenate(list(spread(w_out.T)), axis=1)
    qkv_t = jnp.concatenate(list(spread(after(w_qkv, gate_all))), axis=1)
    down_all = gathered(after(w_down.T, gate_all), SHARE, 0)
    out_all = gathered(after(out_t, gate_all), SHARE, 0)

    tokens_in = layer_input.reshape(rows, width)
    cot = cotangent.reshape(rows, width)
    normed_low = (unit_rows(tokens_in.astype(f32))[0] * attn_gain_all).astype(bf16)
    joint = dot_nt(qkv_mine, normed_low)
    cos, sin = rope_tables(my_pos)
    gains = qk_gain.T
    queries, kv_mine = prep(joint, cos, sin, gains, heads, 512)
    kv = both_halves(kv_mine)
    chunk_rows = rows // CHUNKS
    part_rows = chunk_rows // ways
    chunks = [slice(c * chunk_rows, (c + 1) * chunk_rows) for c in range(CHUNKS)]

    def own_rows(values, c):
        return lax.dynamic_slice_in_dim(values, c * chunk_rows + mine * part_rows, part_rows, 0)

    keys = (group_pos, group_seg)
    attended, log_total, attended_all = [], [], []
    for c in range(CHUNKS):
        arrived = (down_all,) if c == 0 else (out_all,)
        result, total = attention(
            start + c * chunk_rows, group_seg, after(queries, *arrived), kv, my_pos, my_seg, *keys, QUERY_BLOCK, KEY_BLOCK, c, CHUNKS
        )
        attended.append(result)
        log_total.append(total)
        attended_all.append(gathered(result, "tensor", 0))

    resid_parts, normed_ffns, acts, gate_grads, up_grads, ffn_in_grads = [], [], [], [], [], []
    previous = attended[-1]
    for c, chunk in enumerate(chunks):
        act_grad = dot_nn(after(cot[chunk], previous), down_all)
        resid = tokens_in[chunk].astype(f32) + natural(dot_tt(after(attended_all[c], act_grad), out_all))
        normed_ffn = (unit_rows(resid)[0] * ffn_gain_all).astype(bf16)
        gate, up = dot_nn(normed_ffn, gate_all), dot_nn(normed_ffn, up_all)
        act, silu_pull = jax.vjp(mixed_silu, gate, up)
        gate_grad, up_grad = (g.astype(bf16) for g in silu_pull(act_grad))
        previous = (dot_nt(gate_grad, gate_all) + dot_nt(up_grad, up_all)).astype(bf16)
        ffn_in_grads.append(scattered(previous, "tensor", 0).astype(f32))
        resid_parts.append(own_rows(resid, 0))
        normed_ffns.append(normed_ffn)
        acts.append(act.astype(bf16))
        gate_grads.append(gate_grad)
        up_grads.append(up_grad)
    normed_ffn, act, gate_grad, up_grad = (
        jnp.concatenate(pieces, axis=0) for pieces in (normed_ffns, acts, gate_grads, up_grads)
    )
    act, gate_grad, up_grad, _ = lax.optimization_barrier((act, gate_grad, up_grad, previous))
    ffn_part = dot_nt(act, down_all).astype(bf16)
    grad_down = dot_tn(cot, act).astype(bf16)
    grad_gate = dot_tn(normed_ffn, gate_grad).astype(bf16)
    grad_up = dot_tn(normed_ffn, up_grad).astype(bf16)
    (qkv_all,) = plane_gather([after(qkv_t, ffn_part, grad_down, grad_gate, grad_up)], 1)
    ffn_gain_part, resid_grads, attended_grads, attended_parts, branches = 0.0, [], [], [], []
    for c in range(CHUNKS):
        norm_grad, gain_part = norm_back(ffn_in_grads[c], resid_parts[c], ffn_gain_all)
        ffn_gain_part += gain_part
        resid_grad = own_rows(cot, c).astype(f32) + norm_grad
        branch = resid_grad.astype(bf16)
        resid_grads.append(resid_grad)
        branches.append(branch)
        attended_grad = dot_nn(branch, out_all).astype(bf16)
        attended_grad = swap(jnp.stack(jnp.split(attended_grad, ways, axis=1)))
        attended_grads.append(attended_grad.reshape(chunk_rows, -1))
        attended_parts.append(lax.dynamic_slice_in_dim(attended_all[c], mine * part_rows, part_rows, 1))

    attended_grad = jnp.concatenate(attended_grads, axis=0)
    attended_grad = after(attended_grad, qkv_all)
    branch, attended_part = jnp.concatenate(branches, axis=0), jnp.concatenate(attended_parts, axis=1)
    grad_out = lax.dot_general(branch, attended_part, (((0,), (1,)), ((), ())), preferred_element_type=f32)
    grad_out = halving_scatter(grad_out.astype(bf16), SHARE)
    grad_out = swap(jnp.stack([part.T for part in jnp.split(grad_out, ways, axis=1)]))
    query_grad, kv_grad_group = attention_grad(
        start, group_seg, queries, kv, jnp.concatenate(attended, axis=1), attended_grad, jnp.concatenate(log_total, axis=1),
        my_pos, my_seg, *keys, QUERY_BLOCK, KEY_BLOCK
    )
    kv_grad = halving_scatter(kv_grad_group, ("context",))
    ffn_part = after(ffn_part, attended_grad)
    ffn_sums = [scattered(ffn_part[chunk], "tensor", 0).astype(f32) for chunk in chunks]
    joint_grad, qk_part = unprep(joint, cos, sin, gains, query_grad, kv_grad, heads, 512)
    tokens = joint_grad.reshape(columns, CHUNKS, ways, part_rows)
    joint_grad_part = swap(jnp.stack([tokens[:, :, i].reshape(columns, -1) for i in range(ways)]))
    in_grad = natural(dot_tt(joint_grad_part.reshape(ways * columns, -1), qkv_all))
    grad_qkv = dot_nn(joint_grad, normed_low)
    attn_gain_part = jnp.sum(qkv_mine.astype(f32) * grad_qkv, axis=0) / attn_gain_all
    own_inputs = jnp.concatenate([own_rows(tokens_in, c) for c in range(CHUNKS)], axis=0).astype(f32)
    norm_grad = norm_back(in_grad, own_inputs, attn_gain_all)[0]
    grad_input = (jnp.concatenate(resid_grads, axis=0) + norm_grad).astype(bf16)
    layer_output = [
        (after(part, query_grad) + ffn_sum).astype(bf16) for part, ffn_sum in zip(resid_parts, ffn_sums, strict=True)
    ]

    def all_rows(parts):
        return gathered(jnp.stack(parts), "tensor", 1).reshape(layer_input.shape)

    layer_output = all_rows([after(part, grad_input) for part in layer_output])
    grad_input = all_rows(jnp.split(grad_input, CHUNKS, axis=0))

    qk_rows = jnp.tile(qk_part.T, (1, width // HEAD_DIM))
    grad_qkv = jnp.concatenate(
        [grad_qkv, attn_gain_part[None], ffn_gain_part[None], qk_rows, jnp.zeros((12, width), f32)], axis=0
    )
    grad_qkv = halving_scatter(grad_qkv.astype(bf16).T, SHARE).astype(f32)
    small = line_total(grad_qkv[:, columns:].T)
    return (
        layer_output,
        grad_input,
        grad_qkv[:, :columns],
        jnp.sum(grad_out.astype(f32), axis=0),
        small[0],
        small[2:4, :HEAD_DIM],
        halving_scatter(grad_gate, SHARE).astype(f32),
        halving_scatter(grad_up, SHARE).astype(f32),
        halving_scatter(grad_down, SHARE).astype(f32).T,
        small[1],
    )


def solution(mesh):
    tokens, by_row, by_column = P("dp", "context", None), P(SHARE, "tensor"), P("tensor", SHARE)
    gain = P(SHARE)
    return jax.shard_map(
        body,
        mesh=mesh,
        in_specs=(
            tokens, tokens, by_row, by_column, gain, P(), by_row, by_row, by_column, gain, P("dp", None), P("dp", None)
        ),
        out_specs=(tokens, tokens, by_row, by_column, gain, P(), by_row, by_row, by_column, gain),
        check_vma=False,
    )
```

```python
import functools, math
import jax, jax.numpy as jnp
from jax import lax
from jax.experimental import pallas as pl
from jax.experimental.pallas import tpu as pltpu
from jax.experimental.layout import Layout, with_layout_constraint
from jax.sharding import PartitionSpec as P

HEAD_DIM = 64
LOG2E = math.log2(math.e)
LN2 = math.log(2.0)
f32 = jnp.float32
bf16 = jnp.bfloat16
epsilon = 1e-6


def dot_nt(a, b):
    return lax.dot_general(a, b, (((1,), (1,)), ((), ())), preferred_element_type=f32)

def dot_nn(a, b):
    return lax.dot_general(a, b, (((1,), (0,)), ((), ())), preferred_element_type=f32)

def dot_tn(a, b):
    return lax.dot_general(a, b, (((0,), (0,)), ((), ())), preferred_element_type=f32)


def dot_tt(a, b):
    return lax.dot_general(a, b, (((0,), (1,)), ((), ())), preferred_element_type=f32)


def head_norm(x):
    return x * lax.rsqrt(jnp.mean(x * x, axis=0, keepdims=True) + epsilon)


def prep_kernel(heads, joint_ref, cos_ref, sin_ref, gain_ref, q_ref, kv_ref):
    half = HEAD_DIM // 2
    cos, sin = cos_ref[...], sin_ref[...]

    def one(row, gain, scale):
        x = head_norm(joint_ref[row : row + HEAD_DIM, :]) * gain
        lo, hi = x[:half], x[half:]
        return jnp.concatenate([lo * cos - hi * sin, hi * cos + lo * sin], axis=0) * scale

    for h in range(heads):
        row = h * HEAD_DIM
        q_ref[row : row + HEAD_DIM, :] = one(row, gain_ref[:, 0:1], LOG2E * HEAD_DIM**-0.5).astype(bf16)
    row = heads * HEAD_DIM
    key = one(row, gain_ref[:, 1:2], 1.0)
    both = jnp.concatenate([key, joint_ref[row + HEAD_DIM : row + 2 * HEAD_DIM, :]], axis=0)
    kv_ref[...] = both.T.astype(bf16)


def prep(joint, cos, sin, gains, heads, block):
    rows, count = joint.shape
    block = min(block, count)
    return pl.pallas_call(
        functools.partial(prep_kernel, heads),
        out_shape=(
            jax.ShapeDtypeStruct((heads * HEAD_DIM, count), bf16),
            jax.ShapeDtypeStruct((count, 2 * HEAD_DIM), bf16),
        ),
        grid=(count // block,),
        in_specs=[
            pl.BlockSpec((rows, block), lambda i: (0, i)),
            pl.BlockSpec((HEAD_DIM // 2, block), lambda i: (0, i)),
            pl.BlockSpec((HEAD_DIM // 2, block), lambda i: (0, i)),
            pl.BlockSpec((HEAD_DIM, 2), lambda i: (0, 0)),
        ],
        out_specs=(
            pl.BlockSpec((heads * HEAD_DIM, block), lambda i: (0, i)),
            pl.BlockSpec((block, 2 * HEAD_DIM), lambda i: (i, 0)),
        ),
        cost_estimate=pl.CostEstimate(flops=rows * count * 20, bytes_accessed=rows * count * 6, transcendentals=0),
        name="prep",
    )(joint, cos, sin, gains)


def unprep_kernel(heads, joint_ref, cos_ref, sin_ref, gain_ref, dq_ref, dkv_ref, out_ref, dgain_ref):
    half = HEAD_DIM // 2
    cos, sin = cos_ref[...], sin_ref[...]

    @pl.when(pl.program_id(0) == 0)
    def _():
        dgain_ref[...] = jnp.zeros_like(dgain_ref)

    def one(row, grad, gain):
        x = joint_ref[row : row + HEAD_DIM, :]
        r = lax.rsqrt(jnp.mean(x * x, axis=0, keepdims=True) + epsilon)
        n = x * r
        lo, hi = grad[:half], grad[half:]
        back = jnp.concatenate([lo * cos + hi * sin, hi * cos - lo * sin], axis=0)
        scaled = back * gain
        result = r * (scaled - n * jnp.mean(scaled * n, axis=0, keepdims=True))
        out_ref[row : row + HEAD_DIM, :] = result.astype(bf16)
        return jnp.sum(back * n, axis=1, keepdims=True)

    total = None
    for h in range(heads):
        row = h * HEAD_DIM
        part = one(row, dq_ref[row : row + HEAD_DIM, :], gain_ref[:, 0:1])
        total = part if total is None else total + part
    row = heads * HEAD_DIM
    dkv = dkv_ref[...].astype(f32).T
    part = one(row, dkv[:HEAD_DIM], gain_ref[:, 1:2])
    out_ref[row + HEAD_DIM : row + 2 * HEAD_DIM, :] = dkv[HEAD_DIM:].astype(bf16)
    dgain_ref[...] += jnp.concatenate([total, part], axis=1)


def unprep(joint, cos, sin, gains, dq, dkv, heads, block):
    rows, count = joint.shape
    block = min(block, count)
    return pl.pallas_call(
        functools.partial(unprep_kernel, heads),
        out_shape=(
            jax.ShapeDtypeStruct((rows, count), bf16),
            jax.ShapeDtypeStruct((HEAD_DIM, 2), f32),
        ),
        grid=(count // block,),
        in_specs=[
            pl.BlockSpec((rows, block), lambda i: (0, i)),
            pl.BlockSpec((HEAD_DIM // 2, block), lambda i: (0, i)),
            pl.BlockSpec((HEAD_DIM // 2, block), lambda i: (0, i)),
            pl.BlockSpec((HEAD_DIM, 2), lambda i: (0, 0)),
            pl.BlockSpec((heads * HEAD_DIM, block), lambda i: (0, i)),
            pl.BlockSpec((block, 2 * HEAD_DIM), lambda i: (i, 0)),
        ],
        out_specs=(
            pl.BlockSpec((rows, block), lambda i: (0, i)),
            pl.BlockSpec((HEAD_DIM, 2), lambda i: (0, 0)),
        ),
        cost_estimate=pl.CostEstimate(flops=rows * count * 30, bytes_accessed=rows * count * 10, transcendentals=0),
        name="unprep",
    )(joint, cos, sin, gains, dq, dkv)


def block_state(seg_ref, start_ref, q_index, k_index, bq, bk):
    q_first = start_ref[0] + q_index * bq
    k_first = k_index * bk
    k_last_seg = seg_ref[k_first + bk - 1]
    needed = (k_first <= q_first + bq - 1) & ((k_last_seg == 0) | (k_last_seg >= seg_ref[q_first]) | (seg_ref[k_first] == 0))
    whole = (k_last_seg == 0) & (k_first + bk - 1 <= q_first)
    return needed, whole


def fwd_kernel(heads, bq, bk, start_ref, seg_ref, q_ref, kv_ref, qpos_ref, qseg_ref, kpos_ref, kseg_ref, o_ref, l_ref, vaug, qs, acc):
    qi = pl.program_id(0)
    nk = kv_ref.shape[0] // bk
    lane = lax.broadcasted_iota(jnp.int32, kv_ref.shape, 1)

    @pl.when(qi == 0)
    def _():
        vaug[...] = jnp.where(lane >= HEAD_DIM, kv_ref[...].astype(f32), jnp.where(lane == 0, 1.0, 0.0)).astype(bf16)

    zeros = jnp.zeros((HEAD_DIM, bq), f32)
    for h in range(heads):
        full = jnp.concatenate([q_ref[h * HEAD_DIM : (h + 1) * HEAD_DIM, :].astype(f32), zeros], axis=0)
        qs[h * bq : (h + 1) * bq, :] = full.T.astype(bf16)
    acc[...] = jnp.zeros_like(acc)

    def step(k_index, masked):
        rows = pl.ds(pl.multiple_of(k_index * bk, bk), bk)
        kb, vb = kv_ref[rows, :], vaug[rows, :]
        if masked:
            kseg = kseg_ref[k_index]
            mask = (kpos_ref[k_index] <= qpos_ref[...]) & ((kseg == 0) | (kseg == qseg_ref[...]))
        for h in range(heads):
            s = dot_nt(qs[h * bq : (h + 1) * bq, :], kb)
            p = jnp.exp2(s)
            if masked:
                p = jnp.where(mask, p, 0.0)
            acc[h * bq : (h + 1) * bq, :] += dot_nn(p.astype(bf16), vb)

    @pl.loop(0, nk)
    def _(k_index):
        needed, whole = block_state(seg_ref, start_ref, qi, k_index, bq, bk)

        @pl.when(needed & whole)
        def _():
            step(k_index, False)

        @pl.when(needed & jnp.logical_not(whole))
        def _():
            step(k_index, True)

    for h in range(heads):
        out = acc[h * bq : (h + 1) * bq, :].T
        total = out[0:1, :]
        o_ref[h * HEAD_DIM : (h + 1) * HEAD_DIM, :] = (out[HEAD_DIM:, :] / total).astype(bf16)
        l_ref[h : h + 1, :] = jnp.log2(total)


def attention(start, seg, q, kv, qpos, qseg, kpos, kseg, bq, bk, part, parts):
    heads = q.shape[0] // HEAD_DIM
    count, total = q.shape[1] // parts, kv.shape[0]
    bq, bk = min(bq, count), min(bk, total)
    first = part * (count // bq)
    whole = lambda *shape: pl.BlockSpec(shape, lambda i, *_: (0,) * len(shape))
    return pl.pallas_call(
        functools.partial(fwd_kernel, heads, bq, bk),
        out_shape=(
            jax.ShapeDtypeStruct((q.shape[0], count), bf16),
            jax.ShapeDtypeStruct((heads, count), f32),
        ),
        grid_spec=pltpu.PrefetchScalarGridSpec(
            num_scalar_prefetch=2,
            grid=(count // bq,),
            in_specs=[
                pl.BlockSpec((q.shape[0], bq), lambda i, *_: (0, i + first)),
                whole(*kv.shape),
                pl.BlockSpec((bq, 1), lambda i, *_: (i + first, 0)),
                pl.BlockSpec((bq, 1), lambda i, *_: (i + first, 0)),
                whole(total // bk, 1, bk),
                whole(total // bk, 1, bk),
            ],
            out_specs=(
                pl.BlockSpec((q.shape[0], bq), lambda i, *_: (0, i)),
                pl.BlockSpec((heads, bq), lambda i, *_: (0, i)),
            ),
            scratch_shapes=[
                pltpu.VMEM(kv.shape, bf16),
                pltpu.VMEM((heads * bq, 2 * HEAD_DIM), bf16),
                pltpu.VMEM((heads * bq, 2 * HEAD_DIM), f32),
            ],
        ),
        cost_estimate=pl.CostEstimate(flops=heads * count * total * 256, bytes_accessed=4 << 20, transcendentals=heads * count * total // 2),
        name="attend",
    )(start, seg, q, kv, qpos.reshape(-1, 1), qseg.reshape(-1, 1), kpos.reshape(-1, 1, bk), kseg.reshape(-1, 1, bk))


def split3(x):
    a = x.astype(bf16).astype(f32)
    b = (x - a).astype(bf16).astype(f32)
    return a, b, x - a - b


def bwd_kernel(heads, bq, bk, start_ref, seg_ref, q_ref, kv_ref, o_ref, do_ref, l_ref, qpos_ref, qseg_ref, kpos_ref, kseg_ref,
               dq_ref, dkv_ref, kaug, vaug, qst, dst, qs, ds, dacc, dkv):
    qi = pl.program_id(0)
    nk = kv_ref.shape[0] // bk
    D = HEAD_DIM

    @pl.when(qi == 0)
    def _():
        lane = lax.broadcasted_iota(jnp.int32, kv_ref.shape, 1)
        kv = kv_ref[...].astype(f32)
        kaug[...] = jnp.where(lane < D, kv, jnp.where(lane < D + 3, -1.0, 0.0)).astype(bf16)
        vaug[...] = jnp.where(lane >= D, kv, jnp.where(lane < 3, -1.0, 0.0)).astype(bf16)
        dkv[...] = jnp.zeros_like(dkv)

    row = lax.broadcasted_iota(jnp.int32, (D, bq), 0)

    def extra(x):
        a, b, c = split3(x)
        return jnp.where(row == 0, a, jnp.where(row == 1, b, jnp.where(row == 2, c, 0.0)))

    zeros = jnp.zeros((D, bq), f32)
    do_all = do_ref[...].astype(f32).T
    for h in range(heads):
        part = slice(h * D, (h + 1) * D)
        wide = slice(h * 2 * D, (h + 1) * 2 * D)
        q, do, o = q_ref[part, :].astype(f32), do_all[part, :], o_ref[part, :].astype(f32)
        delta = jnp.sum(do * o, axis=0, keepdims=True)
        qst[wide, :] = jnp.concatenate([q, extra(l_ref[h : h + 1, :])], axis=0).astype(bf16)
        dst[wide, :] = jnp.concatenate([extra(delta), do], axis=0).astype(bf16)
        qs[h * bq : (h + 1) * bq, :] = jnp.concatenate([q, zeros], axis=0).T.astype(bf16)
        ds[h * bq : (h + 1) * bq, :] = jnp.concatenate([zeros, do], axis=0).T.astype(bf16)
    dacc[...] = jnp.zeros_like(dacc)

    def step(k_index, masked):
        rows = pl.ds(pl.multiple_of(k_index * bk, bk), bk)
        kb, vb, kvb = kaug[rows, :], vaug[rows, :], kv_ref[rows, :]
        if masked:
            kseg = kseg_ref[rows, :]
            mask = (kpos_ref[rows, :] <= qpos_ref[...]) & ((kseg == 0) | (kseg == qseg_ref[...]))
        add = None
        for h in range(heads):
            wide = slice(h * 2 * D, (h + 1) * 2 * D)
            tall = slice(h * bq, (h + 1) * bq)
            p = jnp.exp2(dot_nn(kb, qst[wide, :]))
            if masked:
                p = jnp.where(mask, p, 0.0)
            sg = (p * dot_nn(vb, dst[wide, :])).astype(bf16)
            part = dot_nn(sg, qs[tall, :]) + dot_nn(p.astype(bf16), ds[tall, :])
            add = part if add is None else add + part
            dacc[tall, :] += dot_tn(sg, kvb)
        dkv[rows, :] += add

    @pl.loop(0, nk)
    def _(k_index):
        needed, whole = block_state(seg_ref, start_ref, qi, k_index, bq, bk)

        @pl.when(needed & whole)
        def _():
            step(k_index, False)

        @pl.when(needed & jnp.logical_not(whole))
        def _():
            step(k_index, True)

    for h in range(heads):
        dq_ref[h * D : (h + 1) * D, :] = dacc[h * bq : (h + 1) * bq, :].T[:D, :] * D**-0.5

    @pl.when(qi == pl.num_programs(0) - 1)
    def _():
        lane = lax.broadcasted_iota(jnp.int32, dkv.shape, 1)
        dkv_ref[...] = (dkv[...] * jnp.where(lane < D, LN2, 1.0)).astype(bf16)


def attention_grad(start, seg, q, kv, o, do, l, qpos, qseg, kpos, kseg, bq, bk):
    heads = q.shape[0] // HEAD_DIM
    count, total = q.shape[1], kv.shape[0]
    bq, bk = min(bq, count), min(bk, total)
    whole = lambda *shape: pl.BlockSpec(shape, lambda i, *_: (0,) * len(shape))
    wide = pl.BlockSpec((q.shape[0], bq), lambda i, *_: (0, i))
    return pl.pallas_call(
        functools.partial(bwd_kernel, heads, bq, bk),
        out_shape=(
            jax.ShapeDtypeStruct(q.shape, f32),
            jax.ShapeDtypeStruct(kv.shape, bf16),
        ),
        grid_spec=pltpu.PrefetchScalarGridSpec(
            num_scalar_prefetch=2,
            grid=(count // bq,),
            in_specs=[
                wide,
                whole(*kv.shape),
                wide,
                pl.BlockSpec((bq, q.shape[0]), lambda i, *_: (i, 0)),
                pl.BlockSpec((heads, bq), lambda i, *_: (0, i)),
                pl.BlockSpec((1, bq), lambda i, *_: (0, i)),
                pl.BlockSpec((1, bq), lambda i, *_: (0, i)),
                whole(total, 1),
                whole(total, 1),
            ],
            out_specs=(wide, whole(*kv.shape)),
            scratch_shapes=[
                pltpu.VMEM(kv.shape, bf16),
                pltpu.VMEM(kv.shape, bf16),
                pltpu.VMEM((heads * 2 * HEAD_DIM, bq), bf16),
                pltpu.VMEM((heads * 2 * HEAD_DIM, bq), bf16),
                pltpu.VMEM((heads * bq, 2 * HEAD_DIM), bf16),
                pltpu.VMEM((heads * bq, 2 * HEAD_DIM), bf16),
                pltpu.VMEM((heads * bq, 2 * HEAD_DIM), f32),
                pltpu.VMEM(kv.shape, f32),
            ],
        ),
        cost_estimate=pl.CostEstimate(flops=heads * count * total * 640, bytes_accessed=8 << 20, transcendentals=heads * count * total // 2),
        name="attend_grad",
    )(start, seg, q, kv, o, do, l, qpos.reshape(1, -1), qseg.reshape(1, -1), kpos.reshape(-1, 1), kseg.reshape(-1, 1))


HEADS = 16
KV_HEADS = 4
rope_base = 10000.0
SHARE = ("dp", "context")
EVERY = ("dp", "context", "tensor")
QUERY_BLOCK = 512
KEY_BLOCK = 512
CHUNKS = 2


def unit_rows(values):
    r = lax.rsqrt(jnp.mean(values * values, axis=-1, keepdims=True) + epsilon)
    return values * r, r


def norm_back(grad, values, gains):
    n, r = unit_rows(values)
    scaled = grad * gains
    return r * (scaled - n * jnp.mean(scaled * n, axis=-1, keepdims=True)), jnp.sum(grad * n, axis=0)


def mixed_silu(gate_in, up_in):
    return jax.nn.silu(gate_in) * up_in


def gathered(part, axes, axis):
    return lax.all_gather(part, axes, axis=axis, tiled=True)


def scattered(part, axes, axis):
    return lax.psum_scatter(part.astype(bf16), axes, scatter_dimension=axis, tiled=True)


def natural(values):
    return with_layout_constraint(values, Layout(major_to_minor=tuple(range(values.ndim))))


def after(value, *others):
    return lax.optimization_barrier((value,) + others)[0]


def halving_scatter(terms, axes):
    sizes = [lax.axis_size(axis) for axis in axes]
    blocks = terms.reshape(tuple(sizes) + (-1,) + terms.shape[1:])
    for place, axis in enumerate(axes):
        size, me = sizes[place], lax.axis_index(axis)
        stride = 1
        while stride < size:
            shape = blocks.shape
            split = blocks.reshape(shape[:place] + (shape[place] // 2, 2) + shape[place + 1 :])
            bit = (me // stride) % 2
            kept, sent = (
                lax.dynamic_index_in_dim(split, index, place + 1, keepdims=False) for index in (bit, 1 - bit)
            )
            got = lax.ppermute(sent, axis, [(i, i ^ stride) for i in range(size)])
            blocks = (kept.astype(f32) + got.astype(f32)).astype(bf16)
            stride *= 2
    return blocks.reshape((-1,) + terms.shape[1:])


def spread(part):
    ways, me = lax.axis_size("tensor"), lax.axis_index("tensor")
    out = lax.dynamic_update_index_in_dim(jnp.zeros((ways,) + part.shape, part.dtype), part, me, 0)
    for step in range(1, ways):
        got = lax.ppermute(part, "tensor", [(i, (i + step) % ways) for i in range(ways)])
        out = lax.dynamic_update_index_in_dim(out, got, (me - step) % ways, 0)
    return out


def line_total(part):
    total = part
    ways = lax.axis_size("tensor")
    for step in range(1, ways):
        total = total + lax.ppermute(part, "tensor", [(i, (i + step) % ways) for i in range(ways)])
    return total


def swap(blocks):
    ways, me = lax.axis_size("tensor"), lax.axis_index("tensor")
    out = blocks
    for step in range(1, ways):
        sent = lax.dynamic_index_in_dim(blocks, (me + step) % ways, 0, keepdims=False)
        got = lax.ppermute(sent, "tensor", [(i, (i + step) % ways) for i in range(ways)])
        out = lax.dynamic_update_index_in_dim(out, got, (me - step) % ways, 0)
    return out


def remote(source, target, sems, index, device):
    copy = pltpu.make_async_remote_copy(
        src_ref=source,
        dst_ref=target,
        send_sem=sems[0].at[index],
        recv_sem=sems[1].at[index],
        device_id=device,
        device_id_type=pl.DeviceIdType.MESH,
    )
    copy.start()
    return copy


def greet(devices):
    barrier = pltpu.get_barrier_semaphore()
    for device in devices:
        pl.semaphore_signal(barrier, inc=1, device_id=device, device_id_type=pl.DeviceIdType.MESH)
    pl.semaphore_wait(barrier, len(devices))


def aligned(start, size):
    return pl.ds(pl.multiple_of(start, size), size)


def gather_kernel(count, lines, pairs, *refs):
    arrays = count + lines + pairs
    sources, targets = refs[:arrays], refs[arrays : 2 * arrays]
    own_sem, send_sem, recv_sem = refs[2 * arrays : 2 * arrays + 3]
    dp, context = lax.axis_index("dp"), lax.axis_index("context")
    outer, inner = dp // 2, dp % 2
    across, along, beside = (
        {"dp": dp + 2 - 4 * outer},
        {"context": 1 - context},
        {"dp": dp + 1 - 2 * inner},
    )
    me, ways = lax.axis_index("tensor"), lax.axis_size("tensor")
    peers = [{"tensor": lax.rem(me + step, ways)} for step in range(1, ways)] if lines else []
    greet(([across, along, beside] if count else [along]) + peers)

    def place(array, o, k, first=0, parts=1):
        rows = sources[array].shape[0]
        start = ((2 * o + inner) * 2 + k) * rows + first * (rows // parts)
        return targets[array].at[aligned(start, rows // parts), :]

    def send(array, kind, source, target, device):
        copy = pltpu.make_async_remote_copy(
            src_ref=source,
            dst_ref=target,
            send_sem=send_sem.at[array, kind],
            recv_sem=recv_sem.at[array, kind],
            device_id=device,
            device_id_type=pl.DeviceIdType.MESH,
        )
        copy.start()
        return copy

    copies, kept = {}, []
    passed = []
    for a in range(count + lines, arrays):
        rows = sources[a].shape[0]
        mine = targets[a].at[aligned(context * rows, rows), :]
        passed.append(send(a, 0, sources[a], mine, along))
        keep = pltpu.make_async_copy(sources[a], mine, own_sem.at[a])
        keep.start()
        kept.append(keep)
    for a in range(count):
        mine = place(a, outer, context)
        copies[a, 0] = send(a, 0, sources[a], mine, across)
        copies[a, 1] = send(a, 1, sources[a], mine, along)
        copies[a, 2] = send(a, 2, sources[a], mine, beside)
        keep = pltpu.make_async_copy(sources[a], mine, own_sem.at[a])
        keep.start()
        kept.append(keep)
    for a in range(count, count + lines):
        width = sources[a].shape[1]
        mine = targets[a].at[:, aligned(me * width, width)]
        for k, peer in enumerate(peers):
            passed.append(send(a, k, sources[a], mine, peer))
        keep = pltpu.make_async_copy(sources[a], mine, own_sem.at[a])
        keep.start()
        kept.append(keep)
    for a in range(count):
        copies[a, 0].wait_recv()
        got = place(a, 1 - outer, context)
        half = place(a, 1 - outer, context, 0, 2)
        copies[a, 3] = send(a, 3, half, half, along)
        copies[a, 4] = send(a, 4, got, got, beside)
        copies[a, 1].wait_recv()
        got = place(a, outer, 1 - context)
        half = place(a, outer, 1 - context, 1, 2)
        copies[a, 5] = send(a, 5, half, half, across)
        copies[a, 6] = send(a, 6, got, got, beside)
    for a in range(count):
        for kind, first in ((3, 0), (5, 1)):
            copies[a, kind].wait_recv()
            half = place(a, 1 - outer, 1 - context, first, 2)
            copies[a, 7 + first] = send(a, 7 + first, half, half, beside)
    for keep in kept:
        keep.wait()
    for copy in passed:
        copy.wait()
    for a in range(count):
        for kind in (2, 4, 6, 7, 8):
            copies[a, kind].wait_recv()
    for copy in copies.values():
        copy.wait_send()


def plane_gather(parts, lines, pairs, collective):
    share, ways = lax.axis_size("dp") * lax.axis_size("context"), lax.axis_size("tensor")
    if (lax.axis_size("dp"), lax.axis_size("context")) != (4, 2):
        whole = [gathered(part, SHARE, 0) for part in parts] + [jnp.concatenate(list(spread(line)), axis=1) for line in lines]
        return whole + [gathered(pair, "context", 0) for pair in pairs]
    arrays = len(parts) + len(lines) + len(pairs)
    shapes = [(share * part.shape[0], part.shape[1]) for part in parts] + [(line.shape[0], ways * line.shape[1]) for line in lines]
    shapes += [(2 * pair.shape[0], pair.shape[1]) for pair in pairs]
    return pl.pallas_call(
        functools.partial(gather_kernel, len(parts), len(lines), len(pairs)),
        out_shape=tuple(jax.ShapeDtypeStruct(shape, bf16) for shape in shapes),
        in_specs=[pl.BlockSpec(memory_space=pltpu.VMEM)] * arrays,
        out_specs=(pl.BlockSpec(memory_space=pl.ANY),) * arrays,
        scratch_shapes=[
            pltpu.SemaphoreType.DMA((arrays,)),
            pltpu.SemaphoreType.DMA((arrays, 9)),
            pltpu.SemaphoreType.DMA((arrays, 9)),
        ],
        compiler_params=pltpu.CompilerParams(collective_id=collective, has_side_effects=True),
        name="plane_gather",
    )(*parts, *lines, *pairs)


def heads_kernel(ways, chunks, grad_ref, out_ref, own_sem, send_sem, recv_sem):
    me = lax.axis_index("tensor")
    peers = [lax.rem(me + step, ways) for step in range(1, ways)]
    greet([{"tensor": peer} for peer in peers])
    size, width = grad_ref.shape[0] // chunks, grad_ref.shape[1] // ways
    copies = []
    for c in range(chunks):
        rows = pl.ds(c * size, size)
        target = out_ref.at[aligned((c * ways + me) * size, size), :]
        for k, peer in enumerate(peers):
            source = grad_ref.at[rows, aligned(peer * width, width)]
            copies.append(remote(source, target, (send_sem, recv_sem), c * (ways - 1) + k, {"tensor": peer}))
        kept = pltpu.make_async_copy(grad_ref.at[rows, aligned(me * width, width)], target, own_sem.at[c])
        kept.start()
        copies.append(kept)
    for copy in copies:
        copy.wait()


def to_heads(grad, chunks, collective):
    ways = lax.axis_size("tensor")
    count = chunks * (ways - 1)
    return pl.pallas_call(
        functools.partial(heads_kernel, ways, chunks),
        out_shape=jax.ShapeDtypeStruct((grad.shape[0] * ways, grad.shape[1] // ways), grad.dtype),
        in_specs=[pl.BlockSpec(memory_space=pltpu.VMEM)],
        out_specs=pl.BlockSpec(memory_space=pl.ANY),
        scratch_shapes=[pltpu.SemaphoreType.DMA((chunks,))] + [pltpu.SemaphoreType.DMA((count,))] * 2,
        compiler_params=pltpu.CompilerParams(collective_id=collective, has_side_effects=True),
        name="to_heads",
    )(grad)


def tail_kernel(heads, ways, chunks, joint_ref, cos_ref, sin_ref, gain_ref, dq_ref, dkv_ref,
                grad_ref, part_ref, dgain_ref, got_ref, own_sem, send_sem, recv_sem):
    D, half = HEAD_DIM, HEAD_DIM // 2
    rows, count = joint_ref.shape
    queries = heads * D
    me, context = lax.axis_index("tensor"), lax.axis_index("context")
    peers = [lax.rem(me + step, ways) for step in range(1, ways)]
    along = {"context": 1 - context}
    greet([along] + [{"tensor": peer} for peer in peers])
    sems = (send_sem, recv_sem)
    block = min(count, 512)
    size = count // chunks // ways
    copies = [remote(dkv_ref.at[aligned((1 - context) * count, count), :], got_ref, sems, 0, along)]

    def one(first, columns, grad, gain):
        x = joint_ref[first : first + D, columns]
        cos, sin = cos_ref[:, columns], sin_ref[:, columns]
        r = lax.rsqrt(jnp.mean(x * x, axis=0, keepdims=True) + epsilon)
        n = x * r
        lo, hi = grad[:half], grad[half:]
        back = jnp.concatenate([lo * cos + hi * sin, hi * cos - lo * sin], axis=0)
        scaled = back * gain
        result = r * (scaled - n * jnp.mean(scaled * n, axis=0, keepdims=True))
        grad_ref[first : first + D, columns] = result.astype(bf16)
        return jnp.sum(back * n, axis=1, keepdims=True)

    def hand_out(first, height, index):
        for c in range(chunks):
            target = part_ref.at[pl.ds(pl.multiple_of(me * rows + first, 128), height), pl.ds(c * size, size)]
            for k, peer in enumerate(peers):
                source = grad_ref.at[pl.ds(first, height), aligned((c * ways + peer) * size, size)]
                copies.append(remote(source, target, sems, 1 + (index * chunks + c) * (ways - 1) + k, {"tensor": peer}))
            kept = pltpu.make_async_copy(
                grad_ref.at[pl.ds(first, height), aligned((c * ways + me) * size, size)], target, own_sem.at[index * chunks + c]
            )
            kept.start()
            copies.append(kept)

    total = jnp.zeros((D, 1), f32)
    for b in range(count // block):
        columns = slice(b * block, (b + 1) * block)
        for h in range(heads):
            total += one(h * D, columns, dq_ref[h * D : (h + 1) * D, columns], gain_ref[:, 0:1])
    hand_out(0, queries, 0)
    copies[0].wait_recv()
    key_total = jnp.zeros((D, 1), f32)
    for b in range(count // block):
        columns = slice(b * block, (b + 1) * block)
        mine = dkv_ref[aligned(context * count + b * block, block), :].astype(f32)
        both = (mine + got_ref[columns, :].astype(f32)).T
        key_total += one(queries, columns, both[:D], gain_ref[:, 1:2])
        grad_ref[queries + D : queries + 2 * D, columns] = both[D:].astype(bf16)
    hand_out(queries, 2 * D, 1)
    dgain_ref[...] = jnp.concatenate([total, key_total], axis=1)
    copies[0].wait_send()
    for copy in copies[1:]:
        copy.wait()


def joint_tail(joint, cos, sin, gains, dq, dkv, heads, chunks, collective):
    rows, count = joint.shape
    ways = lax.axis_size("tensor")
    number = 1 + 2 * chunks * (ways - 1)
    vmem = pl.BlockSpec(memory_space=pltpu.VMEM)
    return pl.pallas_call(
        functools.partial(tail_kernel, heads, ways, chunks),
        out_shape=(
            jax.ShapeDtypeStruct((rows, count), bf16),
            jax.ShapeDtypeStruct((ways * rows, count // ways), bf16),
            jax.ShapeDtypeStruct((HEAD_DIM, 2), f32),
        ),
        in_specs=[vmem] * 6,
        out_specs=(vmem, pl.BlockSpec(memory_space=pl.ANY), vmem),
        scratch_shapes=[
            pltpu.VMEM((count, 2 * HEAD_DIM), bf16),
            pltpu.SemaphoreType.DMA((2 * chunks,)),
            pltpu.SemaphoreType.DMA((number,)),
            pltpu.SemaphoreType.DMA((number,)),
        ],
        compiler_params=pltpu.CompilerParams(collective_id=collective, has_side_effects=True),
        name="joint_tail",
    )(joint, cos, sin, gains, dq, dkv)


def rope_tables(positions):
    half = HEAD_DIM // 2
    inverse = jnp.exp(-math.log(rope_base) * jnp.arange(half, dtype=f32) * 2.0 / HEAD_DIM)
    angles = inverse[:, None] * positions.astype(f32)[None, :]
    return jnp.cos(angles), jnp.sin(angles)


def body(
    layer_input, cotangent, w_qkv, w_out, attn_gain, qk_gain, w_gate, w_up, w_down, ffn_gain, seg_ids, pos_ids
):
    _, rows, width = layer_input.shape
    ways = lax.axis_size("tensor")
    heads = HEADS // ways
    mine = lax.axis_index("tensor")
    group_seg, group_pos = seg_ids[0], pos_ids[0]
    first_row = lax.axis_index("context") * rows
    my_seg = lax.dynamic_slice_in_dim(group_seg, first_row, rows, 0)
    my_pos = lax.dynamic_slice_in_dim(group_pos, first_row, rows, 0)
    start = jnp.reshape(first_row, (1,)).astype(jnp.int32)
    columns = w_qkv.shape[1]
    qkv_shard = w_qkv.T
    packed = jnp.concatenate(
        [qkv_shard, attn_gain[None], ffn_gain[None], jnp.zeros((14, w_qkv.shape[0]), bf16)], axis=0
    )
    packed_all, gate_all, out_t, qkv_t = plane_gather([packed.T, w_gate], [w_out.T, w_qkv], [], 0)
    packed_all = packed_all.T
    up_all = gathered(after(w_up, gate_all), SHARE, 0)
    qkv_mine = packed_all[:columns]
    attn_gain_all = packed_all[columns].astype(f32)
    ffn_gain_all = packed_all[columns + 1].astype(f32)

    tokens_in = layer_input.reshape(rows, width)
    cot = cotangent.reshape(rows, width)
    normed_low = (unit_rows(tokens_in.astype(f32))[0] * attn_gain_all).astype(bf16)
    joint = dot_nt(qkv_mine, normed_low)
    cos, sin = rope_tables(my_pos)
    gains = qk_gain.T
    queries, kv_mine = prep(joint, cos, sin, gains, heads, 512)
    (kv,) = plane_gather([], [], [kv_mine], 1)
    chunk_rows = rows // CHUNKS
    part_rows = chunk_rows // ways
    chunks = [slice(c * chunk_rows, (c + 1) * chunk_rows) for c in range(CHUNKS)]

    def own_rows(values, c):
        return lax.dynamic_slice_in_dim(values, c * chunk_rows + mine * part_rows, part_rows, 0)

    keys = (group_pos, group_seg)
    attended, log_total, attended_all = [], [], []
    for c in range(CHUNKS):
        result, total = attention(
            start + c * chunk_rows, group_seg, after(queries, up_all) if c else queries, kv, my_pos, my_seg, *keys, QUERY_BLOCK, KEY_BLOCK, c, CHUNKS
        )
        attended.append(result)
        log_total.append(total)
        attended_all.append(gathered(result, "tensor", 0))

    out_all, down_all = plane_gather([after(out_t, *attended), w_down.T], [], [], 5)

    resid_parts, normed_ffns, acts, gate_grads, up_grads, ffn_in_grads = [], [], [], [], [], []
    previous = attended[-1]
    for c, chunk in enumerate(chunks):
        act_grad = dot_nn(after(cot[chunk], previous), down_all)
        resid = tokens_in[chunk].astype(f32) + natural(dot_tt(after(attended_all[c], act_grad), out_all))
        normed_ffn = (unit_rows(resid)[0] * ffn_gain_all).astype(bf16)
        gate, up = dot_nn(normed_ffn, gate_all), dot_nn(normed_ffn, up_all)
        act, silu_pull = jax.vjp(mixed_silu, gate, up)
        gate_grad, up_grad = (g.astype(bf16) for g in silu_pull(act_grad))
        previous = (dot_nt(gate_grad, gate_all) + dot_nt(up_grad, up_all)).astype(bf16)
        ffn_in_grads.append(scattered(previous, "tensor", 0).astype(f32))
        resid_parts.append(own_rows(resid, 0))
        normed_ffns.append(normed_ffn)
        acts.append(act.astype(bf16))
        gate_grads.append(gate_grad)
        up_grads.append(up_grad)
    normed_ffn, act, gate_grad, up_grad = (
        jnp.concatenate(pieces, axis=0) for pieces in (normed_ffns, acts, gate_grads, up_grads)
    )
    act, gate_grad, up_grad, _ = lax.optimization_barrier((act, gate_grad, up_grad, previous))
    ffn_part = dot_nt(act, down_all).astype(bf16)
    grad_down = dot_tn(cot, act).astype(bf16)
    (qkv_all,) = plane_gather([after(qkv_t, ffn_part, grad_down)], [], [], 4)
    ffn_gain_part, resid_grads, attended_grads, attended_parts, branches = 0.0, [], [], [], []
    for c in range(CHUNKS):
        norm_grad, gain_part = norm_back(ffn_in_grads[c], resid_parts[c], ffn_gain_all)
        ffn_gain_part += gain_part
        resid_grad = own_rows(cot, c).astype(f32) + norm_grad
        branch = resid_grad.astype(bf16)
        resid_grads.append(resid_grad)
        branches.append(branch)
        attended_grads.append(dot_nn(branch, out_all).astype(bf16))
        attended_parts.append(lax.dynamic_slice_in_dim(attended_all[c], mine * part_rows, part_rows, 1))

    attended_grad = to_heads(after(jnp.concatenate(attended_grads, axis=0), qkv_all), CHUNKS, 2)
    branch, attended_part = jnp.concatenate(branches, axis=0), jnp.concatenate(attended_parts, axis=1)
    grad_out = lax.dot_general(branch, attended_part, (((0,), (1,)), ((), ())), preferred_element_type=f32)
    grad_out = halving_scatter(grad_out.astype(bf16), SHARE)
    grad_out = swap(jnp.stack([part.T for part in jnp.split(grad_out, ways, axis=1)]))
    query_grad, kv_grad_group = attention_grad(
        start, group_seg, queries, kv, jnp.concatenate(attended, axis=1), attended_grad, jnp.concatenate(log_total, axis=1),
        my_pos, my_seg, *keys, QUERY_BLOCK, KEY_BLOCK
    )
    ffn_sums = [scattered(ffn_part[chunk], "tensor", 0).astype(f32) for chunk in chunks]
    if lax.axis_size("context") == 2:
        joint_grad, joint_grad_part, qk_part = joint_tail(
            joint, cos, sin, gains, query_grad, kv_grad_group, heads, CHUNKS, 3
        )
    else:
        kv_grad = halving_scatter(kv_grad_group, ("context",))
        joint_grad, qk_part = unprep(joint, cos, sin, gains, query_grad, kv_grad, heads, 512)
        tokens = joint_grad.reshape(columns, CHUNKS, ways, part_rows)
        joint_grad_part = swap(jnp.stack([tokens[:, :, i].reshape(columns, -1) for i in range(ways)]))
        joint_grad_part = joint_grad_part.reshape(ways * columns, -1)
    in_grad = natural(dot_tt(joint_grad_part, qkv_all))
    own_inputs = jnp.concatenate([own_rows(tokens_in, c) for c in range(CHUNKS)], axis=0).astype(f32)
    norm_grad = norm_back(in_grad, own_inputs, attn_gain_all)[0]
    grad_input = (jnp.concatenate(resid_grads, axis=0) + norm_grad).astype(bf16)
    gate_grad, up_grad, joint_late, _ = lax.optimization_barrier((gate_grad, up_grad, joint_grad, grad_input))
    grad_gate = dot_tn(normed_ffn, gate_grad).astype(bf16)
    grad_up = dot_tn(normed_ffn, up_grad).astype(bf16)
    layer_output = [
        (after(part, query_grad) + ffn_sum).astype(bf16) for part, ffn_sum in zip(resid_parts, ffn_sums, strict=True)
    ]

    def all_rows(parts):
        return gathered(jnp.stack(parts), "tensor", 1).reshape(layer_input.shape)

    layer_output = all_rows([after(part, grad_input) for part in layer_output])
    grad_input = all_rows(jnp.split(grad_input, CHUNKS, axis=0))

    grad_qkv = dot_nn(joint_late, normed_low)
    attn_gain_part = jnp.sum(qkv_mine.astype(f32) * grad_qkv, axis=0) / attn_gain_all
    qk_rows = jnp.tile(qk_part.T, (1, width // HEAD_DIM))
    grad_qkv = jnp.concatenate(
        [grad_qkv, attn_gain_part[None], ffn_gain_part[None], qk_rows, jnp.zeros((12, width), f32)], axis=0
    )
    grad_qkv = halving_scatter(grad_qkv.astype(bf16).T, SHARE).astype(f32)
    small = line_total(grad_qkv[:, columns:].T)
    return (
        layer_output,
        grad_input,
        grad_qkv[:, :columns],
        jnp.sum(grad_out.astype(f32), axis=0),
        small[0],
        small[2:4, :HEAD_DIM],
        halving_scatter(grad_gate, SHARE).astype(f32),
        halving_scatter(grad_up, SHARE).astype(f32),
        halving_scatter(grad_down, SHARE).astype(f32).T,
        small[1],
    )


def solution(mesh):
    tokens, by_row, by_column = P("dp", "context", None), P(SHARE, "tensor"), P("tensor", SHARE)
    gain = P(SHARE)
    return jax.shard_map(
        body,
        mesh=mesh,
        in_specs=(
            tokens, tokens, by_row, by_column, gain, P(), by_row, by_row, by_column, gain, P("dp", None), P("dp", None)
        ),
        out_specs=(tokens, tokens, by_row, by_column, gain, P(), by_row, by_row, by_column, gain),
        check_vma=False,
    )
```

```python
import functools, math
import jax, jax.numpy as jnp
from jax import lax
from jax.experimental import pallas as pl
from jax.experimental.pallas import tpu as pltpu
from jax.experimental.layout import Layout, with_layout_constraint
from jax.sharding import PartitionSpec as P

HEAD_DIM = 64
LOG2E = math.log2(math.e)
LN2 = math.log(2.0)
f32 = jnp.float32
bf16 = jnp.bfloat16
epsilon = 1e-6


def dot_nt(a, b):
    return lax.dot_general(a, b, (((1,), (1,)), ((), ())), preferred_element_type=f32)

def dot_nn(a, b):
    return lax.dot_general(a, b, (((1,), (0,)), ((), ())), preferred_element_type=f32)

def dot_tn(a, b):
    return lax.dot_general(a, b, (((0,), (0,)), ((), ())), preferred_element_type=f32)


def dot_tt(a, b):
    return lax.dot_general(a, b, (((0,), (1,)), ((), ())), preferred_element_type=f32)


def head_norm(x):
    return x * lax.rsqrt(jnp.mean(x * x, axis=0, keepdims=True) + epsilon)


def prep_kernel(heads, joint_ref, cos_ref, sin_ref, gain_ref, q_ref, kv_ref):
    half = HEAD_DIM // 2
    cos, sin = cos_ref[...], sin_ref[...]

    def one(row, gain, scale):
        x = head_norm(joint_ref[row : row + HEAD_DIM, :]) * gain
        lo, hi = x[:half], x[half:]
        return jnp.concatenate([lo * cos - hi * sin, hi * cos + lo * sin], axis=0) * scale

    for h in range(heads):
        row = h * HEAD_DIM
        q_ref[row : row + HEAD_DIM, :] = one(row, gain_ref[:, 0:1], LOG2E * HEAD_DIM**-0.5).astype(bf16)
    row = heads * HEAD_DIM
    key = one(row, gain_ref[:, 1:2], 1.0)
    both = jnp.concatenate([key, joint_ref[row + HEAD_DIM : row + 2 * HEAD_DIM, :]], axis=0)
    kv_ref[...] = both.T.astype(bf16)


def prep(joint, cos, sin, gains, heads, block):
    rows, count = joint.shape
    block = min(block, count)
    return pl.pallas_call(
        functools.partial(prep_kernel, heads),
        out_shape=(
            jax.ShapeDtypeStruct((heads * HEAD_DIM, count), bf16),
            jax.ShapeDtypeStruct((count, 2 * HEAD_DIM), bf16),
        ),
        grid=(count // block,),
        in_specs=[
            pl.BlockSpec((rows, block), lambda i: (0, i)),
            pl.BlockSpec((HEAD_DIM // 2, block), lambda i: (0, i)),
            pl.BlockSpec((HEAD_DIM // 2, block), lambda i: (0, i)),
            pl.BlockSpec((HEAD_DIM, 2), lambda i: (0, 0)),
        ],
        out_specs=(
            pl.BlockSpec((heads * HEAD_DIM, block), lambda i: (0, i)),
            pl.BlockSpec((block, 2 * HEAD_DIM), lambda i: (i, 0)),
        ),
        cost_estimate=pl.CostEstimate(flops=rows * count * 20, bytes_accessed=rows * count * 6, transcendentals=0),
        name="prep",
    )(joint, cos, sin, gains)


def unprep_kernel(heads, joint_ref, cos_ref, sin_ref, gain_ref, dq_ref, dkv_ref, out_ref, dgain_ref):
    half = HEAD_DIM // 2
    cos, sin = cos_ref[...], sin_ref[...]

    @pl.when(pl.program_id(0) == 0)
    def _():
        dgain_ref[...] = jnp.zeros_like(dgain_ref)

    def one(row, grad, gain):
        x = joint_ref[row : row + HEAD_DIM, :]
        r = lax.rsqrt(jnp.mean(x * x, axis=0, keepdims=True) + epsilon)
        n = x * r
        lo, hi = grad[:half], grad[half:]
        back = jnp.concatenate([lo * cos + hi * sin, hi * cos - lo * sin], axis=0)
        scaled = back * gain
        result = r * (scaled - n * jnp.mean(scaled * n, axis=0, keepdims=True))
        out_ref[row : row + HEAD_DIM, :] = result.astype(bf16)
        return jnp.sum(back * n, axis=1, keepdims=True)

    total = None
    for h in range(heads):
        row = h * HEAD_DIM
        part = one(row, dq_ref[row : row + HEAD_DIM, :], gain_ref[:, 0:1])
        total = part if total is None else total + part
    row = heads * HEAD_DIM
    dkv = dkv_ref[...].astype(f32).T
    part = one(row, dkv[:HEAD_DIM], gain_ref[:, 1:2])
    out_ref[row + HEAD_DIM : row + 2 * HEAD_DIM, :] = dkv[HEAD_DIM:].astype(bf16)
    dgain_ref[...] += jnp.concatenate([total, part], axis=1)


def unprep(joint, cos, sin, gains, dq, dkv, heads, block):
    rows, count = joint.shape
    block = min(block, count)
    return pl.pallas_call(
        functools.partial(unprep_kernel, heads),
        out_shape=(
            jax.ShapeDtypeStruct((rows, count), bf16),
            jax.ShapeDtypeStruct((HEAD_DIM, 2), f32),
        ),
        grid=(count // block,),
        in_specs=[
            pl.BlockSpec((rows, block), lambda i: (0, i)),
            pl.BlockSpec((HEAD_DIM // 2, block), lambda i: (0, i)),
            pl.BlockSpec((HEAD_DIM // 2, block), lambda i: (0, i)),
            pl.BlockSpec((HEAD_DIM, 2), lambda i: (0, 0)),
            pl.BlockSpec((heads * HEAD_DIM, block), lambda i: (0, i)),
            pl.BlockSpec((block, 2 * HEAD_DIM), lambda i: (i, 0)),
        ],
        out_specs=(
            pl.BlockSpec((rows, block), lambda i: (0, i)),
            pl.BlockSpec((HEAD_DIM, 2), lambda i: (0, 0)),
        ),
        cost_estimate=pl.CostEstimate(flops=rows * count * 30, bytes_accessed=rows * count * 10, transcendentals=0),
        name="unprep",
    )(joint, cos, sin, gains, dq, dkv)


def block_state(seg_ref, start_ref, q_index, k_index, bq, bk):
    q_first = start_ref[0] + q_index * bq
    k_first = k_index * bk
    k_last_seg = seg_ref[k_first + bk - 1]
    needed = (k_first <= q_first + bq - 1) & ((k_last_seg == 0) | (k_last_seg >= seg_ref[q_first]) | (seg_ref[k_first] == 0))
    whole = (k_last_seg == 0) & (k_first + bk - 1 <= q_first)
    return needed, whole


def fwd_kernel(heads, bq, bk, start_ref, seg_ref, q_ref, kv_ref, qpos_ref, qseg_ref, kpos_ref, kseg_ref, o_ref, l_ref, vaug, qs, acc):
    qi = pl.program_id(0)
    nk = kv_ref.shape[0] // bk
    lane = lax.broadcasted_iota(jnp.int32, kv_ref.shape, 1)

    @pl.when(qi == 0)
    def _():
        vaug[...] = jnp.where(lane >= HEAD_DIM, kv_ref[...].astype(f32), jnp.where(lane == 0, 1.0, 0.0)).astype(bf16)

    zeros = jnp.zeros((HEAD_DIM, bq), f32)
    for h in range(heads):
        full = jnp.concatenate([q_ref[h * HEAD_DIM : (h + 1) * HEAD_DIM, :].astype(f32), zeros], axis=0)
        qs[h * bq : (h + 1) * bq, :] = full.T.astype(bf16)
    acc[...] = jnp.zeros_like(acc)

    def step(k_index, masked):
        rows = pl.ds(pl.multiple_of(k_index * bk, bk), bk)
        kb, vb = kv_ref[rows, :], vaug[rows, :]
        if masked:
            kseg = kseg_ref[k_index]
            mask = (kpos_ref[k_index] <= qpos_ref[...]) & ((kseg == 0) | (kseg == qseg_ref[...]))
        for h in range(heads):
            s = dot_nt(qs[h * bq : (h + 1) * bq, :], kb)
            p = jnp.exp2(s)
            if masked:
                p = jnp.where(mask, p, 0.0)
            acc[h * bq : (h + 1) * bq, :] += dot_nn(p.astype(bf16), vb)

    @pl.loop(0, nk)
    def _(k_index):
        needed, whole = block_state(seg_ref, start_ref, qi, k_index, bq, bk)

        @pl.when(needed & whole)
        def _():
            step(k_index, False)

        @pl.when(needed & jnp.logical_not(whole))
        def _():
            step(k_index, True)

    for h in range(heads):
        out = acc[h * bq : (h + 1) * bq, :].T
        total = out[0:1, :]
        o_ref[h * HEAD_DIM : (h + 1) * HEAD_DIM, :] = (out[HEAD_DIM:, :] / total).astype(bf16)
        l_ref[h : h + 1, :] = jnp.log2(total)


def attention(start, seg, q, kv, qpos, qseg, kpos, kseg, bq, bk, part, parts):
    heads = q.shape[0] // HEAD_DIM
    count, total = q.shape[1] // parts, kv.shape[0]
    bq, bk = min(bq, count), min(bk, total)
    first = part * (count // bq)
    whole = lambda *shape: pl.BlockSpec(shape, lambda i, *_: (0,) * len(shape))
    return pl.pallas_call(
        functools.partial(fwd_kernel, heads, bq, bk),
        out_shape=(
            jax.ShapeDtypeStruct((q.shape[0], count), bf16),
            jax.ShapeDtypeStruct((heads, count), f32),
        ),
        grid_spec=pltpu.PrefetchScalarGridSpec(
            num_scalar_prefetch=2,
            grid=(count // bq,),
            in_specs=[
                pl.BlockSpec((q.shape[0], bq), lambda i, *_: (0, i + first)),
                whole(*kv.shape),
                pl.BlockSpec((bq, 1), lambda i, *_: (i + first, 0)),
                pl.BlockSpec((bq, 1), lambda i, *_: (i + first, 0)),
                whole(total // bk, 1, bk),
                whole(total // bk, 1, bk),
            ],
            out_specs=(
                pl.BlockSpec((q.shape[0], bq), lambda i, *_: (0, i)),
                pl.BlockSpec((heads, bq), lambda i, *_: (0, i)),
            ),
            scratch_shapes=[
                pltpu.VMEM(kv.shape, bf16),
                pltpu.VMEM((heads * bq, 2 * HEAD_DIM), bf16),
                pltpu.VMEM((heads * bq, 2 * HEAD_DIM), f32),
            ],
        ),
        cost_estimate=pl.CostEstimate(flops=heads * count * total * 256, bytes_accessed=4 << 20, transcendentals=heads * count * total // 2),
        name="attend",
    )(start, seg, q, kv, qpos.reshape(-1, 1), qseg.reshape(-1, 1), kpos.reshape(-1, 1, bk), kseg.reshape(-1, 1, bk))


def split3(x):
    a = x.astype(bf16).astype(f32)
    b = (x - a).astype(bf16).astype(f32)
    return a, b, x - a - b


def bwd_kernel(heads, bq, bk, final, start_ref, seg_ref, q_ref, kv_ref, o_ref, do_ref, l_ref, qpos_ref, qseg_ref, kpos_ref, kseg_ref, *rest):
    carried, (dq_ref, dkv_ref, kaug, vaug, qst, dst, qs, ds, dacc, dkv) = rest[:-10], rest[-10:]
    qi = pl.program_id(0)
    nk = kv_ref.shape[0] // bk
    D = HEAD_DIM

    @pl.when(qi == 0)
    def _():
        lane = lax.broadcasted_iota(jnp.int32, kv_ref.shape, 1)
        kv = kv_ref[...].astype(f32)
        kaug[...] = jnp.where(lane < D, kv, jnp.where(lane < D + 3, -1.0, 0.0)).astype(bf16)
        vaug[...] = jnp.where(lane >= D, kv, jnp.where(lane < 3, -1.0, 0.0)).astype(bf16)
        dkv[...] = carried[0][...] if carried else jnp.zeros_like(dkv)

    row = lax.broadcasted_iota(jnp.int32, (D, bq), 0)

    def extra(x):
        a, b, c = split3(x)
        return jnp.where(row == 0, a, jnp.where(row == 1, b, jnp.where(row == 2, c, 0.0)))

    zeros = jnp.zeros((D, bq), f32)
    do_all = do_ref[...].astype(f32).T
    for h in range(heads):
        part = slice(h * D, (h + 1) * D)
        wide = slice(h * 2 * D, (h + 1) * 2 * D)
        q, do, o = q_ref[part, :].astype(f32), do_all[part, :], o_ref[part, :].astype(f32)
        delta = jnp.sum(do * o, axis=0, keepdims=True)
        qst[wide, :] = jnp.concatenate([q, extra(l_ref[h : h + 1, :])], axis=0).astype(bf16)
        dst[wide, :] = jnp.concatenate([extra(delta), do], axis=0).astype(bf16)
        qs[h * bq : (h + 1) * bq, :] = jnp.concatenate([q, zeros], axis=0).T.astype(bf16)
        ds[h * bq : (h + 1) * bq, :] = jnp.concatenate([zeros, do], axis=0).T.astype(bf16)
    dacc[...] = jnp.zeros_like(dacc)

    def step(k_index, masked):
        rows = pl.ds(pl.multiple_of(k_index * bk, bk), bk)
        kb, vb, kvb = kaug[rows, :], vaug[rows, :], kv_ref[rows, :]
        if masked:
            kseg = kseg_ref[rows, :]
            mask = (kpos_ref[rows, :] <= qpos_ref[...]) & ((kseg == 0) | (kseg == qseg_ref[...]))
        add = None
        for h in range(heads):
            wide = slice(h * 2 * D, (h + 1) * 2 * D)
            tall = slice(h * bq, (h + 1) * bq)
            p = jnp.exp2(dot_nn(kb, qst[wide, :]))
            if masked:
                p = jnp.where(mask, p, 0.0)
            sg = (p * dot_nn(vb, dst[wide, :])).astype(bf16)
            part = dot_nn(sg, qs[tall, :]) + dot_nn(p.astype(bf16), ds[tall, :])
            add = part if add is None else add + part
            dacc[tall, :] += dot_tn(sg, kvb)
        dkv[rows, :] += add

    @pl.loop(0, nk)
    def _(k_index):
        needed, whole = block_state(seg_ref, start_ref, qi, k_index, bq, bk)

        @pl.when(needed & whole)
        def _():
            step(k_index, False)

        @pl.when(needed & jnp.logical_not(whole))
        def _():
            step(k_index, True)

    for h in range(heads):
        dq_ref[h * D : (h + 1) * D, :] = dacc[h * bq : (h + 1) * bq, :].T[:D, :] * D**-0.5

    @pl.when(qi == pl.num_programs(0) - 1)
    def _():
        lane = lax.broadcasted_iota(jnp.int32, dkv.shape, 1)
        scale = jnp.where(lane < D, LN2, 1.0) if final else 1.0
        dkv_ref[...] = (dkv[...] * scale).astype(dkv_ref.dtype)


def attention_grad(start, seg, q, kv, o, do, l, qpos, qseg, kpos, kseg, carried, bq, bk, part, parts):
    heads = q.shape[0] // HEAD_DIM
    count, total = q.shape[1] // parts, kv.shape[0]
    bq, bk = min(bq, count), min(bk, total)
    first = part * (count // bq)
    final = part == parts - 1
    whole = lambda *shape: pl.BlockSpec(shape, lambda i, *_: (0,) * len(shape))
    wide = pl.BlockSpec((q.shape[0], bq), lambda i, *_: (0, i + first))
    near = pl.BlockSpec((q.shape[0], bq), lambda i, *_: (0, i))
    return pl.pallas_call(
        functools.partial(bwd_kernel, heads, bq, bk, final),
        out_shape=(
            jax.ShapeDtypeStruct((q.shape[0], count), f32),
            jax.ShapeDtypeStruct(kv.shape, bf16 if final else f32),
        ),
        grid_spec=pltpu.PrefetchScalarGridSpec(
            num_scalar_prefetch=2,
            grid=(count // bq,),
            in_specs=[
                wide,
                whole(*kv.shape),
                near,
                pl.BlockSpec((bq, q.shape[0]), lambda i, *_: (i + first, 0)),
                pl.BlockSpec((heads, bq), lambda i, *_: (0, i)),
                pl.BlockSpec((1, bq), lambda i, *_: (0, i + first)),
                pl.BlockSpec((1, bq), lambda i, *_: (0, i + first)),
                whole(total, 1),
                whole(total, 1),
            ]
            + [whole(*kv.shape)] * len(carried),
            out_specs=(near, whole(*kv.shape)),
            scratch_shapes=[
                pltpu.VMEM(kv.shape, bf16),
                pltpu.VMEM(kv.shape, bf16),
                pltpu.VMEM((heads * 2 * HEAD_DIM, bq), bf16),
                pltpu.VMEM((heads * 2 * HEAD_DIM, bq), bf16),
                pltpu.VMEM((heads * bq, 2 * HEAD_DIM), bf16),
                pltpu.VMEM((heads * bq, 2 * HEAD_DIM), bf16),
                pltpu.VMEM((heads * bq, 2 * HEAD_DIM), f32),
                pltpu.VMEM(kv.shape, f32),
            ],
        ),
        cost_estimate=pl.CostEstimate(flops=heads * count * total * 640, bytes_accessed=8 << 20, transcendentals=heads * count * total // 2),
        name="attend_grad",
    )(start, seg, q, kv, o, do, l, qpos.reshape(1, -1), qseg.reshape(1, -1), kpos.reshape(-1, 1), kseg.reshape(-1, 1), *carried)


HEADS = 16
KV_HEADS = 4
rope_base = 10000.0
SHARE = ("dp", "context")
EVERY = ("dp", "context", "tensor")
QUERY_BLOCK = 512
KEY_BLOCK = 512
CHUNKS = 2


def unit_rows(values):
    r = lax.rsqrt(jnp.mean(values * values, axis=-1, keepdims=True) + epsilon)
    return values * r, r


def norm_back(grad, values, gains):
    n, r = unit_rows(values)
    scaled = grad * gains
    return r * (scaled - n * jnp.mean(scaled * n, axis=-1, keepdims=True)), jnp.sum(grad * n, axis=0)


def mixed_silu(gate_in, up_in):
    return jax.nn.silu(gate_in) * up_in


def gathered(part, axes, axis):
    return lax.all_gather(part, axes, axis=axis, tiled=True)


def scattered(part, axes, axis):
    return lax.psum_scatter(part.astype(bf16), axes, scatter_dimension=axis, tiled=True)


def natural(values):
    return with_layout_constraint(values, Layout(major_to_minor=tuple(range(values.ndim))))


def after(value, *others):
    return lax.optimization_barrier((value,) + others)[0]


def halving_scatter(terms, axes):
    sizes = [lax.axis_size(axis) for axis in axes]
    blocks = terms.reshape(tuple(sizes) + (-1,) + terms.shape[1:])
    for place, axis in enumerate(axes):
        size, me = sizes[place], lax.axis_index(axis)
        stride = 1
        while stride < size:
            shape = blocks.shape
            split = blocks.reshape(shape[:place] + (shape[place] // 2, 2) + shape[place + 1 :])
            bit = (me // stride) % 2
            kept, sent = (
                lax.dynamic_index_in_dim(split, index, place + 1, keepdims=False) for index in (bit, 1 - bit)
            )
            got = lax.ppermute(sent, axis, [(i, i ^ stride) for i in range(size)])
            blocks = (kept.astype(f32) + got.astype(f32)).astype(bf16)
            stride *= 2
    return blocks.reshape((-1,) + terms.shape[1:])


def spread(part):
    ways, me = lax.axis_size("tensor"), lax.axis_index("tensor")
    out = lax.dynamic_update_index_in_dim(jnp.zeros((ways,) + part.shape, part.dtype), part, me, 0)
    for step in range(1, ways):
        got = lax.ppermute(part, "tensor", [(i, (i + step) % ways) for i in range(ways)])
        out = lax.dynamic_update_index_in_dim(out, got, (me - step) % ways, 0)
    return out


def line_total(part):
    total = part
    ways = lax.axis_size("tensor")
    for step in range(1, ways):
        total = total + lax.ppermute(part, "tensor", [(i, (i + step) % ways) for i in range(ways)])
    return total


def swap(blocks):
    ways, me = lax.axis_size("tensor"), lax.axis_index("tensor")
    out = blocks
    for step in range(1, ways):
        sent = lax.dynamic_index_in_dim(blocks, (me + step) % ways, 0, keepdims=False)
        got = lax.ppermute(sent, "tensor", [(i, (i + step) % ways) for i in range(ways)])
        out = lax.dynamic_update_index_in_dim(out, got, (me - step) % ways, 0)
    return out


def remote(source, target, sems, index, device):
    copy = pltpu.make_async_remote_copy(
        src_ref=source,
        dst_ref=target,
        send_sem=sems[0].at[index],
        recv_sem=sems[1].at[index],
        device_id=device,
        device_id_type=pl.DeviceIdType.MESH,
    )
    copy.start()
    return copy


def greet(devices):
    barrier = pltpu.get_barrier_semaphore()
    for device in devices:
        pl.semaphore_signal(barrier, inc=1, device_id=device, device_id_type=pl.DeviceIdType.MESH)
    pl.semaphore_wait(barrier, len(devices))


def aligned(start, size):
    return pl.ds(pl.multiple_of(start, size), size)


def gather_kernel(count, lines, pairs, shuffles, chunks, *refs):
    arrays = count + lines + pairs + shuffles
    sources, targets = refs[:arrays], refs[arrays : 2 * arrays]
    own_sem, send_sem, recv_sem = refs[2 * arrays : 2 * arrays + 3]
    dp, context = lax.axis_index("dp"), lax.axis_index("context")
    outer, inner = dp // 2, dp % 2
    across, along, beside = (
        {"dp": dp + 2 - 4 * outer},
        {"context": 1 - context},
        {"dp": dp + 1 - 2 * inner},
    )
    me, ways = lax.axis_index("tensor"), lax.axis_size("tensor")
    peers = [{"tensor": lax.rem(me + step, ways)} for step in range(1, ways)] if lines or shuffles else []
    greet(([across, along, beside] if count else [along]) + peers)

    def place(array, o, k, first=0, parts=1):
        rows = sources[array].shape[0]
        start = ((2 * o + inner) * 2 + k) * rows + first * (rows // parts)
        return targets[array].at[aligned(start, rows // parts), :]

    def send(array, kind, source, target, device):
        copy = pltpu.make_async_remote_copy(
            src_ref=source,
            dst_ref=target,
            send_sem=send_sem.at[array, kind],
            recv_sem=recv_sem.at[array, kind],
            device_id=device,
            device_id_type=pl.DeviceIdType.MESH,
        )
        copy.start()
        return copy

    copies, kept = {}, []
    passed = []
    for a in range(count + lines + pairs, arrays):
        size, width = sources[a].shape[0] // chunks, sources[a].shape[1] // ways
        for c in range(chunks):
            rows = pl.ds(c * size, size)
            target = targets[a].at[aligned((c * ways + me) * size, size), :]
            for k, peer in enumerate(peers):
                source = sources[a].at[rows, aligned(peer["tensor"] * width, width)]
                passed.append(send(a, c * (ways - 1) + k, source, target, peer))
            keep = pltpu.make_async_copy(sources[a].at[rows, aligned(me * width, width)], target, own_sem.at[a + c])
            keep.start()
            kept.append(keep)
    for a in range(count + lines, count + lines + pairs):
        rows = sources[a].shape[0]
        mine = targets[a].at[aligned(context * rows, rows), :]
        passed.append(send(a, 0, sources[a], mine, along))
        keep = pltpu.make_async_copy(sources[a], mine, own_sem.at[a])
        keep.start()
        kept.append(keep)
    for a in range(count):
        mine = place(a, outer, context)
        copies[a, 0] = send(a, 0, sources[a], mine, across)
        copies[a, 1] = send(a, 1, sources[a], mine, along)
        copies[a, 2] = send(a, 2, sources[a], mine, beside)
        keep = pltpu.make_async_copy(sources[a], mine, own_sem.at[a])
        keep.start()
        kept.append(keep)
    for a in range(count, count + lines):
        width = sources[a].shape[1]
        mine = targets[a].at[:, aligned(me * width, width)]
        for k, peer in enumerate(peers):
            passed.append(send(a, k, sources[a], mine, peer))
        keep = pltpu.make_async_copy(sources[a], mine, own_sem.at[a])
        keep.start()
        kept.append(keep)
    for a in range(count):
        copies[a, 0].wait_recv()
        got = place(a, 1 - outer, context)
        half = place(a, 1 - outer, context, 0, 2)
        copies[a, 3] = send(a, 3, half, half, along)
        copies[a, 4] = send(a, 4, got, got, beside)
        copies[a, 1].wait_recv()
        got = place(a, outer, 1 - context)
        half = place(a, outer, 1 - context, 1, 2)
        copies[a, 5] = send(a, 5, half, half, across)
        copies[a, 6] = send(a, 6, got, got, beside)
    for a in range(count):
        for kind, first in ((3, 0), (5, 1)):
            copies[a, kind].wait_recv()
            half = place(a, 1 - outer, 1 - context, first, 2)
            copies[a, 7 + first] = send(a, 7 + first, half, half, beside)
    for keep in kept:
        keep.wait()
    for copy in passed:
        copy.wait()
    for a in range(count):
        for kind in (2, 4, 6, 7, 8):
            copies[a, kind].wait_recv()
    for copy in copies.values():
        copy.wait_send()


def plane_gather(parts, lines, pairs, collective, shuffles=(), chunks=1):
    share, ways = lax.axis_size("dp") * lax.axis_size("context"), lax.axis_size("tensor")
    if (lax.axis_size("dp"), lax.axis_size("context")) != (4, 2):
        whole = [gathered(part, SHARE, 0) for part in parts] + [jnp.concatenate(list(spread(line)), axis=1) for line in lines]
        whole += [gathered(pair, "context", 0) for pair in pairs]
        for grad in shuffles:
            blocks = grad.reshape(chunks, grad.shape[0] // chunks, ways, -1).transpose(2, 0, 1, 3)
            whole.append(swap(blocks).transpose(1, 0, 2, 3).reshape(ways * grad.shape[0], -1))
        return whole
    arrays = len(parts) + len(lines) + len(pairs) + len(shuffles)
    shapes = [(share * part.shape[0], part.shape[1]) for part in parts] + [(line.shape[0], ways * line.shape[1]) for line in lines]
    shapes += [(2 * pair.shape[0], pair.shape[1]) for pair in pairs]
    shapes += [(ways * grad.shape[0], grad.shape[1] // ways) for grad in shuffles]
    return pl.pallas_call(
        functools.partial(gather_kernel, len(parts), len(lines), len(pairs), len(shuffles), chunks),
        out_shape=tuple(jax.ShapeDtypeStruct(shape, bf16) for shape in shapes),
        in_specs=[pl.BlockSpec(memory_space=pltpu.VMEM)] * arrays,
        out_specs=(pl.BlockSpec(memory_space=pl.ANY),) * arrays,
        scratch_shapes=[
            pltpu.SemaphoreType.DMA((arrays + chunks,)),
            pltpu.SemaphoreType.DMA((arrays, 9)),
            pltpu.SemaphoreType.DMA((arrays, 9)),
        ],
        compiler_params=pltpu.CompilerParams(collective_id=collective, has_side_effects=True),
        name="plane_gather",
    )(*parts, *lines, *pairs, *shuffles)


def tail_kernel(heads, ways, chunks, joint_ref, cos_ref, sin_ref, gain_ref, dq_ref, dkv_ref,
                grad_ref, part_ref, dgain_ref, got_ref, own_sem, send_sem, recv_sem):
    D, half = HEAD_DIM, HEAD_DIM // 2
    rows, count = joint_ref.shape
    queries = heads * D
    me, context = lax.axis_index("tensor"), lax.axis_index("context")
    peers = [lax.rem(me + step, ways) for step in range(1, ways)]
    along = {"context": 1 - context}
    greet([along] + [{"tensor": peer} for peer in peers])
    sems = (send_sem, recv_sem)
    block = min(count, 512)
    size = count // chunks // ways
    copies = [remote(dkv_ref.at[aligned((1 - context) * count, count), :], got_ref, sems, 0, along)]

    def one(first, columns, grad, gain):
        x = joint_ref[first : first + D, columns]
        cos, sin = cos_ref[:, columns], sin_ref[:, columns]
        r = lax.rsqrt(jnp.mean(x * x, axis=0, keepdims=True) + epsilon)
        n = x * r
        lo, hi = grad[:half], grad[half:]
        back = jnp.concatenate([lo * cos + hi * sin, hi * cos - lo * sin], axis=0)
        scaled = back * gain
        result = r * (scaled - n * jnp.mean(scaled * n, axis=0, keepdims=True))
        grad_ref[first : first + D, columns] = result.astype(bf16)
        return jnp.sum(back * n, axis=1, keepdims=True)

    def hand_out(first, height, index):
        for c in range(chunks):
            target = part_ref.at[pl.ds(pl.multiple_of(me * rows + first, 128), height), pl.ds(c * size, size)]
            for k, peer in enumerate(peers):
                source = grad_ref.at[pl.ds(first, height), aligned((c * ways + peer) * size, size)]
                copies.append(remote(source, target, sems, 1 + (index * chunks + c) * (ways - 1) + k, {"tensor": peer}))
            kept = pltpu.make_async_copy(
                grad_ref.at[pl.ds(first, height), aligned((c * ways + me) * size, size)], target, own_sem.at[index * chunks + c]
            )
            kept.start()
            copies.append(kept)

    total = jnp.zeros((D, 1), f32)
    for b in range(count // block):
        columns = slice(b * block, (b + 1) * block)
        for h in range(heads):
            total += one(h * D, columns, dq_ref[h * D : (h + 1) * D, columns], gain_ref[:, 0:1])
    hand_out(0, queries, 0)
    copies[0].wait_recv()
    key_total = jnp.zeros((D, 1), f32)
    for b in range(count // block):
        columns = slice(b * block, (b + 1) * block)
        mine = dkv_ref[aligned(context * count + b * block, block), :].astype(f32)
        both = (mine + got_ref[columns, :].astype(f32)).T
        key_total += one(queries, columns, both[:D], gain_ref[:, 1:2])
        grad_ref[queries + D : queries + 2 * D, columns] = both[D:].astype(bf16)
    hand_out(queries, 2 * D, 1)
    dgain_ref[...] = jnp.concatenate([total, key_total], axis=1)
    copies[0].wait_send()
    for copy in copies[1:]:
        copy.wait()


def joint_tail(joint, cos, sin, gains, dq, dkv, heads, chunks, collective):
    rows, count = joint.shape
    ways = lax.axis_size("tensor")
    number = 1 + 2 * chunks * (ways - 1)
    vmem = pl.BlockSpec(memory_space=pltpu.VMEM)
    return pl.pallas_call(
        functools.partial(tail_kernel, heads, ways, chunks),
        out_shape=(
            jax.ShapeDtypeStruct((rows, count), bf16),
            jax.ShapeDtypeStruct((ways * rows, count // ways), bf16),
            jax.ShapeDtypeStruct((HEAD_DIM, 2), f32),
        ),
        in_specs=[vmem] * 6,
        out_specs=(vmem, pl.BlockSpec(memory_space=pl.ANY), vmem),
        scratch_shapes=[
            pltpu.VMEM((count, 2 * HEAD_DIM), bf16),
            pltpu.SemaphoreType.DMA((2 * chunks,)),
            pltpu.SemaphoreType.DMA((number,)),
            pltpu.SemaphoreType.DMA((number,)),
        ],
        compiler_params=pltpu.CompilerParams(collective_id=collective, has_side_effects=True),
        name="joint_tail",
    )(joint, cos, sin, gains, dq, dkv)


def rope_tables(positions):
    half = HEAD_DIM // 2
    inverse = jnp.exp(-math.log(rope_base) * jnp.arange(half, dtype=f32) * 2.0 / HEAD_DIM)
    angles = inverse[:, None] * positions.astype(f32)[None, :]
    return jnp.cos(angles), jnp.sin(angles)


def body(
    layer_input, cotangent, w_qkv, w_out, attn_gain, qk_gain, w_gate, w_up, w_down, ffn_gain, seg_ids, pos_ids
):
    _, rows, width = layer_input.shape
    ways = lax.axis_size("tensor")
    heads = HEADS // ways
    mine = lax.axis_index("tensor")
    group_seg, group_pos = seg_ids[0], pos_ids[0]
    first_row = lax.axis_index("context") * rows
    my_seg = lax.dynamic_slice_in_dim(group_seg, first_row, rows, 0)
    my_pos = lax.dynamic_slice_in_dim(group_pos, first_row, rows, 0)
    start = jnp.reshape(first_row, (1,)).astype(jnp.int32)
    columns = w_qkv.shape[1]
    qkv_shard = w_qkv.T
    packed = jnp.concatenate(
        [qkv_shard, attn_gain[None], ffn_gain[None], jnp.zeros((14, w_qkv.shape[0]), bf16)], axis=0
    )
    packed_all, gate_all, out_t, qkv_t = plane_gather([packed.T, w_gate], [w_out.T, w_qkv], [], 0)
    packed_all = packed_all.T
    qkv_mine = packed_all[:columns]
    attn_gain_all = packed_all[columns].astype(f32)
    ffn_gain_all = packed_all[columns + 1].astype(f32)

    tokens_in = layer_input.reshape(rows, width)
    cot = cotangent.reshape(rows, width)
    normed_low = (unit_rows(tokens_in.astype(f32))[0] * attn_gain_all).astype(bf16)
    joint = dot_nt(qkv_mine, normed_low)
    cos, sin = rope_tables(my_pos)
    gains = qk_gain.T
    queries, kv_mine = prep(joint, cos, sin, gains, heads, 512)
    (kv,) = plane_gather([], [], [kv_mine], 1)
    up_all = gathered(after(w_up, kv), SHARE, 0)
    chunk_rows = rows // CHUNKS
    part_rows = chunk_rows // ways
    chunks = [slice(c * chunk_rows, (c + 1) * chunk_rows) for c in range(CHUNKS)]

    def own_rows(values, c):
        return lax.dynamic_slice_in_dim(values, c * chunk_rows + mine * part_rows, part_rows, 0)

    keys = (group_pos, group_seg)
    attended, log_total, attended_all = [], [], []
    for c in range(CHUNKS):
        result, total = attention(
            start + c * chunk_rows, group_seg, queries, kv, my_pos, my_seg, *keys, QUERY_BLOCK, KEY_BLOCK, c, CHUNKS
        )
        attended.append(result)
        log_total.append(total)
        attended_all.append(gathered(result, "tensor", 0))

    out_all, down_all = plane_gather([after(out_t, up_all, *attended), w_down.T], [], [], 5)

    resid_parts, normed_ffns, acts, gate_grads, up_grads, ffn_in_grads = [], [], [], [], [], []
    previous = attended[-1]
    for c, chunk in enumerate(chunks):
        act_grad = dot_nn(cot[chunk], after(down_all, previous))
        resid = tokens_in[chunk].astype(f32) + natural(dot_tt(after(attended_all[c], act_grad), out_all))
        normed_ffn = (unit_rows(resid)[0] * ffn_gain_all).astype(bf16)
        gate, up = dot_nn(normed_ffn, gate_all), dot_nn(normed_ffn, up_all)
        act, silu_pull = jax.vjp(mixed_silu, gate, up)
        gate_grad, up_grad = (g.astype(bf16) for g in silu_pull(act_grad))
        previous = (dot_nt(gate_grad, gate_all) + dot_nt(up_grad, up_all)).astype(bf16)
        ffn_in_grads.append(scattered(previous, "tensor", 0).astype(f32))
        resid_parts.append(own_rows(resid, 0))
        normed_ffns.append(normed_ffn)
        acts.append(act.astype(bf16))
        gate_grads.append(gate_grad)
        up_grads.append(up_grad)
    normed_ffn, act, gate_grad, up_grad = (
        jnp.concatenate(pieces, axis=0) for pieces in (normed_ffns, acts, gate_grads, up_grads)
    )
    act, gate_grad, up_grad, _ = lax.optimization_barrier((act, gate_grad, up_grad, previous))
    ffn_part = dot_nt(act, down_all).astype(bf16)
    grad_down = dot_tn(cot, act).astype(bf16)
    grad_gate = dot_tn(normed_ffn, gate_grad).astype(bf16)
    grad_up = dot_tn(normed_ffn, up_grad).astype(bf16)
    ffn_gain_part, resid_grads, attended_grads, attended_parts, branches = 0.0, [], [], [], []
    for c in range(CHUNKS):
        norm_grad, gain_part = norm_back(ffn_in_grads[c], resid_parts[c], ffn_gain_all)
        ffn_gain_part += gain_part
        resid_grad = own_rows(cot, c).astype(f32) + norm_grad
        branch = resid_grad.astype(bf16)
        resid_grads.append(resid_grad)
        branches.append(branch)
        attended_grads.append(dot_nn(branch, out_all).astype(bf16))
        attended_parts.append(lax.dynamic_slice_in_dim(attended_all[c], mine * part_rows, part_rows, 1))

    attended_grad = after(jnp.concatenate(attended_grads, axis=0), ffn_part, grad_down, grad_gate, grad_up)
    qkv_all, attended_grad = plane_gather([qkv_t], [], [], 2, [attended_grad], CHUNKS)
    branch, attended_part = jnp.concatenate(branches, axis=0), jnp.concatenate(attended_parts, axis=1)
    grad_out = lax.dot_general(branch, attended_part, (((0,), (1,)), ((), ())), preferred_element_type=f32)
    grad_out = grad_out.astype(bf16)
    query_grads, carried, layer_parts, kept_part = [], [], [], ffn_part
    for c, chunk in enumerate(chunks):
        query_grad, kv_grad_group = attention_grad(
            start + c * chunk_rows, group_seg, queries, kv, attended[c], attended_grad, log_total[c],
            my_pos, my_seg, *keys, carried, QUERY_BLOCK, KEY_BLOCK, c, CHUNKS
        )
        query_grads.append(query_grad)
        if c < CHUNKS - 1:
            ffn_sum = scattered(kept_part[chunk], "tensor", 0).astype(f32)
            layer_parts.append((after(resid_parts[c], query_grad) + ffn_sum).astype(bf16))
            carried = [after(kv_grad_group, layer_parts[-1])]
            kept_part = after(ffn_part, layer_parts[-1])
    query_grad = jnp.concatenate(query_grads, axis=1)
    ffn_sum = scattered(kept_part[chunks[-1]], "tensor", 0).astype(f32)
    layer_parts.append((after(resid_parts[-1], query_grad) + ffn_sum).astype(bf16))
    layer_firsts = [gathered(part, "tensor", 0) for part in layer_parts[:-1]]
    if lax.axis_size("context") == 2:
        joint_grad, joint_grad_part, qk_part = joint_tail(
            joint, cos, sin, gains, query_grad, kv_grad_group, heads, CHUNKS, 3
        )
    else:
        kv_grad = halving_scatter(kv_grad_group, ("context",))
        joint_grad, qk_part = unprep(joint, cos, sin, gains, query_grad, kv_grad, heads, 512)
        tokens = joint_grad.reshape(columns, CHUNKS, ways, part_rows)
        joint_grad_part = swap(jnp.stack([tokens[:, :, i].reshape(columns, -1) for i in range(ways)]))
        joint_grad_part = joint_grad_part.reshape(ways * columns, -1)
    in_grad = natural(dot_tt(joint_grad_part, qkv_all))
    own_inputs = jnp.concatenate([own_rows(tokens_in, c) for c in range(CHUNKS)], axis=0).astype(f32)
    norm_grad = norm_back(in_grad, own_inputs, attn_gain_all)[0]
    grad_input = (jnp.concatenate(resid_grads, axis=0) + norm_grad).astype(bf16)
    late = lax.optimization_barrier((joint_grad, grad_input, grad_down, grad_gate, grad_up, grad_out))
    joint_late, _, grad_down, grad_gate, grad_up, grad_out = late
    grad_out = halving_scatter(grad_out, SHARE)
    grad_out = swap(jnp.stack([part.T for part in jnp.split(grad_out, ways, axis=1)]))
    grad_input = after(jnp.stack(jnp.split(grad_input, CHUNKS, axis=0)), *layer_firsts)
    layer_last = gathered(after(layer_parts[-1], grad_input), "tensor", 0)
    layer_output = jnp.concatenate(layer_firsts + [layer_last], axis=0).reshape(layer_input.shape)
    grad_input = gathered(grad_input, "tensor", 1).reshape(layer_input.shape)

    grad_qkv = dot_nn(joint_late, normed_low)
    attn_gain_part = jnp.sum(qkv_mine.astype(f32) * grad_qkv, axis=0) / attn_gain_all
    qk_rows = jnp.tile(qk_part.T, (1, width // HEAD_DIM))
    grad_qkv = jnp.concatenate(
        [grad_qkv, attn_gain_part[None], ffn_gain_part[None], qk_rows, jnp.zeros((12, width), f32)], axis=0
    )
    grad_qkv = halving_scatter(grad_qkv.astype(bf16).T, SHARE).astype(f32)
    small = line_total(grad_qkv[:, columns:].T)
    return (
        layer_output,
        grad_input,
        grad_qkv[:, :columns],
        jnp.sum(grad_out.astype(f32), axis=0),
        small[0],
        small[2:4, :HEAD_DIM],
        halving_scatter(grad_gate, SHARE).astype(f32),
        halving_scatter(grad_up, SHARE).astype(f32),
        halving_scatter(grad_down, SHARE).astype(f32).T,
        small[1],
    )


def solution(mesh):
    tokens, by_row, by_column = P("dp", "context", None), P(SHARE, "tensor"), P("tensor", SHARE)
    gain = P(SHARE)
    return jax.shard_map(
        body,
        mesh=mesh,
        in_specs=(
            tokens, tokens, by_row, by_column, gain, P(), by_row, by_row, by_column, gain, P("dp", None), P("dp", None)
        ),
        out_specs=(tokens, tokens, by_row, by_column, gain, P(), by_row, by_row, by_column, gain),
        check_vma=False,
    )
```

```python
import functools, math
import jax, jax.numpy as jnp
from jax import lax
from jax.experimental import pallas as pl
from jax.experimental.pallas import tpu as pltpu
from jax.experimental.layout import Layout, with_layout_constraint
from jax.sharding import PartitionSpec as P

HEAD_DIM = 64
LOG2E = math.log2(math.e)
LN2 = math.log(2.0)
f32 = jnp.float32
bf16 = jnp.bfloat16
epsilon = 1e-6


def dot_nt(a, b):
    return lax.dot_general(a, b, (((1,), (1,)), ((), ())), preferred_element_type=f32)

def dot_nn(a, b):
    return lax.dot_general(a, b, (((1,), (0,)), ((), ())), preferred_element_type=f32)

def dot_tn(a, b):
    return lax.dot_general(a, b, (((0,), (0,)), ((), ())), preferred_element_type=f32)


def dot_tt(a, b):
    return lax.dot_general(a, b, (((0,), (1,)), ((), ())), preferred_element_type=f32)


def head_norm(x):
    return x * lax.rsqrt(jnp.mean(x * x, axis=0, keepdims=True) + epsilon)


def prep_kernel(heads, joint_ref, cos_ref, sin_ref, gain_ref, q_ref, kv_ref):
    half = HEAD_DIM // 2
    cos, sin = cos_ref[...], sin_ref[...]

    def one(row, gain, scale):
        x = head_norm(joint_ref[row : row + HEAD_DIM, :]) * gain
        lo, hi = x[:half], x[half:]
        return jnp.concatenate([lo * cos - hi * sin, hi * cos + lo * sin], axis=0) * scale

    for h in range(heads):
        row = h * HEAD_DIM
        q_ref[row : row + HEAD_DIM, :] = one(row, gain_ref[:, 0:1], LOG2E * HEAD_DIM**-0.5).astype(bf16)
    row = heads * HEAD_DIM
    key = one(row, gain_ref[:, 1:2], 1.0)
    both = jnp.concatenate([key, joint_ref[row + HEAD_DIM : row + 2 * HEAD_DIM, :]], axis=0)
    kv_ref[...] = both.T.astype(bf16)


def prep(joint, cos, sin, gains, heads, block):
    rows, count = joint.shape
    block = min(block, count)
    return pl.pallas_call(
        functools.partial(prep_kernel, heads),
        out_shape=(
            jax.ShapeDtypeStruct((heads * HEAD_DIM, count), bf16),
            jax.ShapeDtypeStruct((count, 2 * HEAD_DIM), bf16),
        ),
        grid=(count // block,),
        in_specs=[
            pl.BlockSpec((rows, block), lambda i: (0, i)),
            pl.BlockSpec((HEAD_DIM // 2, block), lambda i: (0, i)),
            pl.BlockSpec((HEAD_DIM // 2, block), lambda i: (0, i)),
            pl.BlockSpec((HEAD_DIM, 2), lambda i: (0, 0)),
        ],
        out_specs=(
            pl.BlockSpec((heads * HEAD_DIM, block), lambda i: (0, i)),
            pl.BlockSpec((block, 2 * HEAD_DIM), lambda i: (i, 0)),
        ),
        cost_estimate=pl.CostEstimate(flops=rows * count * 20, bytes_accessed=rows * count * 6, transcendentals=0),
        name="prep",
    )(joint, cos, sin, gains)


def unprep_kernel(heads, joint_ref, cos_ref, sin_ref, gain_ref, dq_ref, dkv_ref, out_ref, dgain_ref):
    half = HEAD_DIM // 2
    cos, sin = cos_ref[...], sin_ref[...]

    @pl.when(pl.program_id(0) == 0)
    def _():
        dgain_ref[...] = jnp.zeros_like(dgain_ref)

    def one(row, grad, gain):
        x = joint_ref[row : row + HEAD_DIM, :]
        r = lax.rsqrt(jnp.mean(x * x, axis=0, keepdims=True) + epsilon)
        n = x * r
        lo, hi = grad[:half], grad[half:]
        back = jnp.concatenate([lo * cos + hi * sin, hi * cos - lo * sin], axis=0)
        scaled = back * gain
        result = r * (scaled - n * jnp.mean(scaled * n, axis=0, keepdims=True))
        out_ref[row : row + HEAD_DIM, :] = result.astype(bf16)
        return jnp.sum(back * n, axis=1, keepdims=True)

    total = None
    for h in range(heads):
        row = h * HEAD_DIM
        part = one(row, dq_ref[row : row + HEAD_DIM, :], gain_ref[:, 0:1])
        total = part if total is None else total + part
    row = heads * HEAD_DIM
    dkv = dkv_ref[...].astype(f32).T
    part = one(row, dkv[:HEAD_DIM], gain_ref[:, 1:2])
    out_ref[row + HEAD_DIM : row + 2 * HEAD_DIM, :] = dkv[HEAD_DIM:].astype(bf16)
    dgain_ref[...] += jnp.concatenate([total, part], axis=1)


def unprep(joint, cos, sin, gains, dq, dkv, heads, block):
    rows, count = joint.shape
    block = min(block, count)
    return pl.pallas_call(
        functools.partial(unprep_kernel, heads),
        out_shape=(
            jax.ShapeDtypeStruct((rows, count), bf16),
            jax.ShapeDtypeStruct((HEAD_DIM, 2), f32),
        ),
        grid=(count // block,),
        in_specs=[
            pl.BlockSpec((rows, block), lambda i: (0, i)),
            pl.BlockSpec((HEAD_DIM // 2, block), lambda i: (0, i)),
            pl.BlockSpec((HEAD_DIM // 2, block), lambda i: (0, i)),
            pl.BlockSpec((HEAD_DIM, 2), lambda i: (0, 0)),
            pl.BlockSpec((heads * HEAD_DIM, block), lambda i: (0, i)),
            pl.BlockSpec((block, 2 * HEAD_DIM), lambda i: (i, 0)),
        ],
        out_specs=(
            pl.BlockSpec((rows, block), lambda i: (0, i)),
            pl.BlockSpec((HEAD_DIM, 2), lambda i: (0, 0)),
        ),
        cost_estimate=pl.CostEstimate(flops=rows * count * 30, bytes_accessed=rows * count * 10, transcendentals=0),
        name="unprep",
    )(joint, cos, sin, gains, dq, dkv)


def block_state(seg_ref, start_ref, q_index, k_index, bq, bk):
    q_first = start_ref[0] + q_index * bq
    k_first = k_index * bk
    k_last_seg = seg_ref[k_first + bk - 1]
    needed = (k_first <= q_first + bq - 1) & ((k_last_seg == 0) | (k_last_seg >= seg_ref[q_first]) | (seg_ref[k_first] == 0))
    whole = (k_last_seg == 0) & (k_first + bk - 1 <= q_first)
    return needed, whole


def fwd_kernel(heads, bq, bk, start_ref, seg_ref, q_ref, kv_ref, qpos_ref, qseg_ref, kpos_ref, kseg_ref, o_ref, l_ref, vaug, qs, acc):
    qi = pl.program_id(0)
    nk = kv_ref.shape[0] // bk
    lane = lax.broadcasted_iota(jnp.int32, kv_ref.shape, 1)

    @pl.when(qi == 0)
    def _():
        vaug[...] = jnp.where(lane >= HEAD_DIM, kv_ref[...].astype(f32), jnp.where(lane == 0, 1.0, 0.0)).astype(bf16)

    zeros = jnp.zeros((HEAD_DIM, bq), f32)
    for h in range(heads):
        full = jnp.concatenate([q_ref[h * HEAD_DIM : (h + 1) * HEAD_DIM, :].astype(f32), zeros], axis=0)
        qs[h * bq : (h + 1) * bq, :] = full.T.astype(bf16)
    acc[...] = jnp.zeros_like(acc)

    def step(k_index, masked):
        rows = pl.ds(pl.multiple_of(k_index * bk, bk), bk)
        kb, vb = kv_ref[rows, :], vaug[rows, :]
        if masked:
            kseg = kseg_ref[k_index]
            mask = (kpos_ref[k_index] <= qpos_ref[...]) & ((kseg == 0) | (kseg == qseg_ref[...]))
        for h in range(heads):
            s = dot_nt(qs[h * bq : (h + 1) * bq, :], kb)
            p = jnp.exp2(s)
            if masked:
                p = jnp.where(mask, p, 0.0)
            acc[h * bq : (h + 1) * bq, :] += dot_nn(p.astype(bf16), vb)

    @pl.loop(0, nk)
    def _(k_index):
        needed, whole = block_state(seg_ref, start_ref, qi, k_index, bq, bk)

        @pl.when(needed & whole)
        def _():
            step(k_index, False)

        @pl.when(needed & jnp.logical_not(whole))
        def _():
            step(k_index, True)

    for h in range(heads):
        out = acc[h * bq : (h + 1) * bq, :].T
        total = out[0:1, :]
        o_ref[h * HEAD_DIM : (h + 1) * HEAD_DIM, :] = (out[HEAD_DIM:, :] / total).astype(bf16)
        l_ref[h : h + 1, :] = jnp.log2(total)


def attention(start, seg, q, kv, qpos, qseg, kpos, kseg, bq, bk, part, parts):
    heads = q.shape[0] // HEAD_DIM
    count, total = q.shape[1] // parts, kv.shape[0]
    bq, bk = min(bq, count), min(bk, total)
    first = part * (count // bq)
    whole = lambda *shape: pl.BlockSpec(shape, lambda i, *_: (0,) * len(shape))
    return pl.pallas_call(
        functools.partial(fwd_kernel, heads, bq, bk),
        out_shape=(
            jax.ShapeDtypeStruct((q.shape[0], count), bf16),
            jax.ShapeDtypeStruct((heads, count), f32),
        ),
        grid_spec=pltpu.PrefetchScalarGridSpec(
            num_scalar_prefetch=2,
            grid=(count // bq,),
            in_specs=[
                pl.BlockSpec((q.shape[0], bq), lambda i, *_: (0, i + first)),
                whole(*kv.shape),
                pl.BlockSpec((bq, 1), lambda i, *_: (i + first, 0)),
                pl.BlockSpec((bq, 1), lambda i, *_: (i + first, 0)),
                whole(total // bk, 1, bk),
                whole(total // bk, 1, bk),
            ],
            out_specs=(
                pl.BlockSpec((q.shape[0], bq), lambda i, *_: (0, i)),
                pl.BlockSpec((heads, bq), lambda i, *_: (0, i)),
            ),
            scratch_shapes=[
                pltpu.VMEM(kv.shape, bf16),
                pltpu.VMEM((heads * bq, 2 * HEAD_DIM), bf16),
                pltpu.VMEM((heads * bq, 2 * HEAD_DIM), f32),
            ],
        ),
        cost_estimate=pl.CostEstimate(flops=heads * count * total * 256, bytes_accessed=4 << 20, transcendentals=heads * count * total // 2),
        name="attend",
    )(start, seg, q, kv, qpos.reshape(-1, 1), qseg.reshape(-1, 1), kpos.reshape(-1, 1, bk), kseg.reshape(-1, 1, bk))


def split3(x):
    a = x.astype(bf16).astype(f32)
    b = (x - a).astype(bf16).astype(f32)
    return a, b, x - a - b


def bwd_kernel(heads, bq, bk, final, start_ref, seg_ref, q_ref, kv_ref, o_ref, do_ref, l_ref, qpos_ref, qseg_ref, kpos_ref, kseg_ref, *rest):
    carried, (dq_ref, dkv_ref, kaug, vaug, qst, dst, qs, ds, dacc, dkv) = rest[:-10], rest[-10:]
    qi = pl.program_id(0)
    nk = kv_ref.shape[0] // bk
    D = HEAD_DIM

    @pl.when(qi == 0)
    def _():
        lane = lax.broadcasted_iota(jnp.int32, kv_ref.shape, 1)
        kv = kv_ref[...].astype(f32)
        kaug[...] = jnp.where(lane < D, kv, jnp.where(lane < D + 3, -1.0, 0.0)).astype(bf16)
        vaug[...] = jnp.where(lane >= D, kv, jnp.where(lane < 3, -1.0, 0.0)).astype(bf16)
        dkv[...] = carried[0][...] if carried else jnp.zeros_like(dkv)

    row = lax.broadcasted_iota(jnp.int32, (D, bq), 0)

    def extra(x):
        a, b, c = split3(x)
        return jnp.where(row == 0, a, jnp.where(row == 1, b, jnp.where(row == 2, c, 0.0)))

    zeros = jnp.zeros((D, bq), f32)
    do_all = do_ref[...].astype(f32).T
    for h in range(heads):
        part = slice(h * D, (h + 1) * D)
        wide = slice(h * 2 * D, (h + 1) * 2 * D)
        q, do, o = q_ref[part, :].astype(f32), do_all[part, :], o_ref[part, :].astype(f32)
        delta = jnp.sum(do * o, axis=0, keepdims=True)
        qst[wide, :] = jnp.concatenate([q, extra(l_ref[h : h + 1, :])], axis=0).astype(bf16)
        dst[wide, :] = jnp.concatenate([extra(delta), do], axis=0).astype(bf16)
        qs[h * bq : (h + 1) * bq, :] = jnp.concatenate([q, zeros], axis=0).T.astype(bf16)
        ds[h * bq : (h + 1) * bq, :] = jnp.concatenate([zeros, do], axis=0).T.astype(bf16)
    dacc[...] = jnp.zeros_like(dacc)

    def step(k_index, masked):
        rows = pl.ds(pl.multiple_of(k_index * bk, bk), bk)
        kb, vb, kvb = kaug[rows, :], vaug[rows, :], kv_ref[rows, :]
        if masked:
            kseg = kseg_ref[rows, :]
            mask = (kpos_ref[rows, :] <= qpos_ref[...]) & ((kseg == 0) | (kseg == qseg_ref[...]))
        add = None
        for h in range(heads):
            wide = slice(h * 2 * D, (h + 1) * 2 * D)
            tall = slice(h * bq, (h + 1) * bq)
            p = jnp.exp2(dot_nn(kb, qst[wide, :]))
            if masked:
                p = jnp.where(mask, p, 0.0)
            sg = (p * dot_nn(vb, dst[wide, :])).astype(bf16)
            part = dot_nn(sg, qs[tall, :]) + dot_nn(p.astype(bf16), ds[tall, :])
            add = part if add is None else add + part
            dacc[tall, :] += dot_tn(sg, kvb)
        dkv[rows, :] += add

    @pl.loop(0, nk)
    def _(k_index):
        needed, whole = block_state(seg_ref, start_ref, qi, k_index, bq, bk)

        @pl.when(needed & whole)
        def _():
            step(k_index, False)

        @pl.when(needed & jnp.logical_not(whole))
        def _():
            step(k_index, True)

    for h in range(heads):
        dq_ref[h * D : (h + 1) * D, :] = dacc[h * bq : (h + 1) * bq, :].T[:D, :] * D**-0.5

    @pl.when(qi == pl.num_programs(0) - 1)
    def _():
        lane = lax.broadcasted_iota(jnp.int32, dkv.shape, 1)
        scale = jnp.where(lane < D, LN2, 1.0) if final else 1.0
        dkv_ref[...] = (dkv[...] * scale).astype(dkv_ref.dtype)


def attention_grad(start, seg, q, kv, o, do, l, qpos, qseg, kpos, kseg, carried, bq, bk, part, parts):
    heads = q.shape[0] // HEAD_DIM
    count, total = q.shape[1] // parts, kv.shape[0]
    bq, bk = min(bq, count), min(bk, total)
    first = part * (count // bq)
    final = part == parts - 1
    whole = lambda *shape: pl.BlockSpec(shape, lambda i, *_: (0,) * len(shape))
    wide = pl.BlockSpec((q.shape[0], bq), lambda i, *_: (0, i + first))
    near = pl.BlockSpec((q.shape[0], bq), lambda i, *_: (0, i))
    return pl.pallas_call(
        functools.partial(bwd_kernel, heads, bq, bk, final),
        out_shape=(
            jax.ShapeDtypeStruct((q.shape[0], count), f32),
            jax.ShapeDtypeStruct(kv.shape, bf16 if final else f32),
        ),
        grid_spec=pltpu.PrefetchScalarGridSpec(
            num_scalar_prefetch=2,
            grid=(count // bq,),
            in_specs=[
                wide,
                whole(*kv.shape),
                near,
                pl.BlockSpec((bq, q.shape[0]), lambda i, *_: (i + first, 0)),
                pl.BlockSpec((heads, bq), lambda i, *_: (0, i)),
                pl.BlockSpec((1, bq), lambda i, *_: (0, i + first)),
                pl.BlockSpec((1, bq), lambda i, *_: (0, i + first)),
                whole(total, 1),
                whole(total, 1),
            ]
            + [whole(*kv.shape)] * len(carried),
            out_specs=(near, whole(*kv.shape)),
            scratch_shapes=[
                pltpu.VMEM(kv.shape, bf16),
                pltpu.VMEM(kv.shape, bf16),
                pltpu.VMEM((heads * 2 * HEAD_DIM, bq), bf16),
                pltpu.VMEM((heads * 2 * HEAD_DIM, bq), bf16),
                pltpu.VMEM((heads * bq, 2 * HEAD_DIM), bf16),
                pltpu.VMEM((heads * bq, 2 * HEAD_DIM), bf16),
                pltpu.VMEM((heads * bq, 2 * HEAD_DIM), f32),
                pltpu.VMEM(kv.shape, f32),
            ],
        ),
        cost_estimate=pl.CostEstimate(flops=heads * count * total * 640, bytes_accessed=8 << 20, transcendentals=heads * count * total // 2),
        name="attend_grad",
    )(start, seg, q, kv, o, do, l, qpos.reshape(1, -1), qseg.reshape(1, -1), kpos.reshape(-1, 1), kseg.reshape(-1, 1), *carried)


HEADS = 16
KV_HEADS = 4
rope_base = 10000.0
SHARE = ("dp", "context")
EVERY = ("dp", "context", "tensor")
QUERY_BLOCK = 512
KEY_BLOCK = 512
CHUNKS = 2


def unit_rows(values):
    r = lax.rsqrt(jnp.mean(values * values, axis=-1, keepdims=True) + epsilon)
    return values * r, r


def norm_back(grad, values, gains):
    n, r = unit_rows(values)
    scaled = grad * gains
    return r * (scaled - n * jnp.mean(scaled * n, axis=-1, keepdims=True)), jnp.sum(grad * n, axis=0)


def mixed_silu(gate_in, up_in):
    return jax.nn.silu(gate_in) * up_in


def gathered(part, axes, axis):
    return lax.all_gather(part, axes, axis=axis, tiled=True)


def scattered(part, axes, axis):
    return lax.psum_scatter(part.astype(bf16), axes, scatter_dimension=axis, tiled=True)


def natural(values):
    return with_layout_constraint(values, Layout(major_to_minor=tuple(range(values.ndim))))


def after(value, *others):
    return lax.optimization_barrier((value,) + others)[0]


def halving_scatter(terms, axes):
    sizes = [lax.axis_size(axis) for axis in axes]
    blocks = terms.reshape(tuple(sizes) + (-1,) + terms.shape[1:])
    for place, axis in enumerate(axes):
        size, me = sizes[place], lax.axis_index(axis)
        stride = 1
        while stride < size:
            shape = blocks.shape
            split = blocks.reshape(shape[:place] + (shape[place] // 2, 2) + shape[place + 1 :])
            bit = (me // stride) % 2
            kept, sent = (
                lax.dynamic_index_in_dim(split, index, place + 1, keepdims=False) for index in (bit, 1 - bit)
            )
            got = lax.ppermute(sent, axis, [(i, i ^ stride) for i in range(size)])
            blocks = (kept.astype(f32) + got.astype(f32)).astype(bf16)
            stride *= 2
    return blocks.reshape((-1,) + terms.shape[1:])


def spread(part):
    ways, me = lax.axis_size("tensor"), lax.axis_index("tensor")
    out = lax.dynamic_update_index_in_dim(jnp.zeros((ways,) + part.shape, part.dtype), part, me, 0)
    for step in range(1, ways):
        got = lax.ppermute(part, "tensor", [(i, (i + step) % ways) for i in range(ways)])
        out = lax.dynamic_update_index_in_dim(out, got, (me - step) % ways, 0)
    return out


def line_total(part):
    total = part
    ways = lax.axis_size("tensor")
    for step in range(1, ways):
        total = total + lax.ppermute(part, "tensor", [(i, (i + step) % ways) for i in range(ways)])
    return total


def swap(blocks):
    ways, me = lax.axis_size("tensor"), lax.axis_index("tensor")
    out = blocks
    for step in range(1, ways):
        sent = lax.dynamic_index_in_dim(blocks, (me + step) % ways, 0, keepdims=False)
        got = lax.ppermute(sent, "tensor", [(i, (i + step) % ways) for i in range(ways)])
        out = lax.dynamic_update_index_in_dim(out, got, (me - step) % ways, 0)
    return out


def remote(source, target, sems, index, device):
    copy = pltpu.make_async_remote_copy(
        src_ref=source,
        dst_ref=target,
        send_sem=sems[0].at[index],
        recv_sem=sems[1].at[index],
        device_id=device,
        device_id_type=pl.DeviceIdType.MESH,
    )
    copy.start()
    return copy


def greet(devices):
    barrier = pltpu.get_barrier_semaphore()
    for device in devices:
        pl.semaphore_signal(barrier, inc=1, device_id=device, device_id_type=pl.DeviceIdType.MESH)
    pl.semaphore_wait(barrier, len(devices))


def aligned(start, size):
    return pl.ds(pl.multiple_of(start, size), size)


def gather_kernel(count, lines, pairs, shuffles, chunks, *refs):
    arrays = count + lines + pairs + shuffles
    sources, targets = refs[:arrays], refs[arrays : 2 * arrays]
    own_sem, send_sem, recv_sem = refs[2 * arrays : 2 * arrays + 3]
    dp, context = lax.axis_index("dp"), lax.axis_index("context")
    outer, inner = dp // 2, dp % 2
    across, along, beside = (
        {"dp": dp + 2 - 4 * outer},
        {"context": 1 - context},
        {"dp": dp + 1 - 2 * inner},
    )
    me, ways = lax.axis_index("tensor"), lax.axis_size("tensor")
    peers = [{"tensor": lax.rem(me + step, ways)} for step in range(1, ways)] if lines or shuffles else []
    greet(([across, along, beside] if count else [along]) + peers)

    def place(array, o, k, first=0, parts=1):
        rows = sources[array].shape[0]
        start = ((2 * o + inner) * 2 + k) * rows + first * (rows // parts)
        return targets[array].at[aligned(start, rows // parts), :]

    def send(array, kind, source, target, device):
        copy = pltpu.make_async_remote_copy(
            src_ref=source,
            dst_ref=target,
            send_sem=send_sem.at[array, kind],
            recv_sem=recv_sem.at[array, kind],
            device_id=device,
            device_id_type=pl.DeviceIdType.MESH,
        )
        copy.start()
        return copy

    copies, kept = {}, []
    passed = []
    for a in range(count + lines + pairs, arrays):
        size, width = sources[a].shape[0] // chunks, sources[a].shape[1] // ways
        for c in range(chunks):
            rows = pl.ds(c * size, size)
            target = targets[a].at[aligned((c * ways + me) * size, size), :]
            for k, peer in enumerate(peers):
                source = sources[a].at[rows, aligned(peer["tensor"] * width, width)]
                passed.append(send(a, c * (ways - 1) + k, source, target, peer))
            keep = pltpu.make_async_copy(sources[a].at[rows, aligned(me * width, width)], target, own_sem.at[a + c])
            keep.start()
            kept.append(keep)
    for a in range(count + lines, count + lines + pairs):
        rows = sources[a].shape[0]
        mine = targets[a].at[aligned(context * rows, rows), :]
        passed.append(send(a, 0, sources[a], mine, along))
        keep = pltpu.make_async_copy(sources[a], mine, own_sem.at[a])
        keep.start()
        kept.append(keep)
    for a in range(count):
        mine = place(a, outer, context)
        copies[a, 0] = send(a, 0, sources[a], mine, across)
        copies[a, 1] = send(a, 1, sources[a], mine, along)
        copies[a, 2] = send(a, 2, sources[a], mine, beside)
        keep = pltpu.make_async_copy(sources[a], mine, own_sem.at[a])
        keep.start()
        kept.append(keep)
    for a in range(count, count + lines):
        width = sources[a].shape[1]
        mine = targets[a].at[:, aligned(me * width, width)]
        for k, peer in enumerate(peers):
            passed.append(send(a, k, sources[a], mine, peer))
        keep = pltpu.make_async_copy(sources[a], mine, own_sem.at[a])
        keep.start()
        kept.append(keep)
    for a in range(count):
        copies[a, 0].wait_recv()
        got = place(a, 1 - outer, context)
        half = place(a, 1 - outer, context, 0, 2)
        copies[a, 3] = send(a, 3, half, half, along)
        copies[a, 4] = send(a, 4, got, got, beside)
        copies[a, 1].wait_recv()
        got = place(a, outer, 1 - context)
        half = place(a, outer, 1 - context, 1, 2)
        copies[a, 5] = send(a, 5, half, half, across)
        copies[a, 6] = send(a, 6, got, got, beside)
    for a in range(count):
        for kind, first in ((3, 0), (5, 1)):
            copies[a, kind].wait_recv()
            half = place(a, 1 - outer, 1 - context, first, 2)
            copies[a, 7 + first] = send(a, 7 + first, half, half, beside)
    for keep in kept:
        keep.wait()
    for copy in passed:
        copy.wait()
    for a in range(count):
        for kind in (2, 4, 6, 7, 8):
            copies[a, kind].wait_recv()
    for copy in copies.values():
        copy.wait_send()


def plane_gather(parts, lines, pairs, collective, shuffles=(), chunks=1):
    share, ways = lax.axis_size("dp") * lax.axis_size("context"), lax.axis_size("tensor")
    if (lax.axis_size("dp"), lax.axis_size("context")) != (4, 2):
        whole = [gathered(part, SHARE, 0) for part in parts] + [jnp.concatenate(list(spread(line)), axis=1) for line in lines]
        whole += [gathered(pair, "context", 0) for pair in pairs]
        for grad in shuffles:
            blocks = grad.reshape(chunks, grad.shape[0] // chunks, ways, -1).transpose(2, 0, 1, 3)
            whole.append(swap(blocks).transpose(1, 0, 2, 3).reshape(ways * grad.shape[0], -1))
        return whole
    arrays = len(parts) + len(lines) + len(pairs) + len(shuffles)
    shapes = [(share * part.shape[0], part.shape[1]) for part in parts] + [(line.shape[0], ways * line.shape[1]) for line in lines]
    shapes += [(2 * pair.shape[0], pair.shape[1]) for pair in pairs]
    shapes += [(ways * grad.shape[0], grad.shape[1] // ways) for grad in shuffles]
    return pl.pallas_call(
        functools.partial(gather_kernel, len(parts), len(lines), len(pairs), len(shuffles), chunks),
        out_shape=tuple(jax.ShapeDtypeStruct(shape, bf16) for shape in shapes),
        in_specs=[pl.BlockSpec(memory_space=pltpu.VMEM)] * arrays,
        out_specs=(pl.BlockSpec(memory_space=pl.ANY),) * arrays,
        scratch_shapes=[
            pltpu.SemaphoreType.DMA((arrays + chunks,)),
            pltpu.SemaphoreType.DMA((arrays, 9)),
            pltpu.SemaphoreType.DMA((arrays, 9)),
        ],
        compiler_params=pltpu.CompilerParams(collective_id=collective, has_side_effects=True),
        name="plane_gather",
    )(*parts, *lines, *pairs, *shuffles)


def tail_kernel(heads, ways, chunks, joint_ref, cos_ref, sin_ref, gain_ref, dq_ref, dkv_ref,
                grad_ref, part_ref, dgain_ref, got_ref, own_sem, send_sem, recv_sem):
    D, half = HEAD_DIM, HEAD_DIM // 2
    rows, count = joint_ref.shape
    queries = heads * D
    me, context = lax.axis_index("tensor"), lax.axis_index("context")
    peers = [lax.rem(me + step, ways) for step in range(1, ways)]
    along = {"context": 1 - context}
    greet([along] + [{"tensor": peer} for peer in peers])
    sems = (send_sem, recv_sem)
    block = min(count, 512)
    size = count // chunks // ways
    copies = [remote(dkv_ref.at[aligned((1 - context) * count, count), :], got_ref, sems, 0, along)]

    def one(first, columns, grad, gain):
        x = joint_ref[first : first + D, columns]
        cos, sin = cos_ref[:, columns], sin_ref[:, columns]
        r = lax.rsqrt(jnp.mean(x * x, axis=0, keepdims=True) + epsilon)
        n = x * r
        lo, hi = grad[:half], grad[half:]
        back = jnp.concatenate([lo * cos + hi * sin, hi * cos - lo * sin], axis=0)
        scaled = back * gain
        result = r * (scaled - n * jnp.mean(scaled * n, axis=0, keepdims=True))
        grad_ref[first : first + D, columns] = result.astype(bf16)
        return jnp.sum(back * n, axis=1, keepdims=True)

    def hand_out(first, height, index):
        for c in range(chunks):
            target = part_ref.at[pl.ds(pl.multiple_of(me * rows + first, 128), height), pl.ds(c * size, size)]
            for k, peer in enumerate(peers):
                source = grad_ref.at[pl.ds(first, height), aligned((c * ways + peer) * size, size)]
                copies.append(remote(source, target, sems, 1 + (index * chunks + c) * (ways - 1) + k, {"tensor": peer}))
            kept = pltpu.make_async_copy(
                grad_ref.at[pl.ds(first, height), aligned((c * ways + me) * size, size)], target, own_sem.at[index * chunks + c]
            )
            kept.start()
            copies.append(kept)

    total = jnp.zeros((D, 1), f32)
    for b in range(count // block):
        columns = slice(b * block, (b + 1) * block)
        for h in range(heads):
            total += one(h * D, columns, dq_ref[h * D : (h + 1) * D, columns], gain_ref[:, 0:1])
    hand_out(0, queries, 0)
    copies[0].wait_recv()
    key_total = jnp.zeros((D, 1), f32)
    for b in range(count // block):
        columns = slice(b * block, (b + 1) * block)
        mine = dkv_ref[aligned(context * count + b * block, block), :].astype(f32)
        both = (mine + got_ref[columns, :].astype(f32)).T
        key_total += one(queries, columns, both[:D], gain_ref[:, 1:2])
        grad_ref[queries + D : queries + 2 * D, columns] = both[D:].astype(bf16)
    hand_out(queries, 2 * D, 1)
    dgain_ref[...] = jnp.concatenate([total, key_total], axis=1)
    copies[0].wait_send()
    for copy in copies[1:]:
        copy.wait()


def joint_tail(joint, cos, sin, gains, dq, dkv, heads, chunks, collective):
    rows, count = joint.shape
    ways = lax.axis_size("tensor")
    number = 1 + 2 * chunks * (ways - 1)
    vmem = pl.BlockSpec(memory_space=pltpu.VMEM)
    return pl.pallas_call(
        functools.partial(tail_kernel, heads, ways, chunks),
        out_shape=(
            jax.ShapeDtypeStruct((rows, count), bf16),
            jax.ShapeDtypeStruct((ways * rows, count // ways), bf16),
            jax.ShapeDtypeStruct((HEAD_DIM, 2), f32),
        ),
        in_specs=[vmem] * 6,
        out_specs=(vmem, pl.BlockSpec(memory_space=pl.ANY), vmem),
        scratch_shapes=[
            pltpu.VMEM((count, 2 * HEAD_DIM), bf16),
            pltpu.SemaphoreType.DMA((2 * chunks,)),
            pltpu.SemaphoreType.DMA((number,)),
            pltpu.SemaphoreType.DMA((number,)),
        ],
        compiler_params=pltpu.CompilerParams(collective_id=collective, has_side_effects=True),
        name="joint_tail",
    )(joint, cos, sin, gains, dq, dkv)


def rope_tables(positions):
    half = HEAD_DIM // 2
    inverse = jnp.exp(-math.log(rope_base) * jnp.arange(half, dtype=f32) * 2.0 / HEAD_DIM)
    angles = inverse[:, None] * positions.astype(f32)[None, :]
    return jnp.cos(angles), jnp.sin(angles)


def body(
    layer_input, cotangent, w_qkv, w_out, attn_gain, qk_gain, w_gate, w_up, w_down, ffn_gain, seg_ids, pos_ids
):
    _, rows, width = layer_input.shape
    ways = lax.axis_size("tensor")
    heads = HEADS // ways
    mine = lax.axis_index("tensor")
    group_seg, group_pos = seg_ids[0], pos_ids[0]
    first_row = lax.axis_index("context") * rows
    my_seg = lax.dynamic_slice_in_dim(group_seg, first_row, rows, 0)
    my_pos = lax.dynamic_slice_in_dim(group_pos, first_row, rows, 0)
    start = jnp.reshape(first_row, (1,)).astype(jnp.int32)
    columns = w_qkv.shape[1]
    qkv_shard = w_qkv.T
    packed = jnp.concatenate(
        [qkv_shard, attn_gain[None], ffn_gain[None], jnp.zeros((14, w_qkv.shape[0]), bf16)], axis=0
    )
    gate_all = gathered(w_gate, SHARE, 0)
    (packed_all,) = plane_gather([packed.T], [], [], 0)
    packed_all = packed_all.T
    qkv_mine = packed_all[:columns]
    attn_gain_all = packed_all[columns].astype(f32)
    ffn_gain_all = packed_all[columns + 1].astype(f32)

    tokens_in = layer_input.reshape(rows, width)
    cot = cotangent.reshape(rows, width)
    normed_low = (unit_rows(tokens_in.astype(f32))[0] * attn_gain_all).astype(bf16)
    joint = dot_nt(qkv_mine, normed_low)
    cos, sin = rope_tables(my_pos)
    gains = qk_gain.T
    queries, kv_mine = prep(joint, cos, sin, gains, heads, 512)
    out_t, kv = plane_gather([], [w_out.T], [kv_mine], 1)
    up_all = gathered(after(w_up, kv), SHARE, 0)
    queries = after(queries, gate_all)
    chunk_rows = rows // CHUNKS
    part_rows = chunk_rows // ways
    chunks = [slice(c * chunk_rows, (c + 1) * chunk_rows) for c in range(CHUNKS)]

    def own_rows(values, c):
        return lax.dynamic_slice_in_dim(values, c * chunk_rows + mine * part_rows, part_rows, 0)

    keys = (group_pos, group_seg)
    attended, log_total, attended_all = [], [], []
    for c in range(CHUNKS):
        result, total = attention(
            start + c * chunk_rows, group_seg, queries, kv, my_pos, my_seg, *keys, QUERY_BLOCK, KEY_BLOCK, c, CHUNKS
        )
        attended.append(result)
        log_total.append(total)
        attended_all.append(gathered(result, "tensor", 0))

    out_all, down_all, qkv_t = plane_gather([after(out_t, up_all, *attended), w_down.T], [w_qkv], [], 5)

    resid_parts, normed_ffns, acts, gate_grads, up_grads, ffn_in_grads = [], [], [], [], [], []
    previous = attended[-1]
    for c, chunk in enumerate(chunks):
        act_grad = dot_nn(cot[chunk], after(down_all, previous))
        resid = tokens_in[chunk].astype(f32) + natural(dot_tt(after(attended_all[c], act_grad), out_all))
        normed_ffn = (unit_rows(resid)[0] * ffn_gain_all).astype(bf16)
        gate, up = dot_nn(normed_ffn, gate_all), dot_nn(normed_ffn, up_all)
        act, silu_pull = jax.vjp(mixed_silu, gate, up)
        gate_grad, up_grad = (g.astype(bf16) for g in silu_pull(act_grad))
        previous = (dot_nt(gate_grad, gate_all) + dot_nt(up_grad, up_all)).astype(bf16)
        ffn_in_grads.append(scattered(previous, "tensor", 0).astype(f32))
        resid_parts.append(own_rows(resid, 0))
        normed_ffns.append(normed_ffn)
        acts.append(act.astype(bf16))
        gate_grads.append(gate_grad)
        up_grads.append(up_grad)
    normed_ffn, act, gate_grad, up_grad = (
        jnp.concatenate(pieces, axis=0) for pieces in (normed_ffns, acts, gate_grads, up_grads)
    )
    act, gate_grad, up_grad, _ = lax.optimization_barrier((act, gate_grad, up_grad, previous))
    ffn_part = dot_nt(act, down_all).astype(bf16)
    grad_down = dot_tn(cot, act).astype(bf16)
    ffn_gain_part, resid_grads, attended_grads, attended_parts, branches = 0.0, [], [], [], []
    for c in range(CHUNKS):
        norm_grad, gain_part = norm_back(ffn_in_grads[c], resid_parts[c], ffn_gain_all)
        ffn_gain_part += gain_part
        resid_grad = own_rows(cot, c).astype(f32) + norm_grad
        branch = resid_grad.astype(bf16)
        resid_grads.append(resid_grad)
        branches.append(branch)
        attended_grads.append(dot_nn(branch, out_all).astype(bf16))
        attended_parts.append(lax.dynamic_slice_in_dim(attended_all[c], mine * part_rows, part_rows, 1))

    attended_grad = after(jnp.concatenate(attended_grads, axis=0), ffn_part, grad_down)
    qkv_all, attended_grad = plane_gather([qkv_t], [], [], 2, [attended_grad], CHUNKS)
    branch, attended_part = jnp.concatenate(branches, axis=0), jnp.concatenate(attended_parts, axis=1)
    grad_out = lax.dot_general(branch, attended_part, (((0,), (1,)), ((), ())), preferred_element_type=f32)
    grad_out = grad_out.astype(bf16)
    query_grads, carried, layer_parts, kept_part = [], [], [], ffn_part
    for c, chunk in enumerate(chunks):
        query_grad, kv_grad_group = attention_grad(
            start + c * chunk_rows, group_seg, queries, kv, attended[c], attended_grad, log_total[c],
            my_pos, my_seg, *keys, carried, QUERY_BLOCK, KEY_BLOCK, c, CHUNKS
        )
        query_grads.append(query_grad)
        if c < CHUNKS - 1:
            ffn_sum = scattered(kept_part[chunk], "tensor", 0).astype(f32)
            layer_parts.append((after(resid_parts[c], query_grad) + ffn_sum).astype(bf16))
            carried = [after(kv_grad_group, layer_parts[-1])]
            kept_part = after(ffn_part, layer_parts[-1])
    query_grad = jnp.concatenate(query_grads, axis=1)
    ffn_sum = scattered(kept_part[chunks[-1]], "tensor", 0).astype(f32)
    layer_parts.append((after(resid_parts[-1], query_grad) + ffn_sum).astype(bf16))
    layer_firsts = [gathered(part, "tensor", 0) for part in layer_parts[:-1]]
    if lax.axis_size("context") == 2:
        joint_grad, joint_grad_part, qk_part = joint_tail(
            joint, cos, sin, gains, query_grad, kv_grad_group, heads, CHUNKS, 3
        )
    else:
        kv_grad = halving_scatter(kv_grad_group, ("context",))
        joint_grad, qk_part = unprep(joint, cos, sin, gains, query_grad, kv_grad, heads, 512)
        tokens = joint_grad.reshape(columns, CHUNKS, ways, part_rows)
        joint_grad_part = swap(jnp.stack([tokens[:, :, i].reshape(columns, -1) for i in range(ways)]))
        joint_grad_part = joint_grad_part.reshape(ways * columns, -1)
    in_grad = natural(dot_tt(joint_grad_part, qkv_all))
    own_inputs = jnp.concatenate([own_rows(tokens_in, c) for c in range(CHUNKS)], axis=0).astype(f32)
    norm_grad = norm_back(in_grad, own_inputs, attn_gain_all)[0]
    grad_input = (jnp.concatenate(resid_grads, axis=0) + norm_grad).astype(bf16)
    gate_grad, up_grad, _ = lax.optimization_barrier((gate_grad, up_grad, joint_grad))
    grad_gate = dot_tn(normed_ffn, gate_grad).astype(bf16)
    grad_up = dot_tn(normed_ffn, up_grad).astype(bf16)
    late = lax.optimization_barrier((joint_grad, grad_input, grad_down, grad_gate, grad_up, grad_out))
    joint_late, _, grad_down, grad_gate, grad_up, grad_out = late
    grad_out = halving_scatter(grad_out, SHARE)
    grad_out = swap(jnp.stack([part.T for part in jnp.split(grad_out, ways, axis=1)]))
    grad_input = after(jnp.stack(jnp.split(grad_input, CHUNKS, axis=0)), *layer_firsts)
    layer_last = gathered(after(layer_parts[-1], grad_input), "tensor", 0)
    layer_output = jnp.concatenate(layer_firsts + [layer_last], axis=0).reshape(layer_input.shape)
    grad_input = gathered(grad_input, "tensor", 1).reshape(layer_input.shape)

    grad_qkv = dot_nn(joint_late, normed_low)
    attn_gain_part = jnp.sum(qkv_mine.astype(f32) * grad_qkv, axis=0) / attn_gain_all
    qk_rows = jnp.tile(qk_part.T, (1, width // HEAD_DIM))
    grad_qkv = jnp.concatenate(
        [grad_qkv, attn_gain_part[None], ffn_gain_part[None], qk_rows, jnp.zeros((12, width), f32)], axis=0
    )
    grad_qkv = halving_scatter(grad_qkv.astype(bf16).T, SHARE).astype(f32)
    small = line_total(grad_qkv[:, columns:].T)
    return (
        layer_output,
        grad_input,
        grad_qkv[:, :columns],
        jnp.sum(grad_out.astype(f32), axis=0),
        small[0],
        small[2:4, :HEAD_DIM],
        halving_scatter(grad_gate, SHARE).astype(f32),
        halving_scatter(grad_up, SHARE).astype(f32),
        halving_scatter(grad_down, SHARE).astype(f32).T,
        small[1],
    )


def solution(mesh):
    tokens, by_row, by_column = P("dp", "context", None), P(SHARE, "tensor"), P("tensor", SHARE)
    gain = P(SHARE)
    return jax.shard_map(
        body,
        mesh=mesh,
        in_specs=(
            tokens, tokens, by_row, by_column, gain, P(), by_row, by_row, by_column, gain, P("dp", None), P("dp", None)
        ),
        out_specs=(tokens, tokens, by_row, by_column, gain, P(), by_row, by_row, by_column, gain),
        check_vma=False,
    )
```

```python
import functools, math
import jax, jax.numpy as jnp
from jax import lax
from jax.experimental import pallas as pl
from jax.experimental.pallas import tpu as pltpu
from jax.experimental.layout import Layout, with_layout_constraint
from jax.sharding import PartitionSpec as P

HEAD_DIM = 64
LOG2E = math.log2(math.e)
LN2 = math.log(2.0)
f32 = jnp.float32
bf16 = jnp.bfloat16
epsilon = 1e-6


def dot_nt(a, b):
    return lax.dot_general(a, b, (((1,), (1,)), ((), ())), preferred_element_type=f32)

def dot_nn(a, b):
    return lax.dot_general(a, b, (((1,), (0,)), ((), ())), preferred_element_type=f32)

def dot_tn(a, b):
    return lax.dot_general(a, b, (((0,), (0,)), ((), ())), preferred_element_type=f32)


def dot_tt(a, b):
    return lax.dot_general(a, b, (((0,), (1,)), ((), ())), preferred_element_type=f32)


def head_norm(x):
    return x * lax.rsqrt(jnp.mean(x * x, axis=0, keepdims=True) + epsilon)


def prep_kernel(heads, joint_ref, cos_ref, sin_ref, gain_ref, q_ref, kv_ref):
    half = HEAD_DIM // 2
    cos, sin = cos_ref[...], sin_ref[...]

    def one(row, gain, scale):
        x = head_norm(joint_ref[row : row + HEAD_DIM, :]) * gain
        lo, hi = x[:half], x[half:]
        return jnp.concatenate([lo * cos - hi * sin, hi * cos + lo * sin], axis=0) * scale

    for h in range(heads):
        row = h * HEAD_DIM
        q_ref[row : row + HEAD_DIM, :] = one(row, gain_ref[:, 0:1], LOG2E * HEAD_DIM**-0.5).astype(bf16)
    row = heads * HEAD_DIM
    key = one(row, gain_ref[:, 1:2], 1.0)
    both = jnp.concatenate([key, joint_ref[row + HEAD_DIM : row + 2 * HEAD_DIM, :]], axis=0)
    kv_ref[...] = both.T.astype(bf16)


def prep(joint, cos, sin, gains, heads, block):
    rows, count = joint.shape
    block = min(block, count)
    return pl.pallas_call(
        functools.partial(prep_kernel, heads),
        out_shape=(
            jax.ShapeDtypeStruct((heads * HEAD_DIM, count), bf16),
            jax.ShapeDtypeStruct((count, 2 * HEAD_DIM), bf16),
        ),
        grid=(count // block,),
        in_specs=[
            pl.BlockSpec((rows, block), lambda i: (0, i)),
            pl.BlockSpec((HEAD_DIM // 2, block), lambda i: (0, i)),
            pl.BlockSpec((HEAD_DIM // 2, block), lambda i: (0, i)),
            pl.BlockSpec((HEAD_DIM, 2), lambda i: (0, 0)),
        ],
        out_specs=(
            pl.BlockSpec((heads * HEAD_DIM, block), lambda i: (0, i)),
            pl.BlockSpec((block, 2 * HEAD_DIM), lambda i: (i, 0)),
        ),
        cost_estimate=pl.CostEstimate(flops=rows * count * 20, bytes_accessed=rows * count * 6, transcendentals=0),
        name="prep",
    )(joint, cos, sin, gains)


def unprep_kernel(heads, joint_ref, cos_ref, sin_ref, gain_ref, dq_ref, dkv_ref, out_ref, dgain_ref):
    half = HEAD_DIM // 2
    cos, sin = cos_ref[...], sin_ref[...]

    @pl.when(pl.program_id(0) == 0)
    def _():
        dgain_ref[...] = jnp.zeros_like(dgain_ref)

    def one(row, grad, gain):
        x = joint_ref[row : row + HEAD_DIM, :]
        r = lax.rsqrt(jnp.mean(x * x, axis=0, keepdims=True) + epsilon)
        n = x * r
        lo, hi = grad[:half], grad[half:]
        back = jnp.concatenate([lo * cos + hi * sin, hi * cos - lo * sin], axis=0)
        scaled = back * gain
        result = r * (scaled - n * jnp.mean(scaled * n, axis=0, keepdims=True))
        out_ref[row : row + HEAD_DIM, :] = result.astype(bf16)
        return jnp.sum(back * n, axis=1, keepdims=True)

    total = None
    for h in range(heads):
        row = h * HEAD_DIM
        part = one(row, dq_ref[row : row + HEAD_DIM, :], gain_ref[:, 0:1])
        total = part if total is None else total + part
    row = heads * HEAD_DIM
    dkv = dkv_ref[...].astype(f32).T
    part = one(row, dkv[:HEAD_DIM], gain_ref[:, 1:2])
    out_ref[row + HEAD_DIM : row + 2 * HEAD_DIM, :] = dkv[HEAD_DIM:].astype(bf16)
    dgain_ref[...] += jnp.concatenate([total, part], axis=1)


def unprep(joint, cos, sin, gains, dq, dkv, heads, block):
    rows, count = joint.shape
    block = min(block, count)
    return pl.pallas_call(
        functools.partial(unprep_kernel, heads),
        out_shape=(
            jax.ShapeDtypeStruct((rows, count), bf16),
            jax.ShapeDtypeStruct((HEAD_DIM, 2), f32),
        ),
        grid=(count // block,),
        in_specs=[
            pl.BlockSpec((rows, block), lambda i: (0, i)),
            pl.BlockSpec((HEAD_DIM // 2, block), lambda i: (0, i)),
            pl.BlockSpec((HEAD_DIM // 2, block), lambda i: (0, i)),
            pl.BlockSpec((HEAD_DIM, 2), lambda i: (0, 0)),
            pl.BlockSpec((heads * HEAD_DIM, block), lambda i: (0, i)),
            pl.BlockSpec((block, 2 * HEAD_DIM), lambda i: (i, 0)),
        ],
        out_specs=(
            pl.BlockSpec((rows, block), lambda i: (0, i)),
            pl.BlockSpec((HEAD_DIM, 2), lambda i: (0, 0)),
        ),
        cost_estimate=pl.CostEstimate(flops=rows * count * 30, bytes_accessed=rows * count * 10, transcendentals=0),
        name="unprep",
    )(joint, cos, sin, gains, dq, dkv)


def block_state(seg_ref, start_ref, q_index, k_index, bq, bk):
    q_first = start_ref[0] + q_index * bq
    k_first = k_index * bk
    k_last_seg = seg_ref[k_first + bk - 1]
    needed = (k_first <= q_first + bq - 1) & ((k_last_seg == 0) | (k_last_seg >= seg_ref[q_first]) | (seg_ref[k_first] == 0))
    whole = (k_last_seg == 0) & (k_first + bk - 1 <= q_first)
    return needed, whole


def fwd_kernel(heads, bq, bk, start_ref, seg_ref, q_ref, kv_ref, qpos_ref, qseg_ref, kpos_ref, kseg_ref, o_ref, l_ref, vaug, qs, acc):
    qi = pl.program_id(0)
    nk = kv_ref.shape[0] // bk
    lane = lax.broadcasted_iota(jnp.int32, kv_ref.shape, 1)

    @pl.when(qi == 0)
    def _():
        vaug[...] = jnp.where(lane >= HEAD_DIM, kv_ref[...].astype(f32), jnp.where(lane == 0, 1.0, 0.0)).astype(bf16)

    zeros = jnp.zeros((HEAD_DIM, bq), f32)
    for h in range(heads):
        full = jnp.concatenate([q_ref[h * HEAD_DIM : (h + 1) * HEAD_DIM, :].astype(f32), zeros], axis=0)
        qs[h * bq : (h + 1) * bq, :] = full.T.astype(bf16)
    acc[...] = jnp.zeros_like(acc)

    def step(k_index, masked):
        rows = pl.ds(pl.multiple_of(k_index * bk, bk), bk)
        kb, vb = kv_ref[rows, :], vaug[rows, :]
        if masked:
            kseg = kseg_ref[k_index]
            mask = (kpos_ref[k_index] <= qpos_ref[...]) & ((kseg == 0) | (kseg == qseg_ref[...]))
        for h in range(heads):
            s = dot_nt(qs[h * bq : (h + 1) * bq, :], kb)
            p = jnp.exp2(s)
            if masked:
                p = jnp.where(mask, p, 0.0)
            acc[h * bq : (h + 1) * bq, :] += dot_nn(p.astype(bf16), vb)

    @pl.loop(0, nk)
    def _(k_index):
        needed, whole = block_state(seg_ref, start_ref, qi, k_index, bq, bk)

        @pl.when(needed & whole)
        def _():
            step(k_index, False)

        @pl.when(needed & jnp.logical_not(whole))
        def _():
            step(k_index, True)

    for h in range(heads):
        out = acc[h * bq : (h + 1) * bq, :].T
        total = out[0:1, :]
        o_ref[h * HEAD_DIM : (h + 1) * HEAD_DIM, :] = (out[HEAD_DIM:, :] / total).astype(bf16)
        l_ref[h : h + 1, :] = jnp.log2(total)


def attention(start, seg, q, kv, qpos, qseg, kpos, kseg, bq, bk, part, parts):
    heads = q.shape[0] // HEAD_DIM
    count, total = q.shape[1] // parts, kv.shape[0]
    bq, bk = min(bq, count), min(bk, total)
    first = part * (count // bq)
    whole = lambda *shape: pl.BlockSpec(shape, lambda i, *_: (0,) * len(shape))
    return pl.pallas_call(
        functools.partial(fwd_kernel, heads, bq, bk),
        out_shape=(
            jax.ShapeDtypeStruct((q.shape[0], count), bf16),
            jax.ShapeDtypeStruct((heads, count), f32),
        ),
        grid_spec=pltpu.PrefetchScalarGridSpec(
            num_scalar_prefetch=2,
            grid=(count // bq,),
            in_specs=[
                pl.BlockSpec((q.shape[0], bq), lambda i, *_: (0, i + first)),
                whole(*kv.shape),
                pl.BlockSpec((bq, 1), lambda i, *_: (i + first, 0)),
                pl.BlockSpec((bq, 1), lambda i, *_: (i + first, 0)),
                whole(total // bk, 1, bk),
                whole(total // bk, 1, bk),
            ],
            out_specs=(
                pl.BlockSpec((q.shape[0], bq), lambda i, *_: (0, i)),
                pl.BlockSpec((heads, bq), lambda i, *_: (0, i)),
            ),
            scratch_shapes=[
                pltpu.VMEM(kv.shape, bf16),
                pltpu.VMEM((heads * bq, 2 * HEAD_DIM), bf16),
                pltpu.VMEM((heads * bq, 2 * HEAD_DIM), f32),
            ],
        ),
        cost_estimate=pl.CostEstimate(flops=heads * count * total * 256, bytes_accessed=4 << 20, transcendentals=heads * count * total // 2),
        name="attend",
    )(start, seg, q, kv, qpos.reshape(-1, 1), qseg.reshape(-1, 1), kpos.reshape(-1, 1, bk), kseg.reshape(-1, 1, bk))


def split3(x):
    a = x.astype(bf16).astype(f32)
    b = (x - a).astype(bf16).astype(f32)
    return a, b, x - a - b


def bwd_kernel(heads, bq, bk, final, start_ref, seg_ref, q_ref, kv_ref, o_ref, do_ref, l_ref, qpos_ref, qseg_ref, kpos_ref, kseg_ref, *rest):
    carried, (dq_ref, dkv_ref, kaug, vaug, qst, dst, qs, ds, dacc, dkv) = rest[:-10], rest[-10:]
    qi = pl.program_id(0)
    nk = kv_ref.shape[0] // bk
    D = HEAD_DIM

    @pl.when(qi == 0)
    def _():
        lane = lax.broadcasted_iota(jnp.int32, kv_ref.shape, 1)
        kv = kv_ref[...].astype(f32)
        kaug[...] = jnp.where(lane < D, kv, jnp.where(lane < D + 3, -1.0, 0.0)).astype(bf16)
        vaug[...] = jnp.where(lane >= D, kv, jnp.where(lane < 3, -1.0, 0.0)).astype(bf16)
        dkv[...] = carried[0][...] if carried else jnp.zeros_like(dkv)

    row = lax.broadcasted_iota(jnp.int32, (D, bq), 0)

    def extra(x):
        a, b, c = split3(x)
        return jnp.where(row == 0, a, jnp.where(row == 1, b, jnp.where(row == 2, c, 0.0)))

    zeros = jnp.zeros((D, bq), f32)
    do_all = do_ref[...].astype(f32).T
    for h in range(heads):
        part = slice(h * D, (h + 1) * D)
        wide = slice(h * 2 * D, (h + 1) * 2 * D)
        q, do, o = q_ref[part, :].astype(f32), do_all[part, :], o_ref[part, :].astype(f32)
        delta = jnp.sum(do * o, axis=0, keepdims=True)
        qst[wide, :] = jnp.concatenate([q, extra(l_ref[h : h + 1, :])], axis=0).astype(bf16)
        dst[wide, :] = jnp.concatenate([extra(delta), do], axis=0).astype(bf16)
        qs[h * bq : (h + 1) * bq, :] = jnp.concatenate([q, zeros], axis=0).T.astype(bf16)
        ds[h * bq : (h + 1) * bq, :] = jnp.concatenate([zeros, do], axis=0).T.astype(bf16)
    dacc[...] = jnp.zeros_like(dacc)

    def step(k_index, masked):
        rows = pl.ds(pl.multiple_of(k_index * bk, bk), bk)
        kb, vb, kvb = kaug[rows, :], vaug[rows, :], kv_ref[rows, :]
        if masked:
            kseg = kseg_ref[rows, :]
            mask = (kpos_ref[rows, :] <= qpos_ref[...]) & ((kseg == 0) | (kseg == qseg_ref[...]))
        add = None
        for h in range(heads):
            wide = slice(h * 2 * D, (h + 1) * 2 * D)
            tall = slice(h * bq, (h + 1) * bq)
            p = jnp.exp2(dot_nn(kb, qst[wide, :]))
            if masked:
                p = jnp.where(mask, p, 0.0)
            sg = (p * dot_nn(vb, dst[wide, :])).astype(bf16)
            part = dot_nn(sg, qs[tall, :]) + dot_nn(p.astype(bf16), ds[tall, :])
            add = part if add is None else add + part
            dacc[tall, :] += dot_tn(sg, kvb)
        dkv[rows, :] += add

    @pl.loop(0, nk)
    def _(k_index):
        needed, whole = block_state(seg_ref, start_ref, qi, k_index, bq, bk)

        @pl.when(needed & whole)
        def _():
            step(k_index, False)

        @pl.when(needed & jnp.logical_not(whole))
        def _():
            step(k_index, True)

    for h in range(heads):
        dq_ref[h * D : (h + 1) * D, :] = dacc[h * bq : (h + 1) * bq, :].T[:D, :] * D**-0.5

    @pl.when(qi == pl.num_programs(0) - 1)
    def _():
        lane = lax.broadcasted_iota(jnp.int32, dkv.shape, 1)
        scale = jnp.where(lane < D, LN2, 1.0) if final else 1.0
        dkv_ref[...] = (dkv[...] * scale).astype(dkv_ref.dtype)


def attention_grad(start, seg, q, kv, o, do, l, qpos, qseg, kpos, kseg, carried, bq, bk, part, parts):
    heads = q.shape[0] // HEAD_DIM
    count, total = q.shape[1] // parts, kv.shape[0]
    bq, bk = min(bq, count), min(bk, total)
    first = part * (count // bq)
    final = part == parts - 1
    whole = lambda *shape: pl.BlockSpec(shape, lambda i, *_: (0,) * len(shape))
    wide = pl.BlockSpec((q.shape[0], bq), lambda i, *_: (0, i + first))
    near = pl.BlockSpec((q.shape[0], bq), lambda i, *_: (0, i))
    return pl.pallas_call(
        functools.partial(bwd_kernel, heads, bq, bk, final),
        out_shape=(
            jax.ShapeDtypeStruct((q.shape[0], count), f32),
            jax.ShapeDtypeStruct(kv.shape, bf16 if final else f32),
        ),
        grid_spec=pltpu.PrefetchScalarGridSpec(
            num_scalar_prefetch=2,
            grid=(count // bq,),
            in_specs=[
                wide,
                whole(*kv.shape),
                near,
                pl.BlockSpec((bq, q.shape[0]), lambda i, *_: (i + first, 0)),
                pl.BlockSpec((heads, bq), lambda i, *_: (0, i)),
                pl.BlockSpec((1, bq), lambda i, *_: (0, i + first)),
                pl.BlockSpec((1, bq), lambda i, *_: (0, i + first)),
                whole(total, 1),
                whole(total, 1),
            ]
            + [whole(*kv.shape)] * len(carried),
            out_specs=(near, whole(*kv.shape)),
            scratch_shapes=[
                pltpu.VMEM(kv.shape, bf16),
                pltpu.VMEM(kv.shape, bf16),
                pltpu.VMEM((heads * 2 * HEAD_DIM, bq), bf16),
                pltpu.VMEM((heads * 2 * HEAD_DIM, bq), bf16),
                pltpu.VMEM((heads * bq, 2 * HEAD_DIM), bf16),
                pltpu.VMEM((heads * bq, 2 * HEAD_DIM), bf16),
                pltpu.VMEM((heads * bq, 2 * HEAD_DIM), f32),
                pltpu.VMEM(kv.shape, f32),
            ],
        ),
        cost_estimate=pl.CostEstimate(flops=heads * count * total * 640, bytes_accessed=8 << 20, transcendentals=heads * count * total // 2),
        name="attend_grad",
    )(start, seg, q, kv, o, do, l, qpos.reshape(1, -1), qseg.reshape(1, -1), kpos.reshape(-1, 1), kseg.reshape(-1, 1), *carried)


HEADS = 16
KV_HEADS = 4
rope_base = 10000.0
SHARE = ("dp", "context")
EVERY = ("dp", "context", "tensor")
QUERY_BLOCK = 512
KEY_BLOCK = 512
CHUNKS = 2


def unit_rows(values):
    r = lax.rsqrt(jnp.mean(values * values, axis=-1, keepdims=True) + epsilon)
    return values * r, r


def norm_back(grad, values, gains):
    n, r = unit_rows(values)
    scaled = grad * gains
    return r * (scaled - n * jnp.mean(scaled * n, axis=-1, keepdims=True)), jnp.sum(grad * n, axis=0)


def mixed_silu(gate_in, up_in):
    return jax.nn.silu(gate_in) * up_in


def gathered(part, axes, axis):
    return lax.all_gather(part, axes, axis=axis, tiled=True)


def scattered(part, axes, axis):
    return lax.psum_scatter(part.astype(bf16), axes, scatter_dimension=axis, tiled=True)


def natural(values):
    return with_layout_constraint(values, Layout(major_to_minor=tuple(range(values.ndim))))


def after(value, *others):
    return lax.optimization_barrier((value,) + others)[0]


def halving_scatter(terms, axes):
    sizes = [lax.axis_size(axis) for axis in axes]
    blocks = terms.reshape(tuple(sizes) + (-1,) + terms.shape[1:])
    for place, axis in enumerate(axes):
        size, me = sizes[place], lax.axis_index(axis)
        stride = 1
        while stride < size:
            shape = blocks.shape
            split = blocks.reshape(shape[:place] + (shape[place] // 2, 2) + shape[place + 1 :])
            bit = (me // stride) % 2
            kept, sent = (
                lax.dynamic_index_in_dim(split, index, place + 1, keepdims=False) for index in (bit, 1 - bit)
            )
            got = lax.ppermute(sent, axis, [(i, i ^ stride) for i in range(size)])
            blocks = (kept.astype(f32) + got.astype(f32)).astype(bf16)
            stride *= 2
    return blocks.reshape((-1,) + terms.shape[1:])


def spread(part):
    ways, me = lax.axis_size("tensor"), lax.axis_index("tensor")
    out = lax.dynamic_update_index_in_dim(jnp.zeros((ways,) + part.shape, part.dtype), part, me, 0)
    for step in range(1, ways):
        got = lax.ppermute(part, "tensor", [(i, (i + step) % ways) for i in range(ways)])
        out = lax.dynamic_update_index_in_dim(out, got, (me - step) % ways, 0)
    return out


def line_total(part):
    total = part
    ways = lax.axis_size("tensor")
    for step in range(1, ways):
        total = total + lax.ppermute(part, "tensor", [(i, (i + step) % ways) for i in range(ways)])
    return total


def swap(blocks):
    ways, me = lax.axis_size("tensor"), lax.axis_index("tensor")
    out = blocks
    for step in range(1, ways):
        sent = lax.dynamic_index_in_dim(blocks, (me + step) % ways, 0, keepdims=False)
        got = lax.ppermute(sent, "tensor", [(i, (i + step) % ways) for i in range(ways)])
        out = lax.dynamic_update_index_in_dim(out, got, (me - step) % ways, 0)
    return out


def remote(source, target, sems, index, device):
    copy = pltpu.make_async_remote_copy(
        src_ref=source,
        dst_ref=target,
        send_sem=sems[0].at[index],
        recv_sem=sems[1].at[index],
        device_id=device,
        device_id_type=pl.DeviceIdType.MESH,
    )
    copy.start()
    return copy


def greet(devices):
    barrier = pltpu.get_barrier_semaphore()
    for device in devices:
        pl.semaphore_signal(barrier, inc=1, device_id=device, device_id_type=pl.DeviceIdType.MESH)
    pl.semaphore_wait(barrier, len(devices))


def aligned(start, size):
    return pl.ds(pl.multiple_of(start, size), size)


def gather_kernel(count, lines, pairs, shuffles, chunks, *refs):
    arrays = count + lines + pairs + shuffles
    sources, targets = refs[:arrays], refs[arrays : 2 * arrays]
    own_sem, send_sem, recv_sem = refs[2 * arrays : 2 * arrays + 3]
    dp, context = lax.axis_index("dp"), lax.axis_index("context")
    outer, inner = dp // 2, dp % 2
    across, along, beside = (
        {"dp": dp + 2 - 4 * outer},
        {"context": 1 - context},
        {"dp": dp + 1 - 2 * inner},
    )
    me, ways = lax.axis_index("tensor"), lax.axis_size("tensor")
    peers = [{"tensor": lax.rem(me + step, ways)} for step in range(1, ways)] if lines or shuffles else []
    greet(([across, along, beside] if count else [along]) + peers)

    def place(array, o, k, first=0, parts=1):
        rows = sources[array].shape[0]
        start = ((2 * o + inner) * 2 + k) * rows + first * (rows // parts)
        return targets[array].at[aligned(start, rows // parts), :]

    def send(array, kind, source, target, device):
        copy = pltpu.make_async_remote_copy(
            src_ref=source,
            dst_ref=target,
            send_sem=send_sem.at[array, kind],
            recv_sem=recv_sem.at[array, kind],
            device_id=device,
            device_id_type=pl.DeviceIdType.MESH,
        )
        copy.start()
        return copy

    copies, kept = {}, []
    passed = []
    for a in range(count + lines + pairs, arrays):
        size, width = sources[a].shape[0] // chunks, sources[a].shape[1] // ways
        for c in range(chunks):
            rows = pl.ds(c * size, size)
            target = targets[a].at[aligned((c * ways + me) * size, size), :]
            for k, peer in enumerate(peers):
                source = sources[a].at[rows, aligned(peer["tensor"] * width, width)]
                passed.append(send(a, c * (ways - 1) + k, source, target, peer))
            keep = pltpu.make_async_copy(sources[a].at[rows, aligned(me * width, width)], target, own_sem.at[a + c])
            keep.start()
            kept.append(keep)
    for a in range(count + lines, count + lines + pairs):
        rows = sources[a].shape[0]
        mine = targets[a].at[aligned(context * rows, rows), :]
        passed.append(send(a, 0, sources[a], mine, along))
        keep = pltpu.make_async_copy(sources[a], mine, own_sem.at[a])
        keep.start()
        kept.append(keep)
    for a in range(count):
        mine = place(a, outer, context)
        copies[a, 0] = send(a, 0, sources[a], mine, across)
        copies[a, 1] = send(a, 1, sources[a], mine, along)
        copies[a, 2] = send(a, 2, sources[a], mine, beside)
        keep = pltpu.make_async_copy(sources[a], mine, own_sem.at[a])
        keep.start()
        kept.append(keep)
    for a in range(count, count + lines):
        width = sources[a].shape[1]
        mine = targets[a].at[:, aligned(me * width, width)]
        for k, peer in enumerate(peers):
            passed.append(send(a, k, sources[a], mine, peer))
        keep = pltpu.make_async_copy(sources[a], mine, own_sem.at[a])
        keep.start()
        kept.append(keep)
    for a in range(count):
        copies[a, 0].wait_recv()
        got = place(a, 1 - outer, context)
        half = place(a, 1 - outer, context, 0, 2)
        copies[a, 3] = send(a, 3, half, half, along)
        copies[a, 4] = send(a, 4, got, got, beside)
        copies[a, 1].wait_recv()
        got = place(a, outer, 1 - context)
        half = place(a, outer, 1 - context, 1, 2)
        copies[a, 5] = send(a, 5, half, half, across)
        copies[a, 6] = send(a, 6, got, got, beside)
    for a in range(count):
        for kind, first in ((3, 0), (5, 1)):
            copies[a, kind].wait_recv()
            half = place(a, 1 - outer, 1 - context, first, 2)
            copies[a, 7 + first] = send(a, 7 + first, half, half, beside)
    for keep in kept:
        keep.wait()
    for copy in passed:
        copy.wait()
    for a in range(count):
        for kind in (2, 4, 6, 7, 8):
            copies[a, kind].wait_recv()
    for copy in copies.values():
        copy.wait_send()


def plane_gather(parts, lines, pairs, collective, shuffles=(), chunks=1):
    share, ways = lax.axis_size("dp") * lax.axis_size("context"), lax.axis_size("tensor")
    if (lax.axis_size("dp"), lax.axis_size("context")) != (4, 2):
        whole = [gathered(part, SHARE, 0) for part in parts] + [jnp.concatenate(list(spread(line)), axis=1) for line in lines]
        whole += [gathered(pair, "context", 0) for pair in pairs]
        for grad in shuffles:
            blocks = grad.reshape(chunks, grad.shape[0] // chunks, ways, -1).transpose(2, 0, 1, 3)
            whole.append(swap(blocks).transpose(1, 0, 2, 3).reshape(ways * grad.shape[0], -1))
        return whole
    arrays = len(parts) + len(lines) + len(pairs) + len(shuffles)
    shapes = [(share * part.shape[0], part.shape[1]) for part in parts] + [(line.shape[0], ways * line.shape[1]) for line in lines]
    shapes += [(2 * pair.shape[0], pair.shape[1]) for pair in pairs]
    shapes += [(ways * grad.shape[0], grad.shape[1] // ways) for grad in shuffles]
    return pl.pallas_call(
        functools.partial(gather_kernel, len(parts), len(lines), len(pairs), len(shuffles), chunks),
        out_shape=tuple(jax.ShapeDtypeStruct(shape, bf16) for shape in shapes),
        in_specs=[pl.BlockSpec(memory_space=pltpu.VMEM)] * arrays,
        out_specs=(pl.BlockSpec(memory_space=pl.ANY),) * arrays,
        scratch_shapes=[
            pltpu.SemaphoreType.DMA((arrays + chunks,)),
            pltpu.SemaphoreType.DMA((arrays, 9)),
            pltpu.SemaphoreType.DMA((arrays, 9)),
        ],
        compiler_params=pltpu.CompilerParams(collective_id=collective, has_side_effects=True),
        name="plane_gather",
    )(*parts, *lines, *pairs, *shuffles)


def tail_kernel(heads, ways, chunks, joint_ref, cos_ref, sin_ref, gain_ref, dq_ref, dkv_ref,
                grad_ref, part_ref, dgain_ref, got_ref, own_sem, send_sem, recv_sem):
    D, half = HEAD_DIM, HEAD_DIM // 2
    rows, count = joint_ref.shape
    queries = heads * D
    me, context = lax.axis_index("tensor"), lax.axis_index("context")
    peers = [lax.rem(me + step, ways) for step in range(1, ways)]
    along = {"context": 1 - context}
    greet([along] + [{"tensor": peer} for peer in peers])
    sems = (send_sem, recv_sem)
    block = min(count, 512)
    size = count // chunks // ways
    copies = [remote(dkv_ref.at[aligned((1 - context) * count, count), :], got_ref, sems, 0, along)]

    def one(first, columns, grad, gain):
        x = joint_ref[first : first + D, columns]
        cos, sin = cos_ref[:, columns], sin_ref[:, columns]
        r = lax.rsqrt(jnp.mean(x * x, axis=0, keepdims=True) + epsilon)
        n = x * r
        lo, hi = grad[:half], grad[half:]
        back = jnp.concatenate([lo * cos + hi * sin, hi * cos - lo * sin], axis=0)
        scaled = back * gain
        result = r * (scaled - n * jnp.mean(scaled * n, axis=0, keepdims=True))
        grad_ref[first : first + D, columns] = result.astype(bf16)
        return jnp.sum(back * n, axis=1, keepdims=True)

    def hand_out(first, height, index):
        for c in range(chunks):
            target = part_ref.at[pl.ds(pl.multiple_of(me * rows + first, 128), height), pl.ds(c * size, size)]
            for k, peer in enumerate(peers):
                source = grad_ref.at[pl.ds(first, height), aligned((c * ways + peer) * size, size)]
                copies.append(remote(source, target, sems, 1 + (index * chunks + c) * (ways - 1) + k, {"tensor": peer}))
            kept = pltpu.make_async_copy(
                grad_ref.at[pl.ds(first, height), aligned((c * ways + me) * size, size)], target, own_sem.at[index * chunks + c]
            )
            kept.start()
            copies.append(kept)

    total = jnp.zeros((D, 1), f32)
    for b in range(count // block):
        columns = slice(b * block, (b + 1) * block)
        for h in range(heads):
            total += one(h * D, columns, dq_ref[h * D : (h + 1) * D, columns], gain_ref[:, 0:1])
    hand_out(0, queries, 0)
    copies[0].wait_recv()
    key_total = jnp.zeros((D, 1), f32)
    for b in range(count // block):
        columns = slice(b * block, (b + 1) * block)
        mine = dkv_ref[aligned(context * count + b * block, block), :].astype(f32)
        both = (mine + got_ref[columns, :].astype(f32)).T
        key_total += one(queries, columns, both[:D], gain_ref[:, 1:2])
        grad_ref[queries + D : queries + 2 * D, columns] = both[D:].astype(bf16)
    hand_out(queries, 2 * D, 1)
    dgain_ref[...] = jnp.concatenate([total, key_total], axis=1)
    copies[0].wait_send()
    for copy in copies[1:]:
        copy.wait()


def joint_tail(joint, cos, sin, gains, dq, dkv, heads, chunks, collective):
    rows, count = joint.shape
    ways = lax.axis_size("tensor")
    number = 1 + 2 * chunks * (ways - 1)
    vmem = pl.BlockSpec(memory_space=pltpu.VMEM)
    return pl.pallas_call(
        functools.partial(tail_kernel, heads, ways, chunks),
        out_shape=(
            jax.ShapeDtypeStruct((rows, count), bf16),
            jax.ShapeDtypeStruct((ways * rows, count // ways), bf16),
            jax.ShapeDtypeStruct((HEAD_DIM, 2), f32),
        ),
        in_specs=[vmem] * 6,
        out_specs=(vmem, pl.BlockSpec(memory_space=pl.ANY), vmem),
        scratch_shapes=[
            pltpu.VMEM((count, 2 * HEAD_DIM), bf16),
            pltpu.SemaphoreType.DMA((2 * chunks,)),
            pltpu.SemaphoreType.DMA((number,)),
            pltpu.SemaphoreType.DMA((number,)),
        ],
        compiler_params=pltpu.CompilerParams(collective_id=collective, has_side_effects=True),
        name="joint_tail",
    )(joint, cos, sin, gains, dq, dkv)


def rope_tables(positions):
    half = HEAD_DIM // 2
    inverse = jnp.exp(-math.log(rope_base) * jnp.arange(half, dtype=f32) * 2.0 / HEAD_DIM)
    angles = inverse[:, None] * positions.astype(f32)[None, :]
    return jnp.cos(angles), jnp.sin(angles)


def body(
    layer_input, cotangent, w_qkv, w_out, attn_gain, qk_gain, w_gate, w_up, w_down, ffn_gain, seg_ids, pos_ids
):
    _, rows, width = layer_input.shape
    ways = lax.axis_size("tensor")
    heads = HEADS // ways
    mine = lax.axis_index("tensor")
    group_seg, group_pos = seg_ids[0], pos_ids[0]
    first_row = lax.axis_index("context") * rows
    my_seg = lax.dynamic_slice_in_dim(group_seg, first_row, rows, 0)
    my_pos = lax.dynamic_slice_in_dim(group_pos, first_row, rows, 0)
    start = jnp.reshape(first_row, (1,)).astype(jnp.int32)
    columns = w_qkv.shape[1]
    qkv_shard = w_qkv.T
    packed = jnp.concatenate(
        [qkv_shard, attn_gain[None], ffn_gain[None], jnp.zeros((14, w_qkv.shape[0]), bf16)], axis=0
    )
    gate_all = gathered(w_gate, SHARE, 0)
    (packed_all,) = plane_gather([packed.T], [], [], 0)
    packed_all = packed_all.T
    qkv_mine = packed_all[:columns]
    attn_gain_all = packed_all[columns].astype(f32)
    ffn_gain_all = packed_all[columns + 1].astype(f32)

    tokens_in = layer_input.reshape(rows, width)
    cot = cotangent.reshape(rows, width)
    normed_low = (unit_rows(tokens_in.astype(f32))[0] * attn_gain_all).astype(bf16)
    joint = dot_nt(qkv_mine, normed_low)
    cos, sin = rope_tables(my_pos)
    gains = qk_gain.T
    queries, kv_mine = prep(joint, cos, sin, gains, heads, 512)
    (kv,) = plane_gather([], [], [kv_mine], 1)
    out_t = jnp.concatenate(list(spread(after(w_out.T, kv))), axis=1)
    up_all = gathered(after(w_up, kv), SHARE, 0)
    queries = after(queries, gate_all)
    chunk_rows = rows // CHUNKS
    part_rows = chunk_rows // ways
    chunks = [slice(c * chunk_rows, (c + 1) * chunk_rows) for c in range(CHUNKS)]

    def own_rows(values, c):
        return lax.dynamic_slice_in_dim(values, c * chunk_rows + mine * part_rows, part_rows, 0)

    keys = (group_pos, group_seg)
    attended, log_total, attended_all = [], [], []
    for c in range(CHUNKS):
        result, total = attention(
            start + c * chunk_rows, group_seg, queries, kv, my_pos, my_seg, *keys, QUERY_BLOCK, KEY_BLOCK, c, CHUNKS
        )
        attended.append(result)
        log_total.append(total)
        attended_all.append(gathered(result, "tensor", 0))

    out_all, down_all, qkv_t = plane_gather([after(out_t, up_all, *attended), w_down.T], [w_qkv], [], 5)

    resid_parts, normed_ffns, acts, gate_grads, up_grads, ffn_in_grads = [], [], [], [], [], []
    previous = attended[-1]
    for c, chunk in enumerate(chunks):
        act_grad = dot_nn(cot[chunk], after(down_all, previous))
        resid = tokens_in[chunk].astype(f32) + natural(dot_tt(after(attended_all[c], act_grad), out_all))
        normed_ffn = (unit_rows(resid)[0] * ffn_gain_all).astype(bf16)
        gate, up = dot_nn(normed_ffn, gate_all), dot_nn(normed_ffn, up_all)
        act, silu_pull = jax.vjp(mixed_silu, gate, up)
        gate_grad, up_grad = (g.astype(bf16) for g in silu_pull(act_grad))
        previous = (dot_nt(gate_grad, gate_all) + dot_nt(up_grad, up_all)).astype(bf16)
        ffn_in_grads.append(scattered(previous, "tensor", 0).astype(f32))
        resid_parts.append(own_rows(resid, 0))
        normed_ffns.append(normed_ffn)
        acts.append(act.astype(bf16))
        gate_grads.append(gate_grad)
        up_grads.append(up_grad)
    normed_ffn, act, gate_grad, up_grad = (
        jnp.concatenate(pieces, axis=0) for pieces in (normed_ffns, acts, gate_grads, up_grads)
    )
    act, gate_grad, up_grad, _ = lax.optimization_barrier((act, gate_grad, up_grad, previous))
    ffn_part = dot_nt(act, down_all).astype(bf16)
    grad_down = dot_tn(cot, act).astype(bf16)
    ffn_gain_part, resid_grads, attended_grads, attended_parts, branches = 0.0, [], [], [], []
    for c in range(CHUNKS):
        norm_grad, gain_part = norm_back(ffn_in_grads[c], resid_parts[c], ffn_gain_all)
        ffn_gain_part += gain_part
        resid_grad = own_rows(cot, c).astype(f32) + norm_grad
        branch = resid_grad.astype(bf16)
        resid_grads.append(resid_grad)
        branches.append(branch)
        attended_grads.append(dot_nn(branch, out_all).astype(bf16))
        attended_parts.append(lax.dynamic_slice_in_dim(attended_all[c], mine * part_rows, part_rows, 1))

    attended_grad = after(jnp.concatenate(attended_grads, axis=0), ffn_part, grad_down)
    qkv_all, attended_grad = plane_gather([qkv_t], [], [], 2, [attended_grad], CHUNKS)
    branch, attended_part = jnp.concatenate(branches, axis=0), jnp.concatenate(attended_parts, axis=1)
    grad_out = lax.dot_general(branch, attended_part, (((0,), (1,)), ((), ())), preferred_element_type=f32)
    grad_out = grad_out.astype(bf16)
    query_grads, carried, layer_parts, kept_part = [], [], [], ffn_part
    for c, chunk in enumerate(chunks):
        query_grad, kv_grad_group = attention_grad(
            start + c * chunk_rows, group_seg, queries, kv, attended[c], attended_grad, log_total[c],
            my_pos, my_seg, *keys, carried, QUERY_BLOCK, KEY_BLOCK, c, CHUNKS
        )
        query_grads.append(query_grad)
        if c < CHUNKS - 1:
            ffn_sum = scattered(kept_part[chunk], "tensor", 0).astype(f32)
            layer_parts.append((after(resid_parts[c], query_grad) + ffn_sum).astype(bf16))
            carried = [after(kv_grad_group, layer_parts[-1])]
            kept_part = after(ffn_part, layer_parts[-1])
    query_grad = jnp.concatenate(query_grads, axis=1)
    ffn_sum = scattered(kept_part[chunks[-1]], "tensor", 0).astype(f32)
    layer_parts.append((after(resid_parts[-1], query_grad) + ffn_sum).astype(bf16))
    layer_firsts = [gathered(part, "tensor", 0) for part in layer_parts[:-1]]
    if lax.axis_size("context") == 2:
        joint_grad, joint_grad_part, qk_part = joint_tail(
            joint, cos, sin, gains, query_grad, kv_grad_group, heads, CHUNKS, 3
        )
    else:
        kv_grad = halving_scatter(kv_grad_group, ("context",))
        joint_grad, qk_part = unprep(joint, cos, sin, gains, query_grad, kv_grad, heads, 512)
        tokens = joint_grad.reshape(columns, CHUNKS, ways, part_rows)
        joint_grad_part = swap(jnp.stack([tokens[:, :, i].reshape(columns, -1) for i in range(ways)]))
        joint_grad_part = joint_grad_part.reshape(ways * columns, -1)
    in_grad = natural(dot_tt(joint_grad_part, qkv_all))
    own_inputs = jnp.concatenate([own_rows(tokens_in, c) for c in range(CHUNKS)], axis=0).astype(f32)
    norm_grad = norm_back(in_grad, own_inputs, attn_gain_all)[0]
    grad_input = (jnp.concatenate(resid_grads, axis=0) + norm_grad).astype(bf16)
    gate_grad, up_grad, _ = lax.optimization_barrier((gate_grad, up_grad, joint_grad))
    grad_gate = dot_tn(normed_ffn, gate_grad).astype(bf16)
    grad_up = dot_tn(normed_ffn, up_grad).astype(bf16)
    late = lax.optimization_barrier((joint_grad, grad_input, grad_down, grad_gate, grad_up, grad_out))
    joint_late, _, grad_down, grad_gate, grad_up, grad_out = late
    grad_out = halving_scatter(grad_out, SHARE)
    grad_out = swap(jnp.stack([part.T for part in jnp.split(grad_out, ways, axis=1)]))
    grad_input = after(jnp.stack(jnp.split(grad_input, CHUNKS, axis=0)), *layer_firsts)
    layer_last = gathered(after(layer_parts[-1], grad_input), "tensor", 0)
    layer_output = jnp.concatenate(layer_firsts + [layer_last], axis=0).reshape(layer_input.shape)
    grad_input = gathered(grad_input, "tensor", 1).reshape(layer_input.shape)

    grad_qkv = dot_nn(joint_late, normed_low)
    attn_gain_part = jnp.sum(qkv_mine.astype(f32) * grad_qkv, axis=0) / attn_gain_all
    qk_rows = jnp.tile(qk_part.T, (1, width // HEAD_DIM))
    grad_qkv = jnp.concatenate(
        [grad_qkv, attn_gain_part[None], ffn_gain_part[None], qk_rows, jnp.zeros((12, width), f32)], axis=0
    )
    grad_qkv = halving_scatter(grad_qkv.astype(bf16).T, SHARE).astype(f32)
    small = line_total(grad_qkv[:, columns:].T)
    return (
        layer_output,
        grad_input,
        grad_qkv[:, :columns],
        jnp.sum(grad_out.astype(f32), axis=0),
        small[0],
        small[2:4, :HEAD_DIM],
        halving_scatter(grad_gate, SHARE).astype(f32),
        halving_scatter(grad_up, SHARE).astype(f32),
        halving_scatter(grad_down, SHARE).astype(f32).T,
        small[1],
    )


def solution(mesh):
    tokens, by_row, by_column = P("dp", "context", None), P(SHARE, "tensor"), P("tensor", SHARE)
    gain = P(SHARE)
    return jax.shard_map(
        body,
        mesh=mesh,
        in_specs=(
            tokens, tokens, by_row, by_column, gain, P(), by_row, by_row, by_column, gain, P("dp", None), P("dp", None)
        ),
        out_specs=(tokens, tokens, by_row, by_column, gain, P(), by_row, by_row, by_column, gain),
        check_vma=False,
    )
```
